32 devices in a mesh: dp: 8 (over z, y), bfly: 4 (over x, core).
Axes of the slice: x: 2, y: 2, z: 4, core: 2. Of those that a mesh axis runs over, the one named last changes fastest.
Arguments:
- tokens: bfloat16 [2048, 12288], P('dp', 'bfly'), may hold values from -6 to 6
- grad_out: bfloat16 [2048, 12288], P('dp', 'bfly'), may hold values from -6 to 6
- weight_a: bfloat16 [48, 256, 512], P('bfly', 'dp'), may hold values from -0.375 to 0.375
- weight_b: bfloat16 [96, 256, 256], P('bfly', 'dp'), may hold values from -0.375 to 0.375
- weight_c: bfloat16 [96, 256, 256], P('bfly', 'dp'), may hold values from -0.375 to 0.375
- weight_e: bfloat16 [48, 512, 256], P('bfly', 'dp'), may hold values from -0.25 to 0.25
Outputs:
- output: bfloat16 [2048, 12288], P('dp', 'bfly')
- grad_in: bfloat16 [2048, 12288], P('dp', 'bfly')
- grad_a: float32 [48, 256, 512], P('bfly', 'dp')
- grad_b: float32 [96, 256, 256], P('bfly', 'dp')
- grad_c: float32 [96, 256, 256], P('bfly', 'dp')
- grad_e: float32 [48, 512, 256], P('bfly', 'dp')
The draws below stay inside these ranges and needn't reach their ends.
All inputs are finite; a program needn't handle non-finite values.
Results may differ from the reference program's by a relative error of at most 0.03.
Values may be sent and summed in bfloat16 or wider, within the bound.
No kernel may reach another device: no remote copies, remote signals or barrier semaphores. Data moves between devices by JAX's collectives and lax.ppermute only.
A program may use at most 128 MiB of HBM per device.

```python
import jax
import jax.numpy as jnp
from jax import lax

BLK = 256
INB = 48
HB = 96
TOK_DEV = 256
EXPAND = 2
D = 12288
GROUPS = 4
LOCB = 24
SUB = 64
TOKENS = 2048
N_DP = 8


def block_levels(own_key, shape, cuts, least, high):
    def one(axis_at, parts):
        steps = jax.random.uniform(jax.random.fold_in(jax.random.fold_in(own_key, 6), axis_at), (parts,), jnp.float32, least / len(cuts), high / len(cuts))
        return jnp.repeat(jnp.exp(steps), shape[axis_at] // parts).reshape((-1,) + (1,) * (len(shape) - axis_at - 1))

    level = one(*cuts[0])
    for cut in cuts[1:]:
        level = level * one(*cut)
    return level


def bell_draw(key, extent, deviation, most, shards=(), dtype=jnp.bfloat16):
    values = jax.random.normal(key, extent, jnp.float32) * deviation
    if len(shards) > 0:
        values = block_levels(key, extent, shards, -0.22, 0.18) * values
    return jnp.clip(values, min=-most, max=most).astype(dtype)


def setup_inputs(seed: int = 0) -> dict:
    key_list = jax.random.split(jax.random.key(seed), 7)
    tokens = bell_draw(key_list[0], (TOKENS, D), 1.0, 6.0, ((0, 8), (1, 4)))
    grad_out = bell_draw(key_list[1], (TOKENS, D), 1.0, 6.0, ((0, 8), (1, 4)))
    weight_a = bell_draw(key_list[2], (INB, BLK, EXPAND * BLK), BLK ** -0.5, 0.375, ((0, 4), (1, 8)))
    weight_b = bell_draw(key_list[3], (HB, BLK, BLK), BLK ** -0.5, 0.375, ((0, 4), (1, 8)))
    weight_c = bell_draw(key_list[4], (HB, BLK, BLK), BLK ** -0.5, 0.375, ((0, 4), (1, 8)))
    weight_e = bell_draw(key_list[5], (INB, EXPAND * BLK, BLK), (EXPAND * BLK) ** -0.5, 0.25, ((0, 4), (1, 8)))
    return {"tokens": tokens, "grad_out": grad_out, "weight_a": weight_a, "weight_b": weight_b, "weight_c": weight_c, "weight_e": weight_e}


gelu_scale = 0.7978845608028654


def permute(blocks):
    count = blocks.shape[0]
    pieces = blocks.reshape(count, GROUPS, LOCB, GROUPS, SUB)
    return pieces.transpose(0, 3, 2, 1, 4).reshape(count, HB, BLK)


def gelu_pair(hidden):
    inner_arg = gelu_scale * (hidden + 0.044715 * hidden * hidden * hidden)
    tangent = jnp.tanh(inner_arg)
    gelu_value = 0.5 * hidden * (1.0 + tangent)
    gelu_slope = 0.5 * (1.0 + tangent) + 0.5 * hidden * (1.0 - tangent * tangent) * gelu_scale * (1.0 + 3.0 * 0.044715 * hidden * hidden)
    return gelu_value, gelu_slope


def reference(tokens, grad_out, weight_a, weight_b, weight_c, weight_e):
    wide_a = weight_a.astype(jnp.float32)
    wide_b = weight_b.astype(jnp.float32)
    wide_c = weight_c.astype(jnp.float32)
    wide_e = weight_e.astype(jnp.float32)
    token_runs = tokens.reshape(N_DP, TOK_DEV, INB, BLK)
    grad_runs = grad_out.reshape(N_DP, TOK_DEV, INB, BLK)

    def one_shard(totals, shard_pair):
        inputs = shard_pair[0].astype(jnp.float32)
        upstream = shard_pair[1].astype(jnp.float32)
        spread = jnp.einsum('tki,kio->tko', inputs, wide_a).astype(jnp.bfloat16).reshape(TOK_DEV, HB, BLK)
        permuted = permute(spread).astype(jnp.float32)
        hidden = jnp.einsum('tqi,qij->tqj', permuted, wide_b)
        gelu_value, gelu_slope = gelu_pair(hidden)
        active = gelu_value.astype(jnp.bfloat16).astype(jnp.float32)
        narrowed = jnp.einsum('tqi,qij->tqj', active, wide_c).astype(jnp.bfloat16)
        returned = permute(narrowed).reshape(TOK_DEV, INB, EXPAND * BLK).astype(jnp.float32)
        output = jnp.einsum('tko,koj->tkj', returned, wide_e).astype(jnp.bfloat16)
        back_out = jnp.einsum('tkj,koj->tko', upstream, wide_e).astype(jnp.bfloat16).reshape(TOK_DEV, HB, BLK)
        back_mid = permute(back_out).astype(jnp.float32)
        back_act = jnp.einsum('tqj,qij->tqi', back_mid, wide_c)
        back_hidden = (back_act * gelu_slope).astype(jnp.bfloat16).astype(jnp.float32)
        back_first = jnp.einsum('tqj,qij->tqi', back_hidden, wide_b).astype(jnp.bfloat16)
        back_spread = permute(back_first).reshape(TOK_DEV, INB, EXPAND * BLK).astype(jnp.float32)
        back_input = jnp.einsum('tko,kio->tki', back_spread, wide_a).astype(jnp.bfloat16)
        partials = (
            jnp.einsum('tki,tko->kio', inputs, back_spread),
            jnp.einsum('tqi,tqj->qij', permuted, back_hidden),
            jnp.einsum('tqi,tqj->qij', active, back_mid),
            jnp.einsum('tko,tkj->koj', returned, upstream),
        )
        rounded = tuple(lax.optimization_barrier(piece.astype(jnp.bfloat16)).astype(jnp.float32) for piece in partials)
        totals = tuple(total + piece for total, piece in zip(totals, rounded))
        return totals, (output, back_input)

    start_totals = (
        jnp.zeros((INB, BLK, EXPAND * BLK), jnp.float32),
        jnp.zeros((HB, BLK, BLK), jnp.float32),
        jnp.zeros((HB, BLK, BLK), jnp.float32),
        jnp.zeros((INB, EXPAND * BLK, BLK), jnp.float32),
    )
    totals, results = lax.scan(one_shard, start_totals, (token_runs, grad_runs))
    output = results[0].reshape(TOKENS, D)
    grad_in = results[1].reshape(TOKENS, D)
    return output, grad_in, totals[0], totals[1], totals[2], totals[3]
```

```python
import jax
import jax.numpy as jnp
from jax import lax
from jax.sharding import PartitionSpec as P

BLK = 256

gelu_scale = 0.7978845608028654


def gelu_pair(hidden):
    inner_arg = gelu_scale * (hidden + 0.044715 * hidden * hidden * hidden)
    tangent = jnp.tanh(inner_arg)
    gelu_value = 0.5 * hidden * (1.0 + tangent)
    gelu_slope = 0.5 * (1.0 + tangent) + 0.5 * hidden * (1.0 - tangent * tangent) * gelu_scale * (
        1.0 + 3.0 * 0.044715 * hidden * hidden
    )
    return (gelu_value, gelu_slope)


def mm(spec, a, b):
    return jnp.einsum(spec, a, b, preferred_element_type=jnp.float32)


def regroup(piece, group_count):
    local_blocks, block_width, token_count = piece.shape
    stacked = piece.reshape(local_blocks, group_count, block_width // group_count, token_count)
    arrived = lax.all_to_all(stacked, "bfly", split_axis=1, concat_axis=1, tiled=True)
    return arrived.reshape(local_blocks, block_width, token_count)


def any_mesh(tokens, grad_out, weight_a, weight_b, weight_c, weight_e):
    group_count = lax.axis_size("bfly")
    full_a, full_b, full_c, full_e = (
        lax.all_gather(w, "dp", axis=1, tiled=True)
        for w in (weight_a, weight_b, weight_c, weight_e)
    )
    token_count = tokens.shape[0]
    inner_blocks = full_a.shape[0]
    spread_width = full_a.shape[2]
    local_blocks = full_b.shape[0]
    inputs = tokens.reshape(token_count, inner_blocks, BLK).transpose(1, 2, 0)
    upstream = grad_out.reshape(token_count, inner_blocks, BLK).transpose(1, 2, 0)
    hidden_view = (local_blocks, BLK, token_count)
    wide_view = (inner_blocks, spread_width, token_count)
    spread = mm("kit,kio->kot", inputs, full_a).astype(jnp.bfloat16).reshape(hidden_view)
    back_out = mm("kjt,koj->kot", upstream, full_e).astype(jnp.bfloat16).reshape(hidden_view)
    permuted = regroup(spread, group_count)
    back_mid = regroup(back_out, group_count)
    gelu_value, gelu_slope = gelu_pair(mm("qit,qij->qjt", permuted, full_b))
    active = gelu_value.astype(jnp.bfloat16)
    narrowed = mm("qit,qij->qjt", active, full_c).astype(jnp.bfloat16)
    back_hidden = (mm("qjt,qij->qit", back_mid, full_c) * gelu_slope).astype(jnp.bfloat16)
    back_first = mm("qjt,qij->qit", back_hidden, full_b).astype(jnp.bfloat16)
    returned = regroup(narrowed, group_count).reshape(wide_view)
    back_spread = regroup(back_first, group_count).reshape(wide_view)
    output = mm("kot,koj->kjt", returned, full_e)
    back_input = mm("kot,kio->kit", back_spread, full_a)
    parts = (
        mm("kit,kot->kio", inputs, back_spread),
        mm("qit,qjt->qij", permuted, back_hidden),
        mm("qit,qjt->qij", active, back_mid),
        mm("kot,kjt->koj", returned, upstream),
    )
    grads = tuple(
        lax.psum_scatter(part.astype(jnp.bfloat16), "dp", scatter_dimension=1, tiled=True).astype(
            jnp.float32
        )
        for part in parts
    )

    def rows(x):
        return x.astype(jnp.bfloat16).transpose(2, 0, 1).reshape(token_count, inner_blocks * BLK)

    return (rows(output), rows(back_input)) + grads


def xor_permute(x, mask):
    n = lax.axis_size("bfly")
    return lax.ppermute(x, "bfly", [(i, i ^ mask) for i in range(n)])


def deal_weight(w):
    pairs = lax.axis_size("dp") // 2
    sets = w.reshape(pairs, 3, 2, w.shape[1], w.shape[2])
    own = jnp.stack([sets[:, 0], sets[:, 2]], axis=1)
    mid = jnp.stack([sets[:, 1], sets[:, 1]], axis=1)
    return jnp.stack([own, mid], axis=2).reshape((pairs * 2, 2) + sets.shape[2:])


def gather_bfly(w):
    index = lax.axis_index("bfly")
    high = index // 2 == 1
    other = xor_permute(w, 2)
    pair = jnp.stack([jnp.where(high, other, w), jnp.where(high, w, other)], axis=0)
    odd = index % 2 == 1
    swap = xor_permute(pair, 1)
    both = jnp.stack([jnp.where(odd, swap, pair), jnp.where(odd, pair, swap)], axis=1)
    return both.reshape((4,) + w.shape)


def scatter_bfly(g):
    index = lax.axis_index("bfly")
    high, odd = index // 2, index % 2
    quads = g.astype(jnp.bfloat16).reshape((2, 2) + g.shape[1:])
    keep = lax.dynamic_index_in_dim(quads, odd, 1, keepdims=False)
    send = lax.dynamic_index_in_dim(quads, 1 - odd, 1, keepdims=False)
    got = xor_permute(send, 1)
    half = (keep.astype(jnp.float32) + got.astype(jnp.float32)).astype(jnp.bfloat16)
    keep = lax.dynamic_index_in_dim(half, high, 0, keepdims=False)
    send = lax.dynamic_index_in_dim(half, 1 - high, 0, keepdims=False)
    got = xor_permute(send, 2)
    return (keep.astype(jnp.float32) + got.astype(jnp.float32)).astype(jnp.bfloat16)


def exchange(x, axes):
    return lax.all_to_all(x, axes, split_axis=0, concat_axis=0, tiled=True)


def deal_tokens(x):
    ndp, nb = lax.axis_size("dp"), lax.axis_size("bfly")
    pairs, count = ndp // 2, x.shape[0]
    view = x.reshape(count, pairs, 3, BLK)
    own = view[:, :, 0::2].reshape(nb, count // nb, ndp, BLK).transpose(2, 0, 1, 3)
    mid = view[:, :, 1].reshape(2, nb, count // nb // 2, pairs, BLK).transpose(3, 0, 1, 2, 4)
    mid = mid.reshape(ndp, nb, count // nb // 2, BLK)
    return jnp.concatenate([own, mid], axis=2).reshape(ndp * nb, -1, BLK)


def tokens_in(x):
    ndp, nb = lax.axis_size("dp"), lax.axis_size("bfly")
    own_count = x.shape[0] // nb
    got = exchange(deal_tokens(x), ("dp", "bfly")).reshape(ndp, nb, -1, BLK)
    own, mid = got[:, :, :own_count], got[:, :, own_count:]
    return tuple(part.transpose(1, 0, 2, 3).reshape(nb, -1, BLK) for part in (own, mid))


def tokens_out(own, mid):
    ndp, nb = lax.axis_size("dp"), lax.axis_size("bfly")
    pairs = ndp // 2
    parts = [
        part.reshape(nb, ndp, -1, BLK).transpose(1, 0, 2, 3).reshape(ndp * nb, -1, BLK)
        for part in (own, mid)
    ]
    own_count = parts[0].shape[1]
    got = exchange(jnp.concatenate(parts, axis=1), ("dp", "bfly"))
    count = own_count * nb
    own, mid = got[:, :own_count], got[:, own_count:]
    own = own.reshape(pairs, 2, count, BLK)
    mid = mid.reshape(pairs, 1, count, BLK)
    sets = jnp.concatenate([own[:, :1], mid, own[:, 1:]], axis=1)
    return sets.transpose(2, 0, 1, 3).reshape(count, pairs * 3 * BLK)


def swap_sub(x):
    n, parts, width, count = x.shape
    return x.reshape(n, parts, n, width // n, count).transpose(2, 1, 0, 3, 4).reshape(x.shape)


def one_set(x, g, a, b, c, e):
    spread = mm("dti,drio->drot", x, a).astype(jnp.bfloat16)
    permuted = swap_sub(spread)
    gelu_value, gelu_slope = gelu_pair(mm("srit,srij->srjt", permuted, b))
    active = gelu_value.astype(jnp.bfloat16)
    returned = swap_sub(mm("srit,srij->srjt", active, c).astype(jnp.bfloat16))
    output = mm("drot,droj->dtj", returned, e).astype(jnp.bfloat16)
    back_mid = swap_sub(mm("dtj,droj->drot", g, e).astype(jnp.bfloat16))
    back_hidden = (mm("srjt,srij->srit", back_mid, c) * gelu_slope).astype(jnp.bfloat16)
    back_spread = swap_sub(mm("srjt,srij->srit", back_hidden, b).astype(jnp.bfloat16))
    grad_in = mm("drot,drio->dti", back_spread, a).astype(jnp.bfloat16)
    grad_a = mm("dti,drot->drio", x, back_spread).astype(jnp.bfloat16)
    grad_b = mm("srit,srjt->srij", permuted, back_hidden).astype(jnp.bfloat16)
    grad_c = mm("srit,srjt->srij", active, back_mid).astype(jnp.bfloat16)
    grad_e = mm("drot,dtj->droj", returned, g).astype(jnp.bfloat16)
    return output, grad_in, (grad_a, grad_b, grad_c, grad_e)


def token_plan(tokens, grad_out, weight_a, weight_b, weight_c, weight_e):
    ndp, nb = lax.axis_size("dp"), lax.axis_size("bfly")
    blocks, rows, _ = weight_a.shape
    parts = 2 * blocks
    dealt_a = weight_a.reshape(blocks, rows, 2, BLK).transpose(0, 2, 1, 3).reshape(parts, rows, BLK)
    dealt_e = weight_e.reshape(parts, rows, BLK)

    def weights_in(first, second):
        both = jnp.stack([deal_weight(first), deal_weight(second)], axis=1)
        full = gather_bfly(exchange(both, "dp"))
        return full

    ab = weights_in(dealt_a, weight_b)
    x_own, x_mid = tokens_in(tokens)
    ce = weights_in(weight_c, dealt_e)
    g_own, g_mid = tokens_in(grad_out)

    def by_rows(full, which, slot):
        return full[:, :, which, slot].transpose(0, 2, 1, 3, 4).reshape(nb, 2, BLK, BLK)

    def by_wide_rows(full, which, slot):
        return full[:, :, which, slot].reshape(nb, 2, BLK, BLK)

    results = []
    for slot, (x, g) in enumerate(((x_own, g_own), (x_mid, g_mid))):
        results.append(
            one_set(
                x,
                g,
                by_rows(ab, 0, slot),
                by_rows(ab, 1, slot),
                by_rows(ce, 0, slot),
                by_wide_rows(ce, 1, slot),
            )
        )
    output = tokens_out(results[0][0], results[1][0])
    grad_in = tokens_out(results[0][1], results[1][1])

    def grads_out(which, wide):
        own, mid = results[0][2][which], results[1][2][which]
        mine = scatter_bfly(jnp.stack([own, mid], axis=1))
        if wide:
            dealt = mine.reshape(2, ndp, 2, rows, BLK).transpose(1, 0, 2, 3, 4)
        else:
            dealt = mine.reshape(2, 2, ndp, rows, BLK).transpose(2, 0, 1, 3, 4)
        got = exchange(dealt, "dp").astype(jnp.float32)
        got = got.reshape(ndp // 2, 2, 2, 2, rows, BLK)
        mid = got[:, 0, 1] + got[:, 1, 1]
        return jnp.stack([got[:, 0, 0], mid, got[:, 1, 0]], axis=1).reshape(parts, rows, BLK)

    grad_e = grads_out(3, True).reshape(weight_e.shape)
    grad_c = grads_out(2, False)
    grad_b = grads_out(1, False)
    grad_a = grads_out(0, False)
    grad_a = grad_a.reshape(blocks, 2, rows, BLK).transpose(0, 2, 1, 3).reshape(weight_a.shape)
    return (output, grad_in, grad_a, grad_b, grad_c, grad_e)


def per_device(tokens, grad_out, weight_a, weight_b, weight_c, weight_e):
    ndp, nb = lax.axis_size("dp"), lax.axis_size("bfly")
    fits = nb == 4 and ndp % 2 == 0 and 2 * weight_a.shape[0] == 3 * ndp
    fits = fits and tokens.shape[0] % (32 * nb) == 0 and weight_a.shape[1] * ndp == BLK
    fits = fits and weight_a.shape[2] == 2 * BLK and weight_e.shape[1] == 2 * weight_a.shape[1]
    plan = token_plan if fits else any_mesh
    return plan(tokens, grad_out, weight_a, weight_b, weight_c, weight_e)


def solution(mesh):
    in_specs = (P("dp", "bfly"),) * 2 + (P("bfly", "dp", None),) * 4
    return jax.shard_map(
        per_device, mesh=mesh, in_specs=in_specs, out_specs=in_specs, check_vma=False
    )
```

```python
import jax
import jax.numpy as jnp
from jax import lax
from jax.experimental import pallas as pl
from jax.experimental.pallas import tpu as pltpu
from jax.sharding import PartitionSpec as P

BLK = 256

gelu_scale = 0.7978845608028654


def gelu_pair(hidden):
    inner_arg = gelu_scale * (hidden + 0.044715 * hidden * hidden * hidden)
    tangent = jnp.tanh(inner_arg)
    gelu_value = 0.5 * hidden * (1.0 + tangent)
    gelu_slope = 0.5 * (1.0 + tangent) + 0.5 * hidden * (1.0 - tangent * tangent) * gelu_scale * (
        1.0 + 3.0 * 0.044715 * hidden * hidden
    )
    return (gelu_value, gelu_slope)


def mm(spec, a, b):
    return jnp.einsum(spec, a, b, preferred_element_type=jnp.float32)


def regroup(piece, group_count):
    local_blocks, block_width, token_count = piece.shape
    stacked = piece.reshape(local_blocks, group_count, block_width // group_count, token_count)
    arrived = lax.all_to_all(stacked, "bfly", split_axis=1, concat_axis=1, tiled=True)
    return arrived.reshape(local_blocks, block_width, token_count)


def any_mesh(tokens, grad_out, weight_a, weight_b, weight_c, weight_e):
    group_count = lax.axis_size("bfly")
    full_a, full_b, full_c, full_e = (
        lax.all_gather(w, "dp", axis=1, tiled=True)
        for w in (weight_a, weight_b, weight_c, weight_e)
    )
    token_count = tokens.shape[0]
    inner_blocks = full_a.shape[0]
    spread_width = full_a.shape[2]
    local_blocks = full_b.shape[0]
    inputs = tokens.reshape(token_count, inner_blocks, BLK).transpose(1, 2, 0)
    upstream = grad_out.reshape(token_count, inner_blocks, BLK).transpose(1, 2, 0)
    hidden_view = (local_blocks, BLK, token_count)
    wide_view = (inner_blocks, spread_width, token_count)
    spread = mm("kit,kio->kot", inputs, full_a).astype(jnp.bfloat16).reshape(hidden_view)
    back_out = mm("kjt,koj->kot", upstream, full_e).astype(jnp.bfloat16).reshape(hidden_view)
    permuted = regroup(spread, group_count)
    back_mid = regroup(back_out, group_count)
    gelu_value, gelu_slope = gelu_pair(mm("qit,qij->qjt", permuted, full_b))
    active = gelu_value.astype(jnp.bfloat16)
    narrowed = mm("qit,qij->qjt", active, full_c).astype(jnp.bfloat16)
    back_hidden = (mm("qjt,qij->qit", back_mid, full_c) * gelu_slope).astype(jnp.bfloat16)
    back_first = mm("qjt,qij->qit", back_hidden, full_b).astype(jnp.bfloat16)
    returned = regroup(narrowed, group_count).reshape(wide_view)
    back_spread = regroup(back_first, group_count).reshape(wide_view)
    output = mm("kot,koj->kjt", returned, full_e)
    back_input = mm("kot,kio->kit", back_spread, full_a)
    parts = (
        mm("kit,kot->kio", inputs, back_spread),
        mm("qit,qjt->qij", permuted, back_hidden),
        mm("qit,qjt->qij", active, back_mid),
        mm("kot,kjt->koj", returned, upstream),
    )
    grads = tuple(
        lax.psum_scatter(part.astype(jnp.bfloat16), "dp", scatter_dimension=1, tiled=True).astype(
            jnp.float32
        )
        for part in parts
    )

    def rows(x):
        return x.astype(jnp.bfloat16).transpose(2, 0, 1).reshape(token_count, inner_blocks * BLK)

    return (rows(output), rows(back_input)) + grads


def xor_permute(x, mask):
    n = lax.axis_size("bfly")
    return lax.ppermute(x, "bfly", [(i, i ^ mask) for i in range(n)])


def exchange(x, axes):
    return lax.all_to_all(x, axes, split_axis=0, concat_axis=0, tiled=True)


def deal_weight(w):
    pairs = lax.axis_size("dp") // 2
    sets = w.reshape(pairs, 3, 2, w.shape[1], w.shape[2])
    own = jnp.stack([sets[:, 0], sets[:, 2]], axis=1)
    mid = jnp.stack([sets[:, 1], sets[:, 1]], axis=1)
    return jnp.stack([own, mid], axis=2).reshape((pairs * 2, 2) + sets.shape[2:])


def gather_bfly(w):
    across = xor_permute(w, 2)
    return [w, xor_permute(w, 1), across, xor_permute(across, 1)]


def add(x, y):
    return (x.astype(jnp.float32) + y.astype(jnp.float32)).astype(jnp.bfloat16)


def scatter_bfly(keep, send):
    half = add(keep, xor_permute(send, 1))
    return add(half[0], xor_permute(half[1], 2))


def deal_tokens(x):
    ndp, nb = lax.axis_size("dp"), lax.axis_size("bfly")
    pairs, count = ndp // 2, x.shape[0]
    view = x.reshape(count, pairs, 3, BLK)
    own = view[:, :, 0::2].reshape(nb, count // nb, ndp, BLK).transpose(2, 0, 1, 3)
    mid = view[:, :, 1].reshape(2, nb, count // nb // 2, pairs, BLK).transpose(3, 0, 1, 2, 4)
    mid = mid.reshape(ndp, nb, count // nb // 2, BLK)
    return jnp.concatenate([own, mid], axis=2).reshape(ndp * nb, -1, BLK)


def undeal_tokens(got, count):
    ndp, nb = lax.axis_size("dp"), lax.axis_size("bfly")
    pairs, own_count = ndp // 2, count // nb
    own = got[:, :own_count].reshape(pairs, 2, count, BLK)
    mid = got[:, own_count:].reshape(pairs, 1, count, BLK)
    sets = jnp.concatenate([own[:, :1], mid, own[:, 1:]], axis=1)
    return sets.transpose(2, 0, 1, 3).reshape(count, pairs * 3 * BLK)


def dot(x, y, contract_x, contract_y):
    dims = (((contract_x,), (contract_y,)), ((), ()))
    return lax.dot_general(x, y, dims, preferred_element_type=jnp.float32)


def square(x):
    return x.reshape(BLK, BLK)


def half_src(part, r):
    return pl.ds(r * (part // 2), part // 2)


def forward_kernel(f_ref, x_ref, *refs):
    ab, ce, (out_ref,), saved = refs[:4], refs[4:8], refs[8:9], (refs[9:13], refs[13:17])
    ndp, nb, all_rows, _ = x_ref.shape
    own_rows = 2 * all_rows // 3
    f = f_ref[0]
    for slot, (lo, hi) in enumerate(((0, own_rows), (own_rows, all_rows))):
        perm, active, slope, ret = saved[slot]
        count = ndp * (hi - lo)
        tiles = (nb, BLK // nb, count)
        for m in range(nb):
            d = f ^ m
            x = x_ref[:, d, lo:hi, :].reshape(count, BLK)
            for r in range(2):
                spread = dot(square(ab[m][:, 0, slot, r]), x, 0, 1).astype(jnp.bfloat16)
                perm[r, :, d] = spread.reshape(tiles)
        for m in range(nb):
            s = f ^ m
            for r in range(2):
                p = perm[r, s].reshape(BLK, count)
                value, grade = gelu_pair(dot(square(ab[m][:, 1, slot, r]), p, 0, 0))
                value = value.astype(jnp.bfloat16)
                active[r, s] = value
                slope[r, s] = grade.astype(jnp.bfloat16)
                narrowed = dot(square(ce[m][:, 0, slot, r]), value, 0, 0).astype(jnp.bfloat16)
                ret[r, :, s] = narrowed.reshape(tiles)
        for m in range(nb):
            d = f ^ m
            total = 0.0
            for r in range(2):
                e = square(ce[m][half_src(ndp, r), 1, slot])
                total = total + dot(ret[r, d].reshape(BLK, count), e, 0, 0)
            out_ref[:, d, lo:hi, :] = total.astype(jnp.bfloat16).reshape(ndp, hi - lo, BLK)


def backward_kernel(f_ref, x_ref, g_ref, *refs):
    ab, ce, saved = refs[:4], refs[4:8], (refs[8:12], refs[12:16])
    gin_ref, keep_ref, send_ref = refs[16:19]
    scratch = (refs[19:21], refs[21:23])
    ndp, nb, all_rows, _ = x_ref.shape
    own_rows = 2 * all_rows // 3
    rows = BLK // ndp
    f = f_ref[0]

    def grads(m):
        return (send_ref if m % 2 else keep_ref), m // 2

    for slot, (lo, hi) in enumerate(((0, own_rows), (own_rows, all_rows))):
        perm, active, slope, ret = saved[slot]
        mid, spread = scratch[slot]
        count = ndp * (hi - lo)
        tiles = (nb, BLK // nb, count)
        for m in range(nb):
            d = f ^ m
            g = g_ref[:, d, lo:hi, :].reshape(count, BLK)
            ref, at = grads(m)
            for r in range(2):
                e = square(ce[m][half_src(ndp, r), 1, slot])
                mid[r, :, d] = dot(e, g, 1, 1).astype(jnp.bfloat16).reshape(tiles)
                part = dot(ret[r, d].reshape(BLK, count), g, 1, 0).astype(jnp.bfloat16)
                ref[at, half_src(ndp, r), 3, slot] = part.reshape(ndp // 2, 2, rows, BLK)
        for m in range(nb):
            s = f ^ m
            ref, at = grads(m)
            for r in range(2):
                p = perm[r, s].reshape(BLK, count)
                back_mid = mid[r, s].reshape(BLK, count)
                back = dot(square(ce[m][:, 0, slot, r]), back_mid, 1, 0)
                back = (back * slope[r, s].astype(jnp.float32)).astype(jnp.bfloat16)
                part = dot(active[r, s], back_mid, 1, 1).astype(jnp.bfloat16)
                ref[at, :, 2, slot, r] = part.reshape(ndp, rows, BLK)
                part = dot(p, back, 1, 1).astype(jnp.bfloat16)
                ref[at, :, 1, slot, r] = part.reshape(ndp, rows, BLK)
                first = dot(square(ab[m][:, 1, slot, r]), back, 1, 0).astype(jnp.bfloat16)
                spread[r, :, s] = first.reshape(tiles)
        for m in range(nb):
            d = f ^ m
            x = x_ref[:, d, lo:hi, :].reshape(count, BLK)
            ref, at = grads(m)
            total = 0.0
            for r in range(2):
                back = spread[r, d].reshape(BLK, count)
                total = total + dot(back, square(ab[m][:, 0, slot, r]), 0, 1)
                part = dot(x, back, 0, 1).astype(jnp.bfloat16)
                ref[at, :, 0, slot, r] = part.reshape(ndp, rows, BLK)
            gin_ref[:, d, lo:hi, :] = total.astype(jnp.bfloat16).reshape(ndp, hi - lo, BLK)


def on_chip(kernel, outs, scratch, inputs):
    in_specs = [pl.BlockSpec(memory_space=pltpu.SMEM)]
    in_specs += [pl.BlockSpec(memory_space=pltpu.VMEM)] * (len(inputs) - 1)
    return pl.pallas_call(
        kernel,
        out_shape=[jax.ShapeDtypeStruct(shape, jnp.bfloat16) for shape in outs],
        in_specs=in_specs,
        out_specs=[pl.BlockSpec(memory_space=pltpu.VMEM)] * len(outs),
        scratch_shapes=[pltpu.VMEM(shape, jnp.bfloat16) for shape in scratch],
        compiler_params=pltpu.CompilerParams(vmem_limit_bytes=56 * 2**20),
    )(*inputs)


def token_plan(tokens, grad_out, weight_a, weight_b, weight_c, weight_e):
    ndp, nb = lax.axis_size("dp"), lax.axis_size("bfly")
    blocks, rows, _ = weight_a.shape
    parts, count = 2 * blocks, tokens.shape[0]
    dealt_a = weight_a.reshape(blocks, rows, 2, BLK).transpose(0, 2, 1, 3).reshape(parts, rows, BLK)
    dealt_e = weight_e.reshape(parts, rows, BLK)
    seat = lax.axis_index("bfly").astype(jnp.int32).reshape(1)

    def weights_in(first, second):
        both = jnp.stack([deal_weight(first), deal_weight(second)], axis=1)
        return gather_bfly(exchange(both, "dp"))

    everyone = ("dp", "bfly")
    ab = weights_in(dealt_a, weight_b)
    ce = weights_in(weight_c, dealt_e)
    x = exchange(deal_tokens(tokens), everyone).reshape(ndp, nb, -1, BLK)
    g = exchange(deal_tokens(grad_out), everyone).reshape(ndp, nb, -1, BLK)

    own, mid = count * ndp // nb, count * ndp // nb // 2
    saved = []
    for t in (own, mid):
        tiled, whole = (2, nb, nb, BLK // nb, t), (2, nb, BLK, t)
        saved += [tiled, whole, whole, tiled]
    out, *kept = on_chip(forward_kernel, [x.shape] + saved, [], [seat, x] + ab + ce)
    output = undeal_tokens(exchange(out.reshape(ndp * nb, -1, BLK), everyone), count)
    grad_shape = (2, ndp, 4, 2, 2, rows, BLK)
    gin, keep, send = on_chip(
        backward_kernel,
        [x.shape, grad_shape, grad_shape],
        [saved[0], saved[0], saved[4], saved[4]],
        [seat, x, g] + ab + ce + kept,
    )
    grad_in = undeal_tokens(exchange(gin.reshape(ndp * nb, -1, BLK), everyone), count)
    got = exchange(scatter_bfly(keep, send), "dp").astype(jnp.float32)
    got = got.reshape(ndp // 2, 2, 4, 2, 2, rows, BLK)

    def own_rows(which):
        mid = got[:, 0, which, 1] + got[:, 1, which, 1]
        return jnp.stack([got[:, 0, which, 0], mid, got[:, 1, which, 0]], axis=1)

    grad_a = own_rows(0).reshape(blocks, 2, rows, BLK).transpose(0, 2, 1, 3)
    return (
        output,
        grad_in,
        grad_a.reshape(weight_a.shape),
        own_rows(1).reshape(weight_b.shape),
        own_rows(2).reshape(weight_c.shape),
        own_rows(3).reshape(weight_e.shape),
    )


def per_device(tokens, grad_out, weight_a, weight_b, weight_c, weight_e):
    ndp, nb = lax.axis_size("dp"), lax.axis_size("bfly")
    fits = nb == 4 and ndp % 2 == 0 and 2 * weight_a.shape[0] == 3 * ndp
    fits = fits and tokens.shape[0] % (32 * nb) == 0 and weight_a.shape[1] * ndp == BLK
    fits = fits and weight_a.shape[2] == 2 * BLK and weight_e.shape[1] == 2 * weight_a.shape[1]
    plan = token_plan if fits else any_mesh
    return plan(tokens, grad_out, weight_a, weight_b, weight_c, weight_e)


def solution(mesh):
    in_specs = (P("dp", "bfly"),) * 2 + (P("bfly", "dp", None),) * 4
    return jax.shard_map(
        per_device, mesh=mesh, in_specs=in_specs, out_specs=in_specs, check_vma=False
    )
```

```python
import math

import jax
import jax.numpy as jnp
from jax import lax
from jax.experimental import pallas as pl
from jax.experimental.pallas import tpu as pltpu
from jax.sharding import PartitionSpec as P

BLK = 256

gelu_scale = 0.7978845608028654


def gelu_pair(hidden):
    inner_arg = gelu_scale * (hidden + 0.044715 * hidden * hidden * hidden)
    tangent = jnp.tanh(inner_arg)
    gelu_value = 0.5 * hidden * (1.0 + tangent)
    gelu_slope = 0.5 * (1.0 + tangent) + 0.5 * hidden * (1.0 - tangent * tangent) * gelu_scale * (
        1.0 + 3.0 * 0.044715 * hidden * hidden
    )
    return (gelu_value, gelu_slope)


def mm(spec, a, b):
    return jnp.einsum(spec, a, b, preferred_element_type=jnp.float32)


def regroup(piece, group_count):
    local_blocks, block_width, token_count = piece.shape
    stacked = piece.reshape(local_blocks, group_count, block_width // group_count, token_count)
    arrived = lax.all_to_all(stacked, "bfly", split_axis=1, concat_axis=1, tiled=True)
    return arrived.reshape(local_blocks, block_width, token_count)


def any_mesh(tokens, grad_out, weight_a, weight_b, weight_c, weight_e):
    group_count = lax.axis_size("bfly")
    full_a, full_b, full_c, full_e = (
        lax.all_gather(w, "dp", axis=1, tiled=True)
        for w in (weight_a, weight_b, weight_c, weight_e)
    )
    token_count = tokens.shape[0]
    inner_blocks = full_a.shape[0]
    spread_width = full_a.shape[2]
    local_blocks = full_b.shape[0]
    inputs = tokens.reshape(token_count, inner_blocks, BLK).transpose(1, 2, 0)
    upstream = grad_out.reshape(token_count, inner_blocks, BLK).transpose(1, 2, 0)
    hidden_view = (local_blocks, BLK, token_count)
    wide_view = (inner_blocks, spread_width, token_count)
    spread = mm("kit,kio->kot", inputs, full_a).astype(jnp.bfloat16).reshape(hidden_view)
    back_out = mm("kjt,koj->kot", upstream, full_e).astype(jnp.bfloat16).reshape(hidden_view)
    permuted = regroup(spread, group_count)
    back_mid = regroup(back_out, group_count)
    gelu_value, gelu_slope = gelu_pair(mm("qit,qij->qjt", permuted, full_b))
    active = gelu_value.astype(jnp.bfloat16)
    narrowed = mm("qit,qij->qjt", active, full_c).astype(jnp.bfloat16)
    back_hidden = (mm("qjt,qij->qit", back_mid, full_c) * gelu_slope).astype(jnp.bfloat16)
    back_first = mm("qjt,qij->qit", back_hidden, full_b).astype(jnp.bfloat16)
    returned = regroup(narrowed, group_count).reshape(wide_view)
    back_spread = regroup(back_first, group_count).reshape(wide_view)
    output = mm("kot,koj->kjt", returned, full_e)
    back_input = mm("kot,kio->kit", back_spread, full_a)
    parts = (
        mm("kit,kot->kio", inputs, back_spread),
        mm("qit,qjt->qij", permuted, back_hidden),
        mm("qit,qjt->qij", active, back_mid),
        mm("kot,kjt->koj", returned, upstream),
    )
    grads = tuple(
        lax.psum_scatter(part.astype(jnp.bfloat16), "dp", scatter_dimension=1, tiled=True).astype(
            jnp.float32
        )
        for part in parts
    )

    def rows(x):
        return x.astype(jnp.bfloat16).transpose(2, 0, 1).reshape(token_count, inner_blocks * BLK)

    return (rows(output), rows(back_input)) + grads


def xor_permute(x, mask):
    n = lax.axis_size("bfly")
    return lax.ppermute(x, "bfly", [(i, i ^ mask) for i in range(n)])


def exchange(x, axes):
    return lax.all_to_all(x, axes, split_axis=0, concat_axis=0, tiled=True)


def deal_weight(w):
    pairs = lax.axis_size("dp") // 2
    sets = w.reshape(pairs, 3, 2, w.shape[1], w.shape[2])
    own = jnp.stack([sets[:, 0], sets[:, 2]], axis=1)
    mid = jnp.stack([sets[:, 1], sets[:, 1]], axis=1)
    return jnp.stack([own, mid], axis=2).reshape((pairs * 2, 2) + sets.shape[2:])


def gather_bfly(w, across):
    return [w, xor_permute(w, 1), across, xor_permute(across, 1)]


def after(x, *earlier):
    return lax.optimization_barrier((x,) + earlier)[0]


def add(x, y):
    return (x.astype(jnp.float32) + y.astype(jnp.float32)).astype(jnp.bfloat16)


def deal_tokens(x):
    ndp, nb = lax.axis_size("dp"), lax.axis_size("bfly")
    pairs, count = ndp // 2, x.shape[0]
    view = x.reshape(count, pairs, 3, BLK)
    own = view[:, :, 0::2].reshape(nb, count // nb, ndp, BLK).transpose(2, 0, 1, 3)
    mid = view[:, :, 1].reshape(2, nb, count // nb // 2, pairs, BLK).transpose(3, 0, 1, 2, 4)
    mid = mid.reshape(ndp, nb, count // nb // 2, BLK)
    return jnp.concatenate([own, mid], axis=2).reshape(ndp * nb, -1, BLK)


def undeal_tokens(got, count):
    ndp, nb = lax.axis_size("dp"), lax.axis_size("bfly")
    pairs, own_count = ndp // 2, count // nb
    own = got[:, :own_count].reshape(pairs, 2, count, BLK)
    mid = got[:, own_count:].reshape(pairs, 1, count, BLK)
    sets = jnp.concatenate([own[:, :1], mid, own[:, 1:]], axis=1)
    return sets.transpose(2, 0, 1, 3).reshape(count, pairs * 3 * BLK)


def dot(x, y, contract_x, contract_y):
    dims = (((contract_x,), (contract_y,)), ((), ()))
    return lax.dot_general(x, y, dims, preferred_element_type=jnp.float32)


def square(x):
    return x.reshape(BLK, BLK)


def half_src(part, r):
    return pl.ds(r * (part // 2), part // 2)


def forward_kernel(f_ref, x_ref, *refs):
    ab, ce, (out_ref,), saved = refs[:4], refs[4:8], refs[8:9], (refs[9:13], refs[13:17])
    ndp, nb, all_rows, _ = x_ref.shape
    own_rows = 2 * all_rows // 3
    f = f_ref[0]
    for slot, (lo, hi) in enumerate(((0, own_rows), (own_rows, all_rows))):
        perm, active, slope, ret = saved[slot]
        count = ndp * (hi - lo)
        tiles = (nb, BLK // nb, count)
        for m in range(nb):
            d = f ^ m
            x = x_ref[:, d, lo:hi, :].reshape(count, BLK)
            for r in range(2):
                spread = dot(square(ab[m][:, 0, slot, r]), x, 0, 1).astype(jnp.bfloat16)
                perm[r, :, d] = spread.reshape(tiles)
        for m in range(nb):
            s = f ^ m
            for r in range(2):
                p = perm[r, s].reshape(BLK, count)
                value, grade = gelu_pair(dot(square(ab[m][:, 1, slot, r]), p, 0, 0))
                value = value.astype(jnp.bfloat16)
                active[r, s] = value
                slope[r, s] = grade.astype(jnp.bfloat16)
                narrowed = dot(square(ce[m][:, 0, slot, r]), value, 0, 0).astype(jnp.bfloat16)
                ret[r, :, s] = narrowed.reshape(tiles)
        for m in range(nb):
            d = f ^ m
            total = 0.0
            for r in range(2):
                e = square(ce[m][half_src(ndp, r), 1, slot])
                total = total + dot(ret[r, d].reshape(BLK, count), e, 0, 0)
            out_ref[:, d, lo:hi, :] = total.astype(jnp.bfloat16).reshape(ndp, hi - lo, BLK)


def backward_kernel(f_ref, x_ref, g_ref, *refs):
    ab, ce, saved = refs[:4], refs[4:8], (refs[8:12], refs[12:16])
    gin_ref, keep_ref, send_ref = refs[16:19]
    scratch = (refs[19:21], refs[21:23])
    ndp, nb, all_rows, _ = x_ref.shape
    own_rows = 2 * all_rows // 3
    rows = BLK // ndp
    f = f_ref[0]

    def grads(m):
        return (send_ref if m % 2 else keep_ref), m // 2

    for slot, (lo, hi) in enumerate(((0, own_rows), (own_rows, all_rows))):
        perm, active, slope, ret = saved[slot]
        mid, spread = scratch[slot]
        count = ndp * (hi - lo)
        tiles = (nb, BLK // nb, count)
        for m in range(nb):
            d = f ^ m
            g = g_ref[:, d, lo:hi, :].reshape(count, BLK)
            ref, at = grads(m)
            for r in range(2):
                e = square(ce[m][half_src(ndp, r), 1, slot])
                mid[r, :, d] = dot(e, g, 1, 1).astype(jnp.bfloat16).reshape(tiles)
                part = dot(ret[r, d].reshape(BLK, count), g, 1, 0).astype(jnp.bfloat16)
                ref[at, half_src(ndp, r), 3, slot] = part.reshape(ndp // 2, 2, rows, BLK)
        for m in range(nb):
            s = f ^ m
            ref, at = grads(m)
            for r in range(2):
                p = perm[r, s].reshape(BLK, count)
                back_mid = mid[r, s].reshape(BLK, count)
                back = dot(square(ce[m][:, 0, slot, r]), back_mid, 1, 0)
                back = (back * slope[r, s].astype(jnp.float32)).astype(jnp.bfloat16)
                part = dot(active[r, s], back_mid, 1, 1).astype(jnp.bfloat16)
                ref[at, :, 2, slot, r] = part.reshape(ndp, rows, BLK)
                part = dot(p, back, 1, 1).astype(jnp.bfloat16)
                ref[at, :, 1, slot, r] = part.reshape(ndp, rows, BLK)
                first = dot(square(ab[m][:, 1, slot, r]), back, 1, 0).astype(jnp.bfloat16)
                spread[r, :, s] = first.reshape(tiles)
        for m in range(nb):
            d = f ^ m
            x = x_ref[:, d, lo:hi, :].reshape(count, BLK)
            ref, at = grads(m)
            total = 0.0
            for r in range(2):
                back = spread[r, d].reshape(BLK, count)
                total = total + dot(back, square(ab[m][:, 0, slot, r]), 0, 1)
                part = dot(x, back, 0, 1).astype(jnp.bfloat16)
                ref[at, :, 0, slot, r] = part.reshape(ndp, rows, BLK)
            gin_ref[:, d, lo:hi, :] = total.astype(jnp.bfloat16).reshape(ndp, hi - lo, BLK)


def on_chip(kernel, products, outs, scratch, inputs):
    in_specs = [pl.BlockSpec(memory_space=pltpu.SMEM)]
    in_specs += [pl.BlockSpec(memory_space=pltpu.VMEM)] * (len(inputs) - 1)
    return pl.pallas_call(
        kernel,
        out_shape=[jax.ShapeDtypeStruct(shape, jnp.bfloat16) for shape in outs],
        in_specs=in_specs,
        out_specs=[pl.BlockSpec(memory_space=pltpu.VMEM)] * len(outs),
        scratch_shapes=[pltpu.VMEM(shape, jnp.bfloat16) for shape in scratch],
        cost_estimate=pl.CostEstimate(
            flops=products * 2 * BLK * BLK,
            transcendentals=0,
            bytes_accessed=sum(x.size for x in inputs) * 2 + sum(map(math.prod, outs)) * 2,
        ),
        compiler_params=pltpu.CompilerParams(vmem_limit_bytes=56 * 2**20),
    )(*inputs)


def token_plan(tokens, grad_out, weight_a, weight_b, weight_c, weight_e):
    ndp, nb = lax.axis_size("dp"), lax.axis_size("bfly")
    blocks, rows, _ = weight_a.shape
    parts, count = 2 * blocks, tokens.shape[0]
    dealt_a = weight_a.reshape(blocks, rows, 2, BLK).transpose(0, 2, 1, 3).reshape(parts, rows, BLK)
    dealt_e = weight_e.reshape(parts, rows, BLK)
    seat = lax.axis_index("bfly").astype(jnp.int32).reshape(1)

    def pack(first, second):
        return jnp.stack([deal_weight(first), deal_weight(second)], axis=1)

    everyone = ("dp", "bfly")
    shape = (ndp, nb, -1, BLK)
    ab = exchange(pack(dealt_a, weight_b), "dp")
    ab_across = xor_permute(ab, 2)
    ce = exchange(after(pack(weight_c, dealt_e), ab), "dp")
    ce_across = xor_permute(ce, 2)
    x = exchange(after(deal_tokens(tokens), ab_across, ce), everyone)
    g = exchange(after(deal_tokens(grad_out), ce_across, x), everyone).reshape(shape)
    x = x.reshape(shape)
    ab, ce = gather_bfly(ab, ab_across), gather_bfly(ce, ce_across)

    own, mid = count * ndp // nb, count * ndp // nb // 2
    saved = []
    for t in (own, mid):
        tiled, whole = (2, nb, nb, BLK // nb, t), (2, nb, BLK, t)
        saved += [tiled, whole, whole, tiled]
    products = 2 * nb * (own + mid)
    out, *kept = on_chip(forward_kernel, 4 * products, [x.shape] + saved, [], [seat, x] + ab + ce)
    out = exchange(out.reshape(ndp * nb, -1, BLK), everyone)
    grad_shape = (2, ndp, 4, 2, 2, rows, BLK)
    gin, keep, send = on_chip(
        backward_kernel,
        8 * products,
        [x.shape, grad_shape, grad_shape],
        [saved[0], saved[0], saved[4], saved[4]],
        [seat, x, g] + ab + ce + kept,
    )
    half = add(keep, xor_permute(send, 1))
    gin = exchange(after(gin.reshape(ndp * nb, -1, BLK), half, out), everyone)
    dealt = add(half[0], xor_permute(half[1], 2))
    got = exchange(after(dealt, gin), "dp").astype(jnp.float32)
    got = got.reshape(ndp // 2, 2, 4, 2, 2, rows, BLK)

    def own_rows(which):
        mid = got[:, 0, which, 1] + got[:, 1, which, 1]
        return jnp.stack([got[:, 0, which, 0], mid, got[:, 1, which, 0]], axis=1)

    grad_a = own_rows(0).reshape(blocks, 2, rows, BLK).transpose(0, 2, 1, 3)
    return (
        undeal_tokens(out, count),
        undeal_tokens(gin, count),
        grad_a.reshape(weight_a.shape),
        own_rows(1).reshape(weight_b.shape),
        own_rows(2).reshape(weight_c.shape),
        own_rows(3).reshape(weight_e.shape),
    )


def per_device(tokens, grad_out, weight_a, weight_b, weight_c, weight_e):
    ndp, nb = lax.axis_size("dp"), lax.axis_size("bfly")
    fits = nb == 4 and ndp % 2 == 0 and 2 * weight_a.shape[0] == 3 * ndp
    fits = fits and tokens.shape[0] % (32 * nb) == 0 and weight_a.shape[1] * ndp == BLK
    fits = fits and weight_a.shape[2] == 2 * BLK and weight_e.shape[1] == 2 * weight_a.shape[1]
    plan = token_plan if fits else any_mesh
    return plan(tokens, grad_out, weight_a, weight_b, weight_c, weight_e)


def solution(mesh):
    in_specs = (P("dp", "bfly"),) * 2 + (P("bfly", "dp", None),) * 4
    return jax.shard_map(
        per_device, mesh=mesh, in_specs=in_specs, out_specs=in_specs, check_vma=False
    )
```

```python
import math

import jax
import jax.numpy as jnp
from jax import lax
from jax.experimental import pallas as pl
from jax.experimental.pallas import tpu as pltpu
from jax.sharding import PartitionSpec as P

BLK = 256

gelu_scale = 0.7978845608028654


def gelu_pair(hidden):
    inner_arg = gelu_scale * (hidden + 0.044715 * hidden * hidden * hidden)
    tangent = jnp.tanh(inner_arg)
    gelu_value = 0.5 * hidden * (1.0 + tangent)
    gelu_slope = 0.5 * (1.0 + tangent) + 0.5 * hidden * (1.0 - tangent * tangent) * gelu_scale * (
        1.0 + 3.0 * 0.044715 * hidden * hidden
    )
    return (gelu_value, gelu_slope)


def mm(spec, a, b):
    return jnp.einsum(spec, a, b, preferred_element_type=jnp.float32)


def regroup(piece, group_count):
    local_blocks, block_width, token_count = piece.shape
    stacked = piece.reshape(local_blocks, group_count, block_width // group_count, token_count)
    arrived = lax.all_to_all(stacked, "bfly", split_axis=1, concat_axis=1, tiled=True)
    return arrived.reshape(local_blocks, block_width, token_count)


def any_mesh(tokens, grad_out, weight_a, weight_b, weight_c, weight_e):
    group_count = lax.axis_size("bfly")
    full_a, full_b, full_c, full_e = (
        lax.all_gather(w, "dp", axis=1, tiled=True)
        for w in (weight_a, weight_b, weight_c, weight_e)
    )
    token_count = tokens.shape[0]
    inner_blocks = full_a.shape[0]
    spread_width = full_a.shape[2]
    local_blocks = full_b.shape[0]
    inputs = tokens.reshape(token_count, inner_blocks, BLK).transpose(1, 2, 0)
    upstream = grad_out.reshape(token_count, inner_blocks, BLK).transpose(1, 2, 0)
    hidden_view = (local_blocks, BLK, token_count)
    wide_view = (inner_blocks, spread_width, token_count)
    spread = mm("kit,kio->kot", inputs, full_a).astype(jnp.bfloat16).reshape(hidden_view)
    back_out = mm("kjt,koj->kot", upstream, full_e).astype(jnp.bfloat16).reshape(hidden_view)
    permuted = regroup(spread, group_count)
    back_mid = regroup(back_out, group_count)
    gelu_value, gelu_slope = gelu_pair(mm("qit,qij->qjt", permuted, full_b))
    active = gelu_value.astype(jnp.bfloat16)
    narrowed = mm("qit,qij->qjt", active, full_c).astype(jnp.bfloat16)
    back_hidden = (mm("qjt,qij->qit", back_mid, full_c) * gelu_slope).astype(jnp.bfloat16)
    back_first = mm("qjt,qij->qit", back_hidden, full_b).astype(jnp.bfloat16)
    returned = regroup(narrowed, group_count).reshape(wide_view)
    back_spread = regroup(back_first, group_count).reshape(wide_view)
    output = mm("kot,koj->kjt", returned, full_e)
    back_input = mm("kot,kio->kit", back_spread, full_a)
    parts = (
        mm("kit,kot->kio", inputs, back_spread),
        mm("qit,qjt->qij", permuted, back_hidden),
        mm("qit,qjt->qij", active, back_mid),
        mm("kot,kjt->koj", returned, upstream),
    )
    grads = tuple(
        lax.psum_scatter(part.astype(jnp.bfloat16), "dp", scatter_dimension=1, tiled=True).astype(
            jnp.float32
        )
        for part in parts
    )

    def rows(x):
        return x.astype(jnp.bfloat16).transpose(2, 0, 1).reshape(token_count, inner_blocks * BLK)

    return (rows(output), rows(back_input)) + grads


def xor_permute(x, mask, axis="bfly"):
    return lax.ppermute(x, axis, [(i, i ^ mask) for i in range(lax.axis_size(axis))])


def exchange(x, axes):
    return lax.all_to_all(x, axes, split_axis=0, concat_axis=0, tiled=True)


def deal_weight(w):
    pairs = lax.axis_size("dp") // 2
    sets = w.reshape(pairs, 3, 2, w.shape[1], w.shape[2])
    own = jnp.stack([sets[:, 0], sets[:, 2]], axis=1)
    mid = sets[:, 1][:, :, None]
    return jnp.concatenate([own, mid], axis=2).reshape((pairs * 2, 3) + sets.shape[3:])


def gather_bfly(w, across):
    return [w, xor_permute(w, 1), across, xor_permute(across, 1)]


def after(x, *earlier):
    return lax.optimization_barrier((x,) + earlier)[0]


def add(x, y):
    return (x.astype(jnp.float32) + y.astype(jnp.float32)).astype(jnp.bfloat16)


def deal_tokens(x):
    ndp, nb = lax.axis_size("dp"), lax.axis_size("bfly")
    pairs, count = ndp // 2, x.shape[0]
    view = x.reshape(count, pairs, 3, BLK)
    own = view[:, :, 0::2].reshape(nb, count // nb, ndp, BLK).transpose(2, 0, 1, 3)
    mid = view[:, :, 1].reshape(2, nb, count // nb // 2, pairs, BLK).transpose(3, 0, 1, 2, 4)
    mid = mid.reshape(ndp, nb, count // nb // 2, BLK)
    return jnp.concatenate([own, mid], axis=2).reshape(ndp * nb, -1, BLK)


def undeal_tokens(got, count):
    ndp, nb = lax.axis_size("dp"), lax.axis_size("bfly")
    pairs, own_count = ndp // 2, count // nb
    own = got[:, :own_count].reshape(pairs, 2, count, BLK)
    mid = got[:, own_count:].reshape(pairs, 1, count, BLK)
    sets = jnp.concatenate([own[:, :1], mid, own[:, 1:]], axis=1)
    return sets.transpose(2, 0, 1, 3).reshape(count, pairs * 3 * BLK)


def dot(x, y, contract_x, contract_y):
    dims = (((contract_x,), (contract_y,)), ((), ()))
    return lax.dot_general(x, y, dims, preferred_element_type=jnp.float32)


def square(x):
    return x.reshape(BLK, BLK)


def half_src(part, r):
    return pl.ds(r * (part // 2), part // 2)


def weight_of(slot, w, v):
    def get(m, which, r):
        if slot == 0:
            return square(w[m][:, which, r])
        return square(v[m][:, which] if r else w[m][:, which, 2])

    return get


def wide_weight(slot, w, e_ref, y):
    def get(m, r):
        if slot == 0:
            return square(w[m][half_src(e_ref.shape[1], r), 3, :2])
        return square(e_ref[m, half_src(e_ref.shape[1], r ^ y)])

    return get


def join_halves(w, v, e_ref, y):
    for m in range(len(w)):
        e_ref[m, :, y] = w[m][:, 3, 2]
        e_ref[m, :, 1 - y] = v[m][:, 3]


def forward_kernel(seat_ref, x_ref, *refs):
    w, v, (out_ref,), saved, e_ref = refs[:4], refs[4:8], refs[8:9], (refs[9:13], refs[13:17]), refs[17]
    ndp, nb, all_rows, _ = x_ref.shape
    own_rows = 2 * all_rows // 3
    f, y = seat_ref[0], seat_ref[1]
    join_halves(w, v, e_ref, y)
    for slot, (lo, hi) in enumerate(((0, own_rows), (own_rows, all_rows))):
        perm, active, slope, ret = saved[slot]
        weight, wide = weight_of(slot, w, v), wide_weight(slot, w, e_ref, y)
        count = ndp * (hi - lo)
        tiles = (nb, BLK // nb, count)
        for m in range(nb):
            d = f ^ m
            x = x_ref[:, d, lo:hi, :].reshape(count, BLK)
            for r in range(2):
                spread = dot(weight(m, 0, r), x, 0, 1).astype(jnp.bfloat16)
                perm[r, :, d] = spread.reshape(tiles)
        for m in range(nb):
            s = f ^ m
            for r in range(2):
                p = perm[r, s].reshape(BLK, count)
                value, grade = gelu_pair(dot(weight(m, 1, r), p, 0, 0))
                value = value.astype(jnp.bfloat16)
                active[r, s] = value
                slope[r, s] = grade.astype(jnp.bfloat16)
                narrowed = dot(weight(m, 2, r), value, 0, 0).astype(jnp.bfloat16)
                ret[r, :, s] = narrowed.reshape(tiles)
        for m in range(nb):
            d = f ^ m
            total = 0.0
            for r in range(2):
                total = total + dot(ret[r, d].reshape(BLK, count), wide(m, r), 0, 0)
            out_ref[:, d, lo:hi, :] = total.astype(jnp.bfloat16).reshape(ndp, hi - lo, BLK)


def backward_kernel(seat_ref, x_ref, g_ref, *refs):
    w, v, saved = refs[:4], refs[4:8], (refs[8:12], refs[12:16])
    gin_ref, own_keep, own_send, mid_keep, mid_send = refs[16:21]
    scratch, e_ref = (refs[21:23], refs[23:25]), refs[25]
    ndp, nb, all_rows, _ = x_ref.shape
    own_rows = 2 * all_rows // 3
    rows = BLK // ndp
    f, y = seat_ref[0], seat_ref[1]
    join_halves(w, v, e_ref, y)

    def store(slot, m, which, r, part):
        ref = ((own_keep, own_send), (mid_keep, mid_send))[slot][m % 2]
        if slot == 0:
            ref[m // 2, :, which, r] = part.astype(jnp.bfloat16).reshape(ndp, rows, BLK)
        else:
            ref[r, m // 2, :, which] = part.astype(jnp.bfloat16).reshape(ndp, rows, BLK)

    def store_wide(slot, m, r, part):
        ref = ((own_keep, own_send), (mid_keep, mid_send))[slot][m % 2]
        part = part.astype(jnp.bfloat16).reshape(ndp // 2, 2, rows, BLK)
        if slot == 0:
            ref[m // 2, half_src(ndp, r), 3] = part
        else:
            ref[y, m // 2, half_src(ndp, r ^ y), 3] = part[:, 0]
            ref[1 - y, m // 2, half_src(ndp, r ^ y), 3] = part[:, 1]

    for slot, (lo, hi) in enumerate(((0, own_rows), (own_rows, all_rows))):
        perm, active, slope, ret = saved[slot]
        mid, spread = scratch[slot]
        weight, wide = weight_of(slot, w, v), wide_weight(slot, w, e_ref, y)
        count = ndp * (hi - lo)
        tiles = (nb, BLK // nb, count)
        for m in range(nb):
            d = f ^ m
            g = g_ref[:, d, lo:hi, :].reshape(count, BLK)
            for r in range(2):
                mid[r, :, d] = dot(wide(m, r), g, 1, 1).astype(jnp.bfloat16).reshape(tiles)
                store_wide(slot, m, r, dot(ret[r, d].reshape(BLK, count), g, 1, 0))
        for m in range(nb):
            s = f ^ m
            for r in range(2):
                p = perm[r, s].reshape(BLK, count)
                back_mid = mid[r, s].reshape(BLK, count)
                back = dot(weight(m, 2, r), back_mid, 1, 0)
                back = (back * slope[r, s].astype(jnp.float32)).astype(jnp.bfloat16)
                store(slot, m, 2, r, dot(active[r, s], back_mid, 1, 1))
                store(slot, m, 1, r, dot(p, back, 1, 1))
                first = dot(weight(m, 1, r), back, 1, 0).astype(jnp.bfloat16)
                spread[r, :, s] = first.reshape(tiles)
        for m in range(nb):
            d = f ^ m
            x = x_ref[:, d, lo:hi, :].reshape(count, BLK)
            total = 0.0
            for r in range(2):
                back = spread[r, d].reshape(BLK, count)
                total = total + dot(back, weight(m, 0, r), 0, 1)
                store(slot, m, 0, r, dot(x, back, 0, 1))
            gin_ref[:, d, lo:hi, :] = total.astype(jnp.bfloat16).reshape(ndp, hi - lo, BLK)


def on_chip(kernel, products, outs, scratch, inputs):
    in_specs = [pl.BlockSpec(memory_space=pltpu.SMEM)]
    in_specs += [pl.BlockSpec(memory_space=pltpu.VMEM)] * (len(inputs) - 1)
    return pl.pallas_call(
        kernel,
        out_shape=[jax.ShapeDtypeStruct(shape, jnp.bfloat16) for shape in outs],
        in_specs=in_specs,
        out_specs=[pl.BlockSpec(memory_space=pltpu.VMEM)] * len(outs),
        scratch_shapes=[pltpu.VMEM(shape, jnp.bfloat16) for shape in scratch],
        cost_estimate=pl.CostEstimate(
            flops=products * 2 * BLK * BLK,
            transcendentals=0,
            bytes_accessed=sum(x.size for x in inputs) * 2 + sum(map(math.prod, outs)) * 2,
        ),
        compiler_params=pltpu.CompilerParams(vmem_limit_bytes=56 * 2**20),
    )(*inputs)


def token_plan(tokens, grad_out, weight_a, weight_b, weight_c, weight_e):
    ndp, nb = lax.axis_size("dp"), lax.axis_size("bfly")
    blocks, rows, _ = weight_a.shape
    parts, count = 2 * blocks, tokens.shape[0]
    dealt_a = weight_a.reshape(blocks, rows, 2, BLK).transpose(0, 2, 1, 3).reshape(parts, rows, BLK)
    dealt_e = weight_e.reshape(parts, rows, BLK)
    seat = jnp.stack([lax.axis_index("bfly"), lax.axis_index("dp") % 2]).astype(jnp.int32)

    everyone = ("dp", "bfly")
    shape = (ndp, nb, -1, BLK)
    dealt = [deal_weight(w) for w in (dealt_a, weight_b, weight_c, dealt_e)]
    w = exchange(jnp.stack(dealt, axis=1), "dp")
    across = xor_permute(w, 2)
    v = xor_permute(w[:, :, 2], 1, "dp")
    x = exchange(after(deal_tokens(tokens), w), everyone)
    g = exchange(after(deal_tokens(grad_out), x), everyone).reshape(shape)
    x = x.reshape(shape)
    weights = gather_bfly(w, across) + gather_bfly(v, xor_permute(across[:, :, 2], 1, "dp"))

    own, mid = count * ndp // nb, count * ndp // nb // 2
    saved = []
    for t in (own, mid):
        tiled, whole = (2, nb, nb, BLK // nb, t), (2, nb, BLK, t)
        saved += [tiled, whole, whole, tiled]
    halves = (nb, ndp, 2, rows, BLK)
    products = 2 * nb * (own + mid)
    out, *kept = on_chip(
        forward_kernel, 4 * products, [x.shape] + saved, [halves], [seat, x] + weights
    )
    out = exchange(out.reshape(ndp * nb, -1, BLK), everyone)
    own_shape, mid_shape = (2, ndp, 4, 2, rows, BLK), (2, 2, ndp, 4, rows, BLK)
    gin, own_keep, own_send, mid_keep, mid_send = on_chip(
        backward_kernel,
        8 * products,
        [x.shape, own_shape, own_shape, mid_shape, mid_shape],
        [saved[0], saved[0], saved[4], saved[4], halves],
        [seat, x, g] + weights + kept,
    )
    mid = add(mid_keep, xor_permute(mid_send, 1))
    own = add(own_keep, xor_permute(own_send, 1))
    mid = add(mid[0], xor_permute(mid[1], 1, "dp"))
    gin = exchange(after(gin.reshape(ndp * nb, -1, BLK), out), everyone)
    own = add(own[0], xor_permute(own[1], 2))
    mid = add(mid[0], xor_permute(mid[1], 2))
    dealt = jnp.concatenate([own, mid[:, :, None]], axis=2)
    got = exchange(after(dealt, gin), "dp").astype(jnp.float32)
    got = got.reshape(ndp // 2, 2, 4, 3, rows, BLK)

    def own_rows(which):
        mid = jnp.stack([got[:, 0, which, 2], got[:, 1, which, 2]], axis=1)
        return jnp.stack([got[:, 0, which, :2], mid, got[:, 1, which, :2]], axis=1)

    grad_a = own_rows(0).reshape(blocks, 2, rows, BLK).transpose(0, 2, 1, 3)
    return (
        undeal_tokens(out, count),
        undeal_tokens(gin, count),
        grad_a.reshape(weight_a.shape),
        own_rows(1).reshape(weight_b.shape),
        own_rows(2).reshape(weight_c.shape),
        own_rows(3).reshape(weight_e.shape),
    )


def per_device(tokens, grad_out, weight_a, weight_b, weight_c, weight_e):
    ndp, nb = lax.axis_size("dp"), lax.axis_size("bfly")
    fits = nb == 4 and ndp % 2 == 0 and 2 * weight_a.shape[0] == 3 * ndp
    fits = fits and tokens.shape[0] % (32 * nb) == 0 and weight_a.shape[1] * ndp == BLK
    fits = fits and weight_a.shape[2] == 2 * BLK and weight_e.shape[1] == 2 * weight_a.shape[1]
    plan = token_plan if fits else any_mesh
    return plan(tokens, grad_out, weight_a, weight_b, weight_c, weight_e)


def solution(mesh):
    in_specs = (P("dp", "bfly"),) * 2 + (P("bfly", "dp", None),) * 4
    return jax.shard_map(
        per_device, mesh=mesh, in_specs=in_specs, out_specs=in_specs, check_vma=False
    )
```

```python
import math

import jax
import jax.numpy as jnp
from jax import lax
from jax.experimental import pallas as pl
from jax.experimental.pallas import tpu as pltpu
from jax.sharding import PartitionSpec as P

BLK = 256

gelu_scale = 0.7978845608028654


def gelu_pair(hidden):
    inner_arg = gelu_scale * (hidden + 0.044715 * hidden * hidden * hidden)
    tangent = jnp.tanh(inner_arg)
    gelu_value = 0.5 * hidden * (1.0 + tangent)
    gelu_slope = 0.5 * (1.0 + tangent) + 0.5 * hidden * (1.0 - tangent * tangent) * gelu_scale * (
        1.0 + 3.0 * 0.044715 * hidden * hidden
    )
    return (gelu_value, gelu_slope)


def mm(spec, a, b):
    return jnp.einsum(spec, a, b, preferred_element_type=jnp.float32)


def regroup(piece, group_count):
    local_blocks, block_width, token_count = piece.shape
    stacked = piece.reshape(local_blocks, group_count, block_width // group_count, token_count)
    arrived = lax.all_to_all(stacked, "bfly", split_axis=1, concat_axis=1, tiled=True)
    return arrived.reshape(local_blocks, block_width, token_count)


def any_mesh(tokens, grad_out, weight_a, weight_b, weight_c, weight_e):
    group_count = lax.axis_size("bfly")
    full_a, full_b, full_c, full_e = (
        lax.all_gather(w, "dp", axis=1, tiled=True)
        for w in (weight_a, weight_b, weight_c, weight_e)
    )
    token_count = tokens.shape[0]
    inner_blocks = full_a.shape[0]
    spread_width = full_a.shape[2]
    local_blocks = full_b.shape[0]
    inputs = tokens.reshape(token_count, inner_blocks, BLK).transpose(1, 2, 0)
    upstream = grad_out.reshape(token_count, inner_blocks, BLK).transpose(1, 2, 0)
    hidden_view = (local_blocks, BLK, token_count)
    wide_view = (inner_blocks, spread_width, token_count)
    spread = mm("kit,kio->kot", inputs, full_a).astype(jnp.bfloat16).reshape(hidden_view)
    back_out = mm("kjt,koj->kot", upstream, full_e).astype(jnp.bfloat16).reshape(hidden_view)
    permuted = regroup(spread, group_count)
    back_mid = regroup(back_out, group_count)
    gelu_value, gelu_slope = gelu_pair(mm("qit,qij->qjt", permuted, full_b))
    active = gelu_value.astype(jnp.bfloat16)
    narrowed = mm("qit,qij->qjt", active, full_c).astype(jnp.bfloat16)
    back_hidden = (mm("qjt,qij->qit", back_mid, full_c) * gelu_slope).astype(jnp.bfloat16)
    back_first = mm("qjt,qij->qit", back_hidden, full_b).astype(jnp.bfloat16)
    returned = regroup(narrowed, group_count).reshape(wide_view)
    back_spread = regroup(back_first, group_count).reshape(wide_view)
    output = mm("kot,koj->kjt", returned, full_e)
    back_input = mm("kot,kio->kit", back_spread, full_a)
    parts = (
        mm("kit,kot->kio", inputs, back_spread),
        mm("qit,qjt->qij", permuted, back_hidden),
        mm("qit,qjt->qij", active, back_mid),
        mm("kot,kjt->koj", returned, upstream),
    )
    grads = tuple(
        lax.psum_scatter(part.astype(jnp.bfloat16), "dp", scatter_dimension=1, tiled=True).astype(
            jnp.float32
        )
        for part in parts
    )

    def rows(x):
        return x.astype(jnp.bfloat16).transpose(2, 0, 1).reshape(token_count, inner_blocks * BLK)

    return (rows(output), rows(back_input)) + grads


def xor_permute(x, mask, axis="bfly"):
    return lax.ppermute(x, axis, [(i, i ^ mask) for i in range(lax.axis_size(axis))])


def exchange(x, axes):
    return lax.all_to_all(x, axes, split_axis=0, concat_axis=0, tiled=True)


def deal_weight(w):
    pairs = lax.axis_size("dp") // 2
    sets = w.reshape(pairs, 3, 2, w.shape[1], w.shape[2])
    own = jnp.stack([sets[:, 0], sets[:, 2]], axis=1)
    mid = sets[:, 1][:, :, None]
    return jnp.concatenate([own, mid], axis=2).reshape((pairs * 2, 3) + sets.shape[3:])


def gather_bfly(w, across):
    return [w, xor_permute(w, 1), across, xor_permute(across, 1)]


def after(x, *earlier):
    return lax.optimization_barrier((x,) + earlier)[0]


def add(x, y):
    return (x.astype(jnp.float32) + y.astype(jnp.float32)).astype(jnp.bfloat16)


def deal_tokens(x):
    ndp, nb = lax.axis_size("dp"), lax.axis_size("bfly")
    pairs, count = ndp // 2, x.shape[0]
    view = x.reshape(count, pairs, 3, BLK)
    own = view[:, :, 0::2].reshape(nb, count // nb, ndp, BLK).transpose(2, 0, 1, 3)
    mid = view[:, :, 1].reshape(2, nb, count // nb // 2, pairs, BLK).transpose(3, 0, 1, 2, 4)
    mid = mid.reshape(ndp, nb, count // nb // 2, BLK)
    return jnp.concatenate([own, mid], axis=2).reshape(ndp * nb, -1, BLK)


def undeal_tokens(got, count):
    ndp, nb = lax.axis_size("dp"), lax.axis_size("bfly")
    pairs, own_count = ndp // 2, count // nb
    own = got[:, :own_count].reshape(pairs, 2, count, BLK)
    mid = got[:, own_count:].reshape(pairs, 1, count, BLK)
    sets = jnp.concatenate([own[:, :1], mid, own[:, 1:]], axis=1)
    return sets.transpose(2, 0, 1, 3).reshape(count, pairs * 3 * BLK)


def dot(x, y, contract_x, contract_y):
    dims = (((contract_x,), (contract_y,)), ((), ()))
    return lax.dot_general(x, y, dims, preferred_element_type=jnp.float32)


def square(x):
    return x.reshape(BLK, BLK)


def half_src(part, r):
    return pl.ds(r * (part // 2), part // 2)


def weight_of(slot, w, v):
    def get(m, which, r):
        if slot == 0:
            return square(w[which // 2][m][:, which % 2, r])
        return square(v[m][r, :, which])

    return get


def wide_weight(slot, w, e_ref, y):
    def get(m, r):
        if slot == 0:
            return square(w[1][m][half_src(e_ref.shape[1], r), 1])
        return square(e_ref[m, half_src(e_ref.shape[1], r ^ y)])

    return get


def join_halves(v, e_ref, y):
    for m in range(len(v)):
        e_ref[m, :, y] = v[m][0, :, 3]
        e_ref[m, :, 1 - y] = v[m][1, :, 3]


def forward_kernel(seat_ref, x_ref, *refs):
    w, v, out_ref, saved = (refs[:4], refs[4:8]), refs[8:12], refs[12], (refs[13:17], refs[17:21])
    e_ref = refs[21]
    ndp, nb, all_rows, _ = x_ref.shape
    own_rows = 2 * all_rows // 3
    f, y = seat_ref[0], seat_ref[1]
    join_halves(v, e_ref, y)
    for slot, (lo, hi) in enumerate(((0, own_rows), (own_rows, all_rows))):
        perm, active, slope, ret = saved[slot]
        weight, wide = weight_of(slot, w, v), wide_weight(slot, w, e_ref, y)
        count = ndp * (hi - lo)
        tiles = (nb, BLK // nb, count)
        for m in range(nb):
            d = f ^ m
            x = x_ref[:, d, lo:hi, :].reshape(count, BLK)
            for r in range(2):
                spread = dot(weight(m, 0, r), x, 0, 1).astype(jnp.bfloat16)
                perm[r, :, d] = spread.reshape(tiles)
        for m in range(nb):
            s = f ^ m
            for r in range(2):
                p = perm[r, s].reshape(BLK, count)
                value, grade = gelu_pair(dot(weight(m, 1, r), p, 0, 0))
                value = value.astype(jnp.bfloat16)
                active[r, s] = value
                slope[r, s] = grade.astype(jnp.bfloat16)
                narrowed = dot(weight(m, 2, r), value, 0, 0).astype(jnp.bfloat16)
                ret[r, :, s] = narrowed.reshape(tiles)
        for m in range(nb):
            d = f ^ m
            total = 0.0
            for r in range(2):
                total = total + dot(ret[r, d].reshape(BLK, count), wide(m, r), 0, 0)
            out_ref[:, d, lo:hi, :] = total.astype(jnp.bfloat16).reshape(ndp, hi - lo, BLK)


def backward_kernel(seat_ref, x_ref, g_ref, *refs):
    w, v, saved = (refs[:4], refs[4:8]), refs[8:12], (refs[12:16], refs[16:20])
    gin_ref, own_keep, own_send, mid_keep, mid_send = refs[20:25]
    scratch, e_ref = (refs[25:27], refs[27:29]), refs[29]
    ndp, nb, all_rows, _ = x_ref.shape
    own_rows = 2 * all_rows // 3
    rows = BLK // ndp
    f, y = seat_ref[0], seat_ref[1]
    join_halves(v, e_ref, y)

    def store(slot, m, which, r, part):
        ref = ((own_keep, own_send), (mid_keep, mid_send))[slot][m % 2]
        if slot == 0:
            ref[m // 2, :, which, r] = part.astype(jnp.bfloat16).reshape(ndp, rows, BLK)
        else:
            ref[r, m // 2, :, which] = part.astype(jnp.bfloat16).reshape(ndp, rows, BLK)

    def store_wide(slot, m, r, part):
        ref = ((own_keep, own_send), (mid_keep, mid_send))[slot][m % 2]
        part = part.astype(jnp.bfloat16).reshape(ndp // 2, 2, rows, BLK)
        if slot == 0:
            ref[m // 2, half_src(ndp, r), 3] = part
        else:
            ref[y, m // 2, half_src(ndp, r ^ y), 3] = part[:, 0]
            ref[1 - y, m // 2, half_src(ndp, r ^ y), 3] = part[:, 1]

    for slot, (lo, hi) in enumerate(((0, own_rows), (own_rows, all_rows))):
        perm, active, slope, ret = saved[slot]
        mid, spread = scratch[slot]
        weight, wide = weight_of(slot, w, v), wide_weight(slot, w, e_ref, y)
        count = ndp * (hi - lo)
        tiles = (nb, BLK // nb, count)
        for m in range(nb):
            d = f ^ m
            g = g_ref[:, d, lo:hi, :].reshape(count, BLK)
            for r in range(2):
                mid[r, :, d] = dot(wide(m, r), g, 1, 1).astype(jnp.bfloat16).reshape(tiles)
                store_wide(slot, m, r, dot(ret[r, d].reshape(BLK, count), g, 1, 0))
        for m in range(nb):
            s = f ^ m
            for r in range(2):
                p = perm[r, s].reshape(BLK, count)
                back_mid = mid[r, s].reshape(BLK, count)
                back = dot(weight(m, 2, r), back_mid, 1, 0)
                back = (back * slope[r, s].astype(jnp.float32)).astype(jnp.bfloat16)
                store(slot, m, 2, r, dot(active[r, s], back_mid, 1, 1))
                store(slot, m, 1, r, dot(p, back, 1, 1))
                first = dot(weight(m, 1, r), back, 1, 0).astype(jnp.bfloat16)
                spread[r, :, s] = first.reshape(tiles)
        for m in range(nb):
            d = f ^ m
            x = x_ref[:, d, lo:hi, :].reshape(count, BLK)
            total = 0.0
            for r in range(2):
                back = spread[r, d].reshape(BLK, count)
                total = total + dot(back, weight(m, 0, r), 0, 1)
                store(slot, m, 0, r, dot(x, back, 0, 1))
            gin_ref[:, d, lo:hi, :] = total.astype(jnp.bfloat16).reshape(ndp, hi - lo, BLK)


def on_chip(kernel, products, outs, scratch, inputs):
    in_specs = [pl.BlockSpec(memory_space=pltpu.SMEM)]
    in_specs += [pl.BlockSpec(memory_space=pltpu.VMEM)] * (len(inputs) - 1)
    return pl.pallas_call(
        kernel,
        out_shape=[jax.ShapeDtypeStruct(shape, jnp.bfloat16) for shape in outs],
        in_specs=in_specs,
        out_specs=[pl.BlockSpec(memory_space=pltpu.VMEM)] * len(outs),
        scratch_shapes=[pltpu.VMEM(shape, jnp.bfloat16) for shape in scratch],
        cost_estimate=pl.CostEstimate(
            flops=products * 2 * BLK * BLK,
            transcendentals=0,
            bytes_accessed=sum(x.size for x in inputs) * 2 + sum(map(math.prod, outs)) * 2,
        ),
        compiler_params=pltpu.CompilerParams(vmem_limit_bytes=56 * 2**20),
    )(*inputs)


def token_plan(tokens, grad_out, weight_a, weight_b, weight_c, weight_e):
    ndp, nb = lax.axis_size("dp"), lax.axis_size("bfly")
    blocks, rows, _ = weight_a.shape
    parts, count = 2 * blocks, tokens.shape[0]
    dealt_a = weight_a.reshape(blocks, rows, 2, BLK).transpose(0, 2, 1, 3).reshape(parts, rows, BLK)
    dealt_e = weight_e.reshape(parts, rows, BLK)
    seat = jnp.stack([lax.axis_index("bfly"), lax.axis_index("dp") % 2]).astype(jnp.int32)

    everyone = ("dp", "bfly")
    shape = (ndp, nb, -1, BLK)
    dealt = [deal_weight(w) for w in (dealt_a, weight_b, weight_c, dealt_e)]
    w = exchange(jnp.stack(dealt, axis=1), "dp")
    parts_in = (w[:, :, 2], w[:, :2, :2], w[:, 2:, :2])
    mid_across, ab_across, ce_across = (xor_permute(part, 2) for part in parts_in)
    x = exchange(after(deal_tokens(tokens), w), everyone)
    mid_swapped = xor_permute(parts_in[0], 1, "dp")
    g = after(deal_tokens(grad_out), x, mid_across, ab_across, mid_swapped)
    g = exchange(g, everyone).reshape(shape)
    x = x.reshape(shape)
    both = [
        jnp.stack([parts_in[0], mid_swapped]),
        jnp.stack([mid_across, xor_permute(mid_across, 1, "dp")]),
    ]
    weights = gather_bfly(parts_in[1], ab_across) + gather_bfly(parts_in[2], ce_across)
    weights += gather_bfly(*both)

    own, mid = count * ndp // nb, count * ndp // nb // 2
    saved = []
    for t in (own, mid):
        tiled, whole = (2, nb, nb, BLK // nb, t), (2, nb, BLK, t)
        saved += [tiled, whole, whole, tiled]
    halves = (nb, ndp, 2, rows, BLK)
    products = 2 * nb * (own + mid)
    out, *kept = on_chip(
        forward_kernel, 4 * products, [x.shape] + saved, [halves], [seat, x] + weights
    )
    out = exchange(out.reshape(ndp * nb, -1, BLK), everyone)
    own_shape, mid_shape = (2, ndp, 4, 2, rows, BLK), (2, 2, ndp, 4, rows, BLK)
    gin, own_keep, own_send, mid_keep, mid_send = on_chip(
        backward_kernel,
        8 * products,
        [x.shape, own_shape, own_shape, mid_shape, mid_shape],
        [saved[0], saved[0], saved[4], saved[4], halves],
        [seat, x, g] + weights + kept,
    )
    half_mid = mid = add(mid_keep, xor_permute(mid_send, 1))
    half_own = own = add(own_keep, xor_permute(own_send, 1))
    mid = add(mid[0], xor_permute(mid[1], 1, "dp"))
    gin = exchange(after(gin.reshape(ndp * nb, -1, BLK), out, half_mid, half_own), everyone)
    own = add(own[0], xor_permute(own[1], 2))
    mid = add(mid[0], xor_permute(mid[1], 2))
    dealt = jnp.concatenate([own, mid[:, :, None]], axis=2)
    got = exchange(after(dealt, gin), "dp").astype(jnp.float32)
    got = got.reshape(ndp // 2, 2, 4, 3, rows, BLK)

    def own_rows(which):
        mid = jnp.stack([got[:, 0, which, 2], got[:, 1, which, 2]], axis=1)
        return jnp.stack([got[:, 0, which, :2], mid, got[:, 1, which, :2]], axis=1)

    grad_a = own_rows(0).reshape(blocks, 2, rows, BLK).transpose(0, 2, 1, 3)
    return (
        undeal_tokens(out, count),
        undeal_tokens(gin, count),
        grad_a.reshape(weight_a.shape),
        own_rows(1).reshape(weight_b.shape),
        own_rows(2).reshape(weight_c.shape),
        own_rows(3).reshape(weight_e.shape),
    )


def per_device(tokens, grad_out, weight_a, weight_b, weight_c, weight_e):
    ndp, nb = lax.axis_size("dp"), lax.axis_size("bfly")
    fits = nb == 4 and ndp % 2 == 0 and 2 * weight_a.shape[0] == 3 * ndp
    fits = fits and tokens.shape[0] % (32 * nb) == 0 and weight_a.shape[1] * ndp == BLK
    fits = fits and weight_a.shape[2] == 2 * BLK and weight_e.shape[1] == 2 * weight_a.shape[1]
    plan = token_plan if fits else any_mesh
    return plan(tokens, grad_out, weight_a, weight_b, weight_c, weight_e)


def solution(mesh):
    in_specs = (P("dp", "bfly"),) * 2 + (P("bfly", "dp", None),) * 4
    return jax.shard_map(
        per_device, mesh=mesh, in_specs=in_specs, out_specs=in_specs, check_vma=False
    )
```

```python
import functools
import math

import jax
import jax.numpy as jnp
from jax import lax
from jax.experimental import pallas as pl
from jax.experimental.pallas import tpu as pltpu
from jax.sharding import PartitionSpec as P

BLK = 256

gelu_scale = 0.7978845608028654


def gelu_pair(hidden):
    inner_arg = gelu_scale * (hidden + 0.044715 * hidden * hidden * hidden)
    tangent = jnp.tanh(inner_arg)
    gelu_value = 0.5 * hidden * (1.0 + tangent)
    gelu_slope = 0.5 * (1.0 + tangent) + 0.5 * hidden * (1.0 - tangent * tangent) * gelu_scale * (
        1.0 + 3.0 * 0.044715 * hidden * hidden
    )
    return (gelu_value, gelu_slope)


def mm(spec, a, b):
    return jnp.einsum(spec, a, b, preferred_element_type=jnp.float32)


def regroup(piece, group_count):
    local_blocks, block_width, token_count = piece.shape
    stacked = piece.reshape(local_blocks, group_count, block_width // group_count, token_count)
    arrived = lax.all_to_all(stacked, "bfly", split_axis=1, concat_axis=1, tiled=True)
    return arrived.reshape(local_blocks, block_width, token_count)


def any_mesh(tokens, grad_out, weight_a, weight_b, weight_c, weight_e):
    group_count = lax.axis_size("bfly")
    full_a, full_b, full_c, full_e = (
        lax.all_gather(w, "dp", axis=1, tiled=True)
        for w in (weight_a, weight_b, weight_c, weight_e)
    )
    token_count = tokens.shape[0]
    inner_blocks = full_a.shape[0]
    spread_width = full_a.shape[2]
    local_blocks = full_b.shape[0]
    inputs = tokens.reshape(token_count, inner_blocks, BLK).transpose(1, 2, 0)
    upstream = grad_out.reshape(token_count, inner_blocks, BLK).transpose(1, 2, 0)
    hidden_view = (local_blocks, BLK, token_count)
    wide_view = (inner_blocks, spread_width, token_count)
    spread = mm("kit,kio->kot", inputs, full_a).astype(jnp.bfloat16).reshape(hidden_view)
    back_out = mm("kjt,koj->kot", upstream, full_e).astype(jnp.bfloat16).reshape(hidden_view)
    permuted = regroup(spread, group_count)
    back_mid = regroup(back_out, group_count)
    gelu_value, gelu_slope = gelu_pair(mm("qit,qij->qjt", permuted, full_b))
    active = gelu_value.astype(jnp.bfloat16)
    narrowed = mm("qit,qij->qjt", active, full_c).astype(jnp.bfloat16)
    back_hidden = (mm("qjt,qij->qit", back_mid, full_c) * gelu_slope).astype(jnp.bfloat16)
    back_first = mm("qjt,qij->qit", back_hidden, full_b).astype(jnp.bfloat16)
    returned = regroup(narrowed, group_count).reshape(wide_view)
    back_spread = regroup(back_first, group_count).reshape(wide_view)
    output = mm("kot,koj->kjt", returned, full_e)
    back_input = mm("kot,kio->kit", back_spread, full_a)
    parts = (
        mm("kit,kot->kio", inputs, back_spread),
        mm("qit,qjt->qij", permuted, back_hidden),
        mm("qit,qjt->qij", active, back_mid),
        mm("kot,kjt->koj", returned, upstream),
    )
    grads = tuple(
        lax.psum_scatter(part.astype(jnp.bfloat16), "dp", scatter_dimension=1, tiled=True).astype(
            jnp.float32
        )
        for part in parts
    )

    def rows(x):
        return x.astype(jnp.bfloat16).transpose(2, 0, 1).reshape(token_count, inner_blocks * BLK)

    return (rows(output), rows(back_input)) + grads


def xor_permute(x, mask, axis="bfly"):
    return lax.ppermute(x, axis, [(i, i ^ mask) for i in range(lax.axis_size(axis))])


def exchange(x, axes):
    return lax.all_to_all(x, axes, split_axis=0, concat_axis=0, tiled=True)


def deal_weight(w):
    pairs = lax.axis_size("dp") // 2
    sets = w.reshape(pairs, 3, 2, w.shape[1], w.shape[2])
    own = jnp.stack([sets[:, 0], sets[:, 2]], axis=1)
    mid = sets[:, 1][:, :, None]
    return jnp.concatenate([own, mid], axis=2).reshape((pairs * 2, 3) + sets.shape[3:])


def gather_bfly(w, across):
    return [w, xor_permute(w, 1), across, xor_permute(across, 1)]


def after(x, *earlier):
    return lax.optimization_barrier((x,) + earlier)[0]


def add(x, y):
    return (x.astype(jnp.float32) + y.astype(jnp.float32)).astype(jnp.bfloat16)


def deal_tokens(x):
    ndp, nb = lax.axis_size("dp"), lax.axis_size("bfly")
    pairs, count = ndp // 2, x.shape[0]
    view = x.reshape(count, pairs, 3, BLK)
    own = view[:, :, 0::2].reshape(nb, count // nb, ndp, BLK).transpose(2, 0, 1, 3)
    mid = view[:, :, 1].reshape(2, nb, count // nb // 2, pairs, BLK).transpose(3, 0, 1, 2, 4)
    mid = mid.reshape(ndp, nb, count // nb // 2, BLK)
    return jnp.concatenate([own, mid], axis=2).reshape(ndp * nb, -1, BLK)


def undeal_tokens(got, count):
    ndp, nb = lax.axis_size("dp"), lax.axis_size("bfly")
    pairs, own_count = ndp // 2, count // nb
    own = got[:, :own_count].reshape(pairs, 2, count, BLK)
    mid = got[:, own_count:].reshape(pairs, 1, count, BLK)
    sets = jnp.concatenate([own[:, :1], mid, own[:, 1:]], axis=1)
    return sets.transpose(2, 0, 1, 3).reshape(count, pairs * 3 * BLK)


def dot(x, y, contract_x, contract_y):
    dims = (((contract_x,), (contract_y,)), ((), ()))
    return lax.dot_general(x, y, dims, preferred_element_type=jnp.float32)


def square(x):
    return x.reshape(BLK, BLK)


def half_src(part, r):
    return pl.ds(r * (part // 2), part // 2)


def readers(slot, refs, y):
    if slot == 0:
        pairs = (refs[:4], refs[4:8])
        half = refs[0].shape[0] // 2

        def weight(m, which, r):
            return square(pairs[which // 2][m][:, which % 2, r])

        def wide(m, r):
            return square(pairs[1][m][r * half : (r + 1) * half, 1])

        return weight, wide, refs[8:]

    halves, e_ref, half = (refs[:4], refs[4:8]), refs[-1], refs[0].shape[0] // 2
    for m in range(4):
        e_ref[m, :, y] = halves[0][m][:, 3]
        e_ref[m, :, 1 - y] = halves[1][m][:, 3]

    def shared(m, which, r):
        return square(halves[r][m][:, which])

    def wide_shared(m, r):
        return square(e_ref[m, pl.ds((r ^ y) * half, half)])

    return shared, wide_shared, refs[8:-1]


def slot_rows(slot, x_ref):
    own = 2 * x_ref.shape[2] // 3
    return (0, own) if slot == 0 else (own, x_ref.shape[2])


def forward_kernel(slot, seat_ref, x_ref, *refs):
    ndp, nb = x_ref.shape[:2]
    f, y = seat_ref[0], seat_ref[1]
    weight, wide, refs = readers(slot, refs, y)
    lo, hi = slot_rows(slot, x_ref)
    if slot == 1:
        refs[1][:, :, :lo, :] = refs[0][...]
        refs = refs[1:]
    out_ref, perm, active, slope, ret = refs
    count = ndp * (hi - lo)
    tiles = (nb, BLK // nb, count)
    for m in range(nb):
        d = f ^ m
        x = x_ref[:, d, lo:hi, :].reshape(count, BLK)
        for r in range(2):
            spread = dot(weight(m, 0, r), x, 0, 1).astype(jnp.bfloat16)
            perm[r, :, d] = spread.reshape(tiles)
    for m in range(nb):
        s = f ^ m
        for r in range(2):
            p = perm[r, s].reshape(BLK, count)
            value, grade = gelu_pair(dot(weight(m, 1, r), p, 0, 0))
            value = value.astype(jnp.bfloat16)
            active[r, s] = value
            slope[r, s] = grade.astype(jnp.bfloat16)
            narrowed = dot(weight(m, 2, r), value, 0, 0).astype(jnp.bfloat16)
            ret[r, :, s] = narrowed.reshape(tiles)
    for m in range(nb):
        d = f ^ m
        total = 0.0
        for r in range(2):
            total = total + dot(ret[r, d].reshape(BLK, count), wide(m, r), 0, 0)
        out_ref[:, d, lo:hi, :] = total.astype(jnp.bfloat16).reshape(ndp, hi - lo, BLK)


def backward_kernel(slot, seat_ref, x_ref, g_ref, *refs):
    ndp, nb = x_ref.shape[:2]
    rows, half = BLK // ndp, ndp // 2
    f, y = seat_ref[0], seat_ref[1]
    weight, wide, refs = readers(slot, refs, y)
    (perm, active, slope, ret), refs = refs[:4], refs[4:]
    lo, hi = slot_rows(slot, x_ref)
    if slot == 1:
        refs[1][:, :, :lo, :] = refs[0][...]
        refs = refs[1:]
    gin_ref, keep_ref, send_ref, mid, spread = refs

    def store(m, which, r, part):
        ref = (keep_ref, send_ref)[m % 2]
        part = part.astype(jnp.bfloat16).reshape(ndp, rows, BLK)
        if slot == 0:
            ref[m // 2, :, which, r] = part
        else:
            ref[r, m // 2, :, which] = part

    def store_wide(m, r, part):
        ref = (keep_ref, send_ref)[m % 2]
        part = part.astype(jnp.bfloat16).reshape(half, 2, rows, BLK)
        if slot == 0:
            ref[m // 2, r * half : (r + 1) * half, 3] = part
        else:
            ref[y, m // 2, pl.ds((r ^ y) * half, half), 3] = part[:, 0]
            ref[1 - y, m // 2, pl.ds((r ^ y) * half, half), 3] = part[:, 1]

    count = ndp * (hi - lo)
    tiles = (nb, BLK // nb, count)
    for m in range(nb):
        d = f ^ m
        g = g_ref[:, d, lo:hi, :].reshape(count, BLK)
        for r in range(2):
            mid[r, :, d] = dot(wide(m, r), g, 1, 1).astype(jnp.bfloat16).reshape(tiles)
            store_wide(m, r, dot(ret[r, d].reshape(BLK, count), g, 1, 0))
    for m in range(nb):
        s = f ^ m
        for r in range(2):
            p = perm[r, s].reshape(BLK, count)
            back_mid = mid[r, s].reshape(BLK, count)
            back = dot(weight(m, 2, r), back_mid, 1, 0)
            back = (back * slope[r, s].astype(jnp.float32)).astype(jnp.bfloat16)
            store(m, 2, r, dot(active[r, s], back_mid, 1, 1))
            store(m, 1, r, dot(p, back, 1, 1))
            first = dot(weight(m, 1, r), back, 1, 0).astype(jnp.bfloat16)
            spread[r, :, s] = first.reshape(tiles)
    for m in range(nb):
        d = f ^ m
        x = x_ref[:, d, lo:hi, :].reshape(count, BLK)
        total = 0.0
        for r in range(2):
            back = spread[r, d].reshape(BLK, count)
            total = total + dot(back, weight(m, 0, r), 0, 1)
            store(m, 0, r, dot(x, back, 0, 1))
        gin_ref[:, d, lo:hi, :] = total.astype(jnp.bfloat16).reshape(ndp, hi - lo, BLK)


def on_chip(kernel, slot, products, outs, scratch, inputs):
    in_specs = [pl.BlockSpec(memory_space=pltpu.SMEM)]
    in_specs += [pl.BlockSpec(memory_space=pltpu.VMEM)] * (len(inputs) - 1)
    return pl.pallas_call(
        functools.partial(kernel, slot),
        out_shape=[jax.ShapeDtypeStruct(shape, jnp.bfloat16) for shape in outs],
        in_specs=in_specs,
        out_specs=[pl.BlockSpec(memory_space=pltpu.VMEM)] * len(outs),
        scratch_shapes=[pltpu.VMEM(shape, jnp.bfloat16) for shape in scratch],
        cost_estimate=pl.CostEstimate(
            flops=products * 2 * BLK * BLK,
            transcendentals=0,
            bytes_accessed=sum(x.size for x in inputs) * 2 + sum(map(math.prod, outs)) * 2,
        ),
        compiler_params=pltpu.CompilerParams(vmem_limit_bytes=56 * 2**20),
    )(*inputs)


def token_plan(tokens, grad_out, weight_a, weight_b, weight_c, weight_e):
    ndp, nb = lax.axis_size("dp"), lax.axis_size("bfly")
    blocks, rows, _ = weight_a.shape
    parts, count = 2 * blocks, tokens.shape[0]
    dealt_a = weight_a.reshape(blocks, rows, 2, BLK).transpose(0, 2, 1, 3).reshape(parts, rows, BLK)
    dealt_e = weight_e.reshape(parts, rows, BLK)
    seat = jnp.stack([lax.axis_index("bfly"), lax.axis_index("dp") % 2]).astype(jnp.int32)

    everyone = ("dp", "bfly")
    shape = (ndp, nb, -1, BLK)
    dealt = [deal_weight(w) for w in (dealt_a, weight_b, weight_c, dealt_e)]
    w = exchange(jnp.stack(dealt, axis=1), "dp")
    parts_in = (w[:, :, 2], w[:, :2, :2], w[:, 2:, :2])
    mid_across, ab_across, ce_across = (xor_permute(part, 2) for part in parts_in)
    x = exchange(after(deal_tokens(tokens), w), everyone)
    mid_swapped = xor_permute(parts_in[0], 1, "dp")
    g = after(deal_tokens(grad_out), x, mid_across, ab_across, mid_swapped)
    g = exchange(g, everyone).reshape(shape)
    x = x.reshape(shape)
    swapped_across = xor_permute(mid_across, 1, "dp")
    weights = [
        gather_bfly(parts_in[1], ab_across) + gather_bfly(parts_in[2], ce_across),
        gather_bfly(parts_in[0], mid_across) + [mid_swapped, xor_permute(mid_swapped, 1)],
    ]

    counts = (count * ndp // nb, count * ndp // nb // 2)
    rows_shape = ((ndp, nb, count // nb, BLK), x.shape)
    grad_shapes = ((2, ndp, 4, 2, rows, BLK), (2, 2, ndp, 4, rows, BLK))
    joined = ([], [(nb, ndp, 2, rows, BLK)])
    tiled = [(2, nb, nb, BLK // nb, t) for t in counts]
    whole = [(2, nb, BLK, t) for t in counts]
    out, gin, kept, grads = [], [], [], []
    for slot, t in enumerate(counts):
        shapes = [rows_shape[slot], tiled[slot], whole[slot], whole[slot], tiled[slot]]
        inputs = [seat, x] + weights[slot] + out
        first, *rest = on_chip(forward_kernel, slot, 8 * nb * t, shapes, joined[slot], inputs)
        out = [first]
        kept.append(rest)
        if slot == 0:
            last = after(swapped_across, first)
            weights[1] += [last, xor_permute(last, 1)]
    out = exchange(out[0].reshape(ndp * nb, -1, BLK), everyone)
    for slot, t in enumerate(counts):
        shapes = [rows_shape[slot], grad_shapes[slot], grad_shapes[slot]]
        scratch = [tiled[slot], tiled[slot]] + joined[slot]
        inputs = [seat, x, g] + weights[slot] + kept[slot] + gin
        first, *rest = on_chip(backward_kernel, slot, 16 * nb * t, shapes, scratch, inputs)
        gin = [first]
        grads.append(rest)
    gin = gin[0]
    (own_keep, own_send), (mid_keep, mid_send) = grads
    half_mid = mid = add(mid_keep, xor_permute(mid_send, 1))
    half_own = own = add(own_keep, xor_permute(own_send, 1))
    mid = add(mid[0], xor_permute(mid[1], 1, "dp"))
    gin = exchange(after(gin.reshape(ndp * nb, -1, BLK), out, half_mid, half_own), everyone)
    own = add(own[0], xor_permute(own[1], 2))
    mid = add(mid[0], xor_permute(mid[1], 2))
    dealt = jnp.concatenate([own, mid[:, :, None]], axis=2)
    got = exchange(after(dealt, gin), "dp").astype(jnp.float32)
    got = got.reshape(ndp // 2, 2, 4, 3, rows, BLK)

    def own_rows(which):
        mid = jnp.stack([got[:, 0, which, 2], got[:, 1, which, 2]], axis=1)
        return jnp.stack([got[:, 0, which, :2], mid, got[:, 1, which, :2]], axis=1)

    grad_a = own_rows(0).reshape(blocks, 2, rows, BLK).transpose(0, 2, 1, 3)
    return (
        undeal_tokens(out, count),
        undeal_tokens(gin, count),
        grad_a.reshape(weight_a.shape),
        own_rows(1).reshape(weight_b.shape),
        own_rows(2).reshape(weight_c.shape),
        own_rows(3).reshape(weight_e.shape),
    )


def per_device(tokens, grad_out, weight_a, weight_b, weight_c, weight_e):
    ndp, nb = lax.axis_size("dp"), lax.axis_size("bfly")
    fits = nb == 4 and ndp % 2 == 0 and 2 * weight_a.shape[0] == 3 * ndp
    fits = fits and tokens.shape[0] % (32 * nb) == 0 and weight_a.shape[1] * ndp == BLK
    fits = fits and weight_a.shape[2] == 2 * BLK and weight_e.shape[1] == 2 * weight_a.shape[1]
    plan = token_plan if fits else any_mesh
    return plan(tokens, grad_out, weight_a, weight_b, weight_c, weight_e)


def solution(mesh):
    in_specs = (P("dp", "bfly"),) * 2 + (P("bfly", "dp", None),) * 4
    return jax.shard_map(
        per_device, mesh=mesh, in_specs=in_specs, out_specs=in_specs, check_vma=False
    )
```

```python
import math

import jax
import jax.numpy as jnp
from jax import lax
from jax.experimental import pallas as pl
from jax.experimental.pallas import tpu as pltpu
from jax.sharding import PartitionSpec as P

BLK = 256

gelu_scale = 0.7978845608028654


def gelu_pair(hidden):
    inner_arg = gelu_scale * (hidden + 0.044715 * hidden * hidden * hidden)
    tangent = jnp.tanh(inner_arg)
    gelu_value = 0.5 * hidden * (1.0 + tangent)
    gelu_slope = 0.5 * (1.0 + tangent) + 0.5 * hidden * (1.0 - tangent * tangent) * gelu_scale * (
        1.0 + 3.0 * 0.044715 * hidden * hidden
    )
    return (gelu_value, gelu_slope)


def mm(spec, a, b):
    return jnp.einsum(spec, a, b, preferred_element_type=jnp.float32)


def regroup(piece, group_count):
    local_blocks, block_width, token_count = piece.shape
    stacked = piece.reshape(local_blocks, group_count, block_width // group_count, token_count)
    arrived = lax.all_to_all(stacked, "bfly", split_axis=1, concat_axis=1, tiled=True)
    return arrived.reshape(local_blocks, block_width, token_count)


def any_mesh(tokens, grad_out, weight_a, weight_b, weight_c, weight_e):
    group_count = lax.axis_size("bfly")
    full_a, full_b, full_c, full_e = (
        lax.all_gather(w, "dp", axis=1, tiled=True)
        for w in (weight_a, weight_b, weight_c, weight_e)
    )
    token_count = tokens.shape[0]
    inner_blocks = full_a.shape[0]
    spread_width = full_a.shape[2]
    local_blocks = full_b.shape[0]
    inputs = tokens.reshape(token_count, inner_blocks, BLK).transpose(1, 2, 0)
    upstream = grad_out.reshape(token_count, inner_blocks, BLK).transpose(1, 2, 0)
    hidden_view = (local_blocks, BLK, token_count)
    wide_view = (inner_blocks, spread_width, token_count)
    spread = mm("kit,kio->kot", inputs, full_a).astype(jnp.bfloat16).reshape(hidden_view)
    back_out = mm("kjt,koj->kot", upstream, full_e).astype(jnp.bfloat16).reshape(hidden_view)
    permuted = regroup(spread, group_count)
    back_mid = regroup(back_out, group_count)
    gelu_value, gelu_slope = gelu_pair(mm("qit,qij->qjt", permuted, full_b))
    active = gelu_value.astype(jnp.bfloat16)
    narrowed = mm("qit,qij->qjt", active, full_c).astype(jnp.bfloat16)
    back_hidden = (mm("qjt,qij->qit", back_mid, full_c) * gelu_slope).astype(jnp.bfloat16)
    back_first = mm("qjt,qij->qit", back_hidden, full_b).astype(jnp.bfloat16)
    returned = regroup(narrowed, group_count).reshape(wide_view)
    back_spread = regroup(back_first, group_count).reshape(wide_view)
    output = mm("kot,koj->kjt", returned, full_e)
    back_input = mm("kot,kio->kit", back_spread, full_a)
    parts = (
        mm("kit,kot->kio", inputs, back_spread),
        mm("qit,qjt->qij", permuted, back_hidden),
        mm("qit,qjt->qij", active, back_mid),
        mm("kot,kjt->koj", returned, upstream),
    )
    grads = tuple(
        lax.psum_scatter(part.astype(jnp.bfloat16), "dp", scatter_dimension=1, tiled=True).astype(
            jnp.float32
        )
        for part in parts
    )

    def rows(x):
        return x.astype(jnp.bfloat16).transpose(2, 0, 1).reshape(token_count, inner_blocks * BLK)

    return (rows(output), rows(back_input)) + grads


def xor_permute(x, mask, axis="bfly"):
    return lax.ppermute(x, axis, [(i, i ^ mask) for i in range(lax.axis_size(axis))])


def exchange(x, axes):
    return lax.all_to_all(x, axes, split_axis=0, concat_axis=0, tiled=True)


def deal_weight(w):
    pairs = lax.axis_size("dp") // 2
    sets = w.reshape(pairs, 3, 2, w.shape[1], w.shape[2])
    own = jnp.stack([sets[:, 0], sets[:, 2]], axis=1)
    mid = sets[:, 1][:, :, None]
    return jnp.concatenate([own, mid], axis=2).reshape((pairs * 2, 3) + sets.shape[3:])


def gather_bfly(w, across):
    return [w, xor_permute(w, 1), across, xor_permute(across, 1)]


def after(x, *earlier):
    return lax.optimization_barrier((x,) + earlier)[0]


def add(x, y):
    return (x.astype(jnp.float32) + y.astype(jnp.float32)).astype(jnp.bfloat16)


def deal_tokens(x):
    ndp, nb = lax.axis_size("dp"), lax.axis_size("bfly")
    pairs, count = ndp // 2, x.shape[0]
    view = x.reshape(count, pairs, 3, BLK)
    own = view[:, :, 0::2].reshape(nb, count // nb, ndp, BLK).transpose(2, 0, 1, 3)
    mid = view[:, :, 1].reshape(2, nb, count // nb // 2, pairs, BLK).transpose(3, 0, 1, 2, 4)
    mid = mid.reshape(ndp, nb, count // nb // 2, BLK)
    return jnp.concatenate([own, mid], axis=2).reshape(ndp * nb, -1, BLK)


def undeal_tokens(got, count):
    ndp, nb = lax.axis_size("dp"), lax.axis_size("bfly")
    pairs, own_count = ndp // 2, count // nb
    own = got[:, :own_count].reshape(pairs, 2, count, BLK)
    mid = got[:, own_count:].reshape(pairs, 1, count, BLK)
    sets = jnp.concatenate([own[:, :1], mid, own[:, 1:]], axis=1)
    return sets.transpose(2, 0, 1, 3).reshape(count, pairs * 3 * BLK)


def dot(x, y, contract_x, contract_y):
    dims = (((contract_x,), (contract_y,)), ((), ()))
    return lax.dot_general(x, y, dims, preferred_element_type=jnp.float32)


def square(x):
    return x.reshape(BLK, BLK)


def half_src(part, r):
    return pl.ds(r * (part // 2), part // 2)


def weight_of(slot, w, v):
    def get(m, which, r):
        if slot == 0:
            return square(w[which // 2][m][:, r, which % 2])
        ref = w[which // 2][m] if r == 0 else v[which // 2][m]
        return square(ref[:, 2 if r == 0 else 0, which % 2])

    return get


def wide_weight(slot, w, e_ref, y):
    def get(m, r):
        if slot == 0:
            return square(w[1][m][half_src(e_ref.shape[1], r), :2, 1])
        return square(e_ref[m, half_src(e_ref.shape[1], r ^ y)])

    return get


def join_halves(w, v, e_ref, y):
    for m in range(4):
        e_ref[m, :, y] = w[1][m][:, 2, 1]
        e_ref[m, :, 1 - y] = v[1][m][:, 0, 1]


def weight_refs(refs):
    return (refs[:4], refs[4:8]), (refs[8:12], refs[12:16]), refs[16:]


def forward_kernel(seat_ref, x_ref, *refs):
    w, v, (out_ref, *refs) = weight_refs(refs)
    saved, e_ref = (refs[:4], refs[4:8]), refs[8]
    ndp, nb, all_rows, _ = x_ref.shape
    own_rows = 2 * all_rows // 3
    f, y = seat_ref[0], seat_ref[1]
    join_halves(w, v, e_ref, y)
    for slot, (lo, hi) in enumerate(((0, own_rows), (own_rows, all_rows))):
        perm, active, slope, ret = saved[slot]
        weight, wide = weight_of(slot, w, v), wide_weight(slot, w, e_ref, y)
        count = ndp * (hi - lo)
        tiles = (nb, BLK // nb, count)
        for m in range(nb):
            d = f ^ m
            x = x_ref[:, d, lo:hi, :].reshape(count, BLK)
            for r in range(2):
                spread = dot(weight(m, 0, r), x, 0, 1).astype(jnp.bfloat16)
                perm[r, :, d] = spread.reshape(tiles)
        for m in range(nb):
            s = f ^ m
            for r in range(2):
                p = perm[r, s].reshape(BLK, count)
                value, grade = gelu_pair(dot(weight(m, 1, r), p, 0, 0))
                value = value.astype(jnp.bfloat16)
                active[r, s] = value
                slope[r, s] = grade.astype(jnp.bfloat16)
                narrowed = dot(weight(m, 2, r), value, 0, 0).astype(jnp.bfloat16)
                ret[r, :, s] = narrowed.reshape(tiles)
        for m in range(nb):
            d = f ^ m
            total = 0.0
            for r in range(2):
                total = total + dot(ret[r, d].reshape(BLK, count), wide(m, r), 0, 0)
            out_ref[:, d, lo:hi, :] = total.astype(jnp.bfloat16).reshape(ndp, hi - lo, BLK)


def backward_kernel(seat_ref, x_ref, g_ref, *refs):
    w, v, refs = weight_refs(refs)
    saved = refs[:4], refs[4:8]
    gin_ref, own_keep, own_send, mid_keep, mid_send = refs[8:13]
    scratch, e_ref = (refs[13:15], refs[15:17]), refs[17]
    ndp, nb, all_rows, _ = x_ref.shape
    own_rows = 2 * all_rows // 3
    rows = BLK // ndp
    f, y = seat_ref[0], seat_ref[1]
    join_halves(w, v, e_ref, y)

    def store(slot, m, which, r, part):
        ref = ((own_keep, own_send), (mid_keep, mid_send))[slot][m % 2]
        if slot == 0:
            ref[m // 2, :, r, which] = part.astype(jnp.bfloat16).reshape(ndp, rows, BLK)
        else:
            ref[r, m // 2, :, which] = part.astype(jnp.bfloat16).reshape(ndp, rows, BLK)

    def store_wide(slot, m, r, part):
        ref = ((own_keep, own_send), (mid_keep, mid_send))[slot][m % 2]
        part = part.astype(jnp.bfloat16).reshape(ndp // 2, 2, rows, BLK)
        if slot == 0:
            ref[m // 2, half_src(ndp, r), :, 3] = part
        else:
            ref[y, m // 2, half_src(ndp, r ^ y), 3] = part[:, 0]
            ref[1 - y, m // 2, half_src(ndp, r ^ y), 3] = part[:, 1]

    for slot, (lo, hi) in enumerate(((0, own_rows), (own_rows, all_rows))):
        perm, active, slope, ret = saved[slot]
        mid, spread = scratch[slot]
        weight, wide = weight_of(slot, w, v), wide_weight(slot, w, e_ref, y)
        count = ndp * (hi - lo)
        tiles = (nb, BLK // nb, count)
        for m in range(nb):
            d = f ^ m
            g = g_ref[:, d, lo:hi, :].reshape(count, BLK)
            for r in range(2):
                mid[r, :, d] = dot(wide(m, r), g, 1, 1).astype(jnp.bfloat16).reshape(tiles)
                store_wide(slot, m, r, dot(ret[r, d].reshape(BLK, count), g, 1, 0))
        for m in range(nb):
            s = f ^ m
            for r in range(2):
                p = perm[r, s].reshape(BLK, count)
                back_mid = mid[r, s].reshape(BLK, count)
                back = dot(weight(m, 2, r), back_mid, 1, 0)
                back = (back * slope[r, s].astype(jnp.float32)).astype(jnp.bfloat16)
                store(slot, m, 2, r, dot(active[r, s], back_mid, 1, 1))
                store(slot, m, 1, r, dot(p, back, 1, 1))
                first = dot(weight(m, 1, r), back, 1, 0).astype(jnp.bfloat16)
                spread[r, :, s] = first.reshape(tiles)
        for m in range(nb):
            d = f ^ m
            x = x_ref[:, d, lo:hi, :].reshape(count, BLK)
            total = 0.0
            for r in range(2):
                back = spread[r, d].reshape(BLK, count)
                total = total + dot(back, weight(m, 0, r), 0, 1)
                store(slot, m, 0, r, dot(x, back, 0, 1))
            gin_ref[:, d, lo:hi, :] = total.astype(jnp.bfloat16).reshape(ndp, hi - lo, BLK)


def on_chip(kernel, products, outs, scratch, inputs):
    cells = sum(x.size for x in inputs) + sum(map(math.prod, outs + scratch))
    in_specs = [pl.BlockSpec(memory_space=pltpu.SMEM)]
    in_specs += [pl.BlockSpec(memory_space=pltpu.VMEM)] * (len(inputs) - 1)
    return pl.pallas_call(
        kernel,
        out_shape=[jax.ShapeDtypeStruct(shape, jnp.bfloat16) for shape in outs],
        in_specs=in_specs,
        out_specs=[pl.BlockSpec(memory_space=pltpu.VMEM)] * len(outs),
        scratch_shapes=[pltpu.VMEM(shape, jnp.bfloat16) for shape in scratch],
        cost_estimate=pl.CostEstimate(
            flops=products * 2 * BLK * BLK,
            transcendentals=0,
            bytes_accessed=sum(x.size for x in inputs) * 2 + sum(map(math.prod, outs)) * 2,
        ),
        compiler_params=pltpu.CompilerParams(vmem_limit_bytes=2 * cells + 6 * 2**20),
    )(*inputs)


def token_plan(tokens, grad_out, weight_a, weight_b, weight_c, weight_e):
    ndp, nb = lax.axis_size("dp"), lax.axis_size("bfly")
    blocks, rows, _ = weight_a.shape
    parts, count = 2 * blocks, tokens.shape[0]
    dealt_a = weight_a.reshape(blocks, rows, 2, BLK).transpose(0, 2, 1, 3).reshape(parts, rows, BLK)
    dealt_e = weight_e.reshape(parts, rows, BLK)
    seat = jnp.stack([lax.axis_index("bfly"), lax.axis_index("dp") % 2]).astype(jnp.int32)

    everyone = ("dp", "bfly")
    shape = (ndp, nb, -1, BLK)
    def deal(first, second):
        return jnp.stack([deal_weight(first), deal_weight(second)], axis=2)

    def halves(w):
        swapped = xor_permute(w[:, 2:], 1, "dp")
        return w, xor_permute(w, 2), swapped, xor_permute(swapped, 2)

    ab = halves(exchange(deal(dealt_a, weight_b), "dp"))
    ce = halves(exchange(after(deal(weight_c, dealt_e), ab[0]), "dp"))
    x = exchange(after(deal_tokens(tokens), ce[0], ab[1], ab[3]), everyone)
    g = exchange(after(deal_tokens(grad_out), x, ce[1], ce[3]), everyone).reshape(shape)
    x = x.reshape(shape)
    weights = gather_bfly(*ab[:2]) + gather_bfly(*ce[:2])
    weights += gather_bfly(*ab[2:]) + gather_bfly(*ce[2:])

    own, mid = count * ndp // nb, count * ndp // nb // 2
    saved = []
    for t in (own, mid):
        tiled, whole = (2, nb, nb, BLK // nb, t), (2, nb, BLK, t)
        saved += [tiled, whole, whole, tiled]
    halves = (nb, ndp, 2, rows, BLK)
    products = 2 * nb * (own + mid)
    out, *kept = on_chip(
        forward_kernel, 4 * products, [x.shape] + saved, [halves], [seat, x] + weights
    )
    out = exchange(out.reshape(ndp * nb, -1, BLK), everyone)
    own_shape, mid_shape = (2, ndp, 2, 4, rows, BLK), (2, 2, ndp, 4, rows, BLK)
    gin, own_keep, own_send, mid_keep, mid_send = on_chip(
        backward_kernel,
        8 * products,
        [x.shape, own_shape, own_shape, mid_shape, mid_shape],
        [saved[0], saved[0], saved[4], saved[4], halves],
        [seat, x, g] + weights + kept,
    )
    half_mid = mid = add(mid_keep, xor_permute(mid_send, 1))
    half_own = own = add(own_keep, xor_permute(own_send, 1))
    mid = add(mid[0], xor_permute(mid[1], 1, "dp"))
    gin = exchange(after(gin.reshape(ndp * nb, -1, BLK), out, half_mid, half_own), everyone)
    own = add(own[0], xor_permute(own[1], 2))
    mid = add(mid[0], xor_permute(mid[1], 2))
    dealt = jnp.concatenate([own, mid[:, None]], axis=1)
    got = exchange(after(dealt, gin), "dp").astype(jnp.float32)
    got = got.reshape(ndp // 2, 2, 3, 4, rows, BLK)

    def own_rows(which):
        mid = jnp.stack([got[:, 0, 2, which], got[:, 1, 2, which]], axis=1)
        return jnp.stack([got[:, 0, :2, which], mid, got[:, 1, :2, which]], axis=1)

    grad_a = own_rows(0).reshape(blocks, 2, rows, BLK).transpose(0, 2, 1, 3)
    return (
        undeal_tokens(out, count),
        undeal_tokens(gin, count),
        grad_a.reshape(weight_a.shape),
        own_rows(1).reshape(weight_b.shape),
        own_rows(2).reshape(weight_c.shape),
        own_rows(3).reshape(weight_e.shape),
    )


def per_device(tokens, grad_out, weight_a, weight_b, weight_c, weight_e):
    ndp, nb = lax.axis_size("dp"), lax.axis_size("bfly")
    fits = nb == 4 and ndp % 2 == 0 and 2 * weight_a.shape[0] == 3 * ndp
    fits = fits and tokens.shape[0] % (32 * nb) == 0 and weight_a.shape[1] * ndp == BLK
    fits = fits and weight_a.shape[2] == 2 * BLK and weight_e.shape[1] == 2 * weight_a.shape[1]
    plan = token_plan if fits else any_mesh
    return plan(tokens, grad_out, weight_a, weight_b, weight_c, weight_e)


def solution(mesh):
    in_specs = (P("dp", "bfly"),) * 2 + (P("bfly", "dp", None),) * 4
    return jax.shard_map(
        per_device, mesh=mesh, in_specs=in_specs, out_specs=in_specs, check_vma=False
    )
```

```python
import math

import jax
import jax.numpy as jnp
from jax import lax
from jax.experimental import pallas as pl
from jax.experimental.pallas import tpu as pltpu
from jax.sharding import PartitionSpec as P

BLK = 256

gelu_scale = 0.7978845608028654


def gelu_pair(hidden):
    inner_arg = gelu_scale * (hidden + 0.044715 * hidden * hidden * hidden)
    tangent = jnp.tanh(inner_arg)
    gelu_value = 0.5 * hidden * (1.0 + tangent)
    gelu_slope = 0.5 * (1.0 + tangent) + 0.5 * hidden * (1.0 - tangent * tangent) * gelu_scale * (
        1.0 + 3.0 * 0.044715 * hidden * hidden
    )
    return (gelu_value, gelu_slope)


def mm(spec, a, b):
    return jnp.einsum(spec, a, b, preferred_element_type=jnp.float32)


def regroup(piece, group_count):
    local_blocks, block_width, token_count = piece.shape
    stacked = piece.reshape(local_blocks, group_count, block_width // group_count, token_count)
    arrived = lax.all_to_all(stacked, "bfly", split_axis=1, concat_axis=1, tiled=True)
    return arrived.reshape(local_blocks, block_width, token_count)


def any_mesh(tokens, grad_out, weight_a, weight_b, weight_c, weight_e):
    group_count = lax.axis_size("bfly")
    full_a, full_b, full_c, full_e = (
        lax.all_gather(w, "dp", axis=1, tiled=True)
        for w in (weight_a, weight_b, weight_c, weight_e)
    )
    token_count = tokens.shape[0]
    inner_blocks = full_a.shape[0]
    spread_width = full_a.shape[2]
    local_blocks = full_b.shape[0]
    inputs = tokens.reshape(token_count, inner_blocks, BLK).transpose(1, 2, 0)
    upstream = grad_out.reshape(token_count, inner_blocks, BLK).transpose(1, 2, 0)
    hidden_view = (local_blocks, BLK, token_count)
    wide_view = (inner_blocks, spread_width, token_count)
    spread = mm("kit,kio->kot", inputs, full_a).astype(jnp.bfloat16).reshape(hidden_view)
    back_out = mm("kjt,koj->kot", upstream, full_e).astype(jnp.bfloat16).reshape(hidden_view)
    permuted = regroup(spread, group_count)
    back_mid = regroup(back_out, group_count)
    gelu_value, gelu_slope = gelu_pair(mm("qit,qij->qjt", permuted, full_b))
    active = gelu_value.astype(jnp.bfloat16)
    narrowed = mm("qit,qij->qjt", active, full_c).astype(jnp.bfloat16)
    back_hidden = (mm("qjt,qij->qit", back_mid, full_c) * gelu_slope).astype(jnp.bfloat16)
    back_first = mm("qjt,qij->qit", back_hidden, full_b).astype(jnp.bfloat16)
    returned = regroup(narrowed, group_count).reshape(wide_view)
    back_spread = regroup(back_first, group_count).reshape(wide_view)
    output = mm("kot,koj->kjt", returned, full_e)
    back_input = mm("kot,kio->kit", back_spread, full_a)
    parts = (
        mm("kit,kot->kio", inputs, back_spread),
        mm("qit,qjt->qij", permuted, back_hidden),
        mm("qit,qjt->qij", active, back_mid),
        mm("kot,kjt->koj", returned, upstream),
    )
    grads = tuple(
        lax.psum_scatter(part.astype(jnp.bfloat16), "dp", scatter_dimension=1, tiled=True).astype(
            jnp.float32
        )
        for part in parts
    )

    def rows(x):
        return x.astype(jnp.bfloat16).transpose(2, 0, 1).reshape(token_count, inner_blocks * BLK)

    return (rows(output), rows(back_input)) + grads


def xor_permute(x, mask, axis="bfly"):
    return lax.ppermute(x, axis, [(i, i ^ mask) for i in range(lax.axis_size(axis))])


def exchange(x, axes):
    return lax.all_to_all(x, axes, split_axis=0, concat_axis=0, tiled=True)


def deal_weight(w):
    pairs = lax.axis_size("dp") // 2
    sets = w.reshape(pairs, 3, 2, w.shape[1], w.shape[2])
    own = jnp.stack([sets[:, 0], sets[:, 2]], axis=1)
    mid = sets[:, 1][:, :, None]
    return jnp.concatenate([own, mid], axis=2).reshape((pairs * 2, 3) + sets.shape[3:])


def gather_bfly(w, across):
    return [w, xor_permute(w, 1), across, xor_permute(across, 1)]


def after(x, *earlier):
    return lax.optimization_barrier((x,) + earlier)[0]


def add(x, y):
    return (x.astype(jnp.float32) + y.astype(jnp.float32)).astype(jnp.bfloat16)


def deal_tokens(x):
    ndp, nb = lax.axis_size("dp"), lax.axis_size("bfly")
    pairs, count = ndp // 2, x.shape[0]
    view = x.reshape(count, pairs, 3, BLK)
    own = view[:, :, 0::2].reshape(nb, count // nb, ndp, BLK).transpose(2, 0, 1, 3)
    mid = view[:, :, 1].reshape(2, nb, count // nb // 2, pairs, BLK).transpose(3, 0, 1, 2, 4)
    mid = mid.reshape(ndp, nb, count // nb // 2, BLK)
    return jnp.concatenate([own, mid], axis=2).reshape(ndp * nb, -1, BLK)


def undeal_tokens(got, count):
    ndp, nb = lax.axis_size("dp"), lax.axis_size("bfly")
    pairs, own_count = ndp // 2, count // nb
    own = got[:, :own_count].reshape(pairs, 2, count, BLK)
    mid = got[:, own_count:].reshape(pairs, 1, count, BLK)
    sets = jnp.concatenate([own[:, :1], mid, own[:, 1:]], axis=1)
    return sets.transpose(2, 0, 1, 3).reshape(count, pairs * 3 * BLK)


def dot(x, y, contract_x, contract_y):
    dims = (((contract_x,), (contract_y,)), ((), ()))
    return lax.dot_general(x, y, dims, preferred_element_type=jnp.float32)


def square(x):
    return x.reshape(BLK, BLK)


def half_src(part, r):
    return pl.ds(r * (part // 2), part // 2)


def weight_of(slot, w, v):
    def get(m, which, r):
        if slot == 0:
            return square(w[which // 2][m][:, r, which % 2])
        ref = w[which // 2][m] if r == 0 else v[which // 2][m]
        return square(ref[:, 2 if r == 0 else 0, which % 2])

    return get


def wide_weight(slot, w, e_ref, y):
    def get(m, r):
        if slot == 0:
            return square(w[1][m][half_src(e_ref.shape[1], r), :2, 1])
        return square(e_ref[m, half_src(e_ref.shape[1], r ^ y)])

    return get


def join_halves(w, v, e_ref, y):
    for m in range(4):
        e_ref[m, :, y] = w[1][m][:, 2, 1]
        e_ref[m, :, 1 - y] = v[1][m][:, 0, 1]


def weight_refs(refs):
    return (refs[:4], refs[4:8]), (refs[8:12], refs[12:16]), refs[16:]


def forward_kernel(seat_ref, x_ref, *refs):
    w, v, (out_ref, *refs) = weight_refs(refs)
    saved, e_ref = (refs[:4], refs[4:8]), refs[8]
    ndp, nb, all_rows, _ = x_ref.shape
    own_rows = 2 * all_rows // 3
    f, y = seat_ref[0], seat_ref[1]
    join_halves(w, v, e_ref, y)
    for slot, (lo, hi) in enumerate(((0, own_rows), (own_rows, all_rows))):
        perm, active, slope, ret = saved[slot]
        weight, wide = weight_of(slot, w, v), wide_weight(slot, w, e_ref, y)
        count = ndp * (hi - lo)
        tiles = (nb, BLK // nb, count)
        for m in range(nb):
            d = f ^ m
            x = x_ref[:, d, lo:hi, :].reshape(count, BLK)
            for r in range(2):
                spread = dot(weight(m, 0, r), x, 0, 1).astype(jnp.bfloat16)
                perm[r, :, d] = spread.reshape(tiles)
        for m in range(nb):
            s = f ^ m
            for r in range(2):
                p = perm[r, s].reshape(BLK, count)
                value, grade = gelu_pair(dot(weight(m, 1, r), p, 0, 0))
                value = value.astype(jnp.bfloat16)
                active[r, s] = value
                slope[r, s] = grade.astype(jnp.bfloat16)
                narrowed = dot(weight(m, 2, r), value, 0, 0).astype(jnp.bfloat16)
                ret[r, :, s] = narrowed.reshape(tiles)
        for m in range(nb):
            d = f ^ m
            total = 0.0
            for r in range(2):
                total = total + dot(ret[r, d].reshape(BLK, count), wide(m, r), 0, 0)
            out_ref[:, d, lo:hi, :] = total.astype(jnp.bfloat16).reshape(ndp, hi - lo, BLK)


class Streamed:
    def __init__(self, sources, targets, sems, order):
        self.targets, self.waiting = targets, {}
        for i in order:
            self.waiting[i] = pltpu.make_async_copy(sources[i], targets[i], sems.at[i])
            self.waiting[i].start()

    def get(self, i):
        if i in self.waiting:
            self.waiting.pop(i).wait()
        return self.targets[i]


class Lookup:
    def __init__(self, streamed, indices):
        self.streamed, self.indices = streamed, indices

    def __getitem__(self, at):
        return self.streamed.get(self.indices[at])


BACKWARD_ORDER = (
    (1, 6, 21, 7, 8, 9, 2, 18, 19, 20, 3, 4, 5, 0) + tuple(range(14, 18)) + (25,) + tuple(range(10, 14)) + (22, 23, 24)
)


def backward_kernel(seat_ref, *refs):
    count_in = len(BACKWARD_ORDER)
    sources, refs = refs[:count_in], refs[count_in:]
    results, refs = refs[:9], refs[9:]
    targets, refs = refs[:count_in], refs[count_in:]
    staged, refs = refs[:5], refs[5:]
    scratch, (e_ref, in_sems, out_sems) = (refs[:2], refs[2:4]), refs[4:]
    streamed = Streamed(sources, targets, in_sems, BACKWARD_ORDER)
    at = [Lookup(streamed, range(i, i + 4)) for i in range(2, 26, 4)]
    w, v, saved = at[:2], at[2:4], at[4:]
    gin_ref, own_keep, own_send, mid_keep, mid_send = staged
    sent = []

    def send(source, target):
        sent.append(pltpu.make_async_copy(source, target, out_sems.at[len(sent)]))
        sent[-1].start()

    ndp, nb, all_rows, _ = targets[0].shape
    own_rows = 2 * all_rows // 3
    rows = BLK // ndp
    f, y = seat_ref[0], seat_ref[1]

    def store(slot, m, which, r, part):
        ref = ((own_keep, own_send), (mid_keep, mid_send))[slot][m % 2]
        if slot == 0:
            ref[m // 2, :, r, which] = part.astype(jnp.bfloat16).reshape(ndp, rows, BLK)
        else:
            ref[r, m // 2, :, which] = part.astype(jnp.bfloat16).reshape(ndp, rows, BLK)

    def store_wide(slot, m, r, part):
        ref = ((own_keep, own_send), (mid_keep, mid_send))[slot][m % 2]
        part = part.astype(jnp.bfloat16).reshape(ndp // 2, 2, rows, BLK)
        if slot == 0:
            ref[m // 2, half_src(ndp, r), :, 3] = part
        else:
            ref[y, m // 2, half_src(ndp, r ^ y), 3] = part[:, 0]
            ref[1 - y, m // 2, half_src(ndp, r ^ y), 3] = part[:, 1]

    for slot, (lo, hi) in enumerate(((0, own_rows), (own_rows, all_rows))):
        perm, active, slope, ret = range(4)
        mid, spread = scratch[slot]
        if slot == 1:
            join_halves(w, v, e_ref, y)
        weight, wide = weight_of(slot, w, v), wide_weight(slot, w, e_ref, y)
        count = ndp * (hi - lo)
        tiles = (nb, BLK // nb, count)
        for m in range(nb):
            d = f ^ m
            g = streamed.get(1)[:, d, lo:hi, :].reshape(count, BLK)
            for r in range(2):
                mid[r, :, d] = dot(wide(m, r), g, 1, 1).astype(jnp.bfloat16).reshape(tiles)
                store_wide(slot, m, r, dot(saved[slot][ret][r, d].reshape(BLK, count), g, 1, 0))
        for m in range(nb):
            s = f ^ m
            for r in range(2):
                p = saved[slot][perm][r, s].reshape(BLK, count)
                back_mid = mid[r, s].reshape(BLK, count)
                back = dot(weight(m, 2, r), back_mid, 1, 0)
                back = (back * saved[slot][slope][r, s].astype(jnp.float32)).astype(jnp.bfloat16)
                store(slot, m, 2, r, dot(saved[slot][active][r, s], back_mid, 1, 1))
                store(slot, m, 1, r, dot(p, back, 1, 1))
                first = dot(weight(m, 1, r), back, 1, 0).astype(jnp.bfloat16)
                spread[r, :, s] = first.reshape(tiles)
        for m in range(nb):
            d = f ^ m
            x = streamed.get(0)[:, d, lo:hi, :].reshape(count, BLK)
            total = 0.0
            for r in range(2):
                back = spread[r, d].reshape(BLK, count)
                total = total + dot(back, weight(m, 0, r), 0, 1)
                store(slot, m, 0, r, dot(x, back, 0, 1))
            gin_ref[:, d, lo:hi, :] = total.astype(jnp.bfloat16).reshape(ndp, hi - lo, BLK)
        if slot == 0:
            send(own_keep, results[1])
            send(own_send.at[0], results[2])
            send(own_send.at[1], results[3])
    send(mid_keep, results[4])
    for i in range(4):
        send(mid_send.at[i // 2, i % 2], results[5 + i])
    send(gin_ref, results[0])
    for copy in sent:
        copy.wait()


def on_chip(kernel, products, outs, scratch, inputs, results=None):
    streamed = results is not None
    space = pl.ANY if streamed else pltpu.VMEM
    staged = [x.shape for x in inputs[1:]] + outs if streamed else []
    outs = results or outs
    sems = [pltpu.SemaphoreType.DMA((n,)) for n in (len(inputs) - 1, len(outs))]
    return pl.pallas_call(
        kernel,
        out_shape=[jax.ShapeDtypeStruct(shape, jnp.bfloat16) for shape in outs],
        in_specs=[pl.BlockSpec(memory_space=pltpu.SMEM)]
        + [pl.BlockSpec(memory_space=space)] * (len(inputs) - 1),
        out_specs=[pl.BlockSpec(memory_space=space)] * len(outs),
        scratch_shapes=[pltpu.VMEM(shape, jnp.bfloat16) for shape in staged + scratch]
        + (sems if streamed else []),
        cost_estimate=pl.CostEstimate(
            flops=products * 2 * BLK * BLK,
            transcendentals=0,
            bytes_accessed=sum(x.size for x in inputs) * 2 + sum(map(math.prod, outs)) * 2,
        ),
        compiler_params=pltpu.CompilerParams(vmem_limit_bytes=56 * 2**20),
    )(*inputs)


def token_plan(tokens, grad_out, weight_a, weight_b, weight_c, weight_e):
    ndp, nb = lax.axis_size("dp"), lax.axis_size("bfly")
    blocks, rows, _ = weight_a.shape
    parts, count = 2 * blocks, tokens.shape[0]
    dealt_a = weight_a.reshape(blocks, rows, 2, BLK).transpose(0, 2, 1, 3).reshape(parts, rows, BLK)
    dealt_e = weight_e.reshape(parts, rows, BLK)
    seat = jnp.stack([lax.axis_index("bfly"), lax.axis_index("dp") % 2]).astype(jnp.int32)

    everyone = ("dp", "bfly")
    shape = (ndp, nb, -1, BLK)
    def deal(first, second):
        return jnp.stack([deal_weight(first), deal_weight(second)], axis=2)

    def halves(w):
        swapped = xor_permute(w[:, 2:], 1, "dp")
        return w, xor_permute(w, 2), swapped, xor_permute(swapped, 2)

    ab = halves(exchange(deal(dealt_a, weight_b), "dp"))
    ce = halves(exchange(after(deal(weight_c, dealt_e), ab[0]), "dp"))
    x = exchange(after(deal_tokens(tokens), ce[0], ab[1], ab[3]), everyone)
    g = exchange(after(deal_tokens(grad_out), x, ce[1], ce[3]), everyone).reshape(shape)
    x = x.reshape(shape)
    weights = gather_bfly(*ab[:2]) + gather_bfly(*ce[:2])
    weights += gather_bfly(*ab[2:]) + gather_bfly(*ce[2:])

    own, mid = count * ndp // nb, count * ndp // nb // 2
    saved = []
    for t in (own, mid):
        tiled, whole = (2, nb, nb, BLK // nb, t), (2, nb, BLK, t)
        saved += [tiled, whole, whole, tiled]
    halves = (nb, ndp, 2, rows, BLK)
    products = 2 * nb * (own + mid)
    out, *kept = on_chip(
        forward_kernel, 4 * products, [x.shape] + saved, [halves], [seat, x] + weights
    )
    out = exchange(out.reshape(ndp * nb, -1, BLK), everyone)
    own_shape, mid_shape = (2, ndp, 2, 4, rows, BLK), (2, 2, ndp, 4, rows, BLK)
    gin, own_keep, *sends = on_chip(
        backward_kernel,
        8 * products,
        [x.shape, own_shape, own_shape, mid_shape, mid_shape],
        [saved[0], saved[0], saved[4], saved[4], halves],
        [seat, x, g] + weights + kept,
        [x.shape, own_shape] + [own_shape[1:]] * 2 + [mid_shape] + [mid_shape[2:]] * 4,
    )
    mid_keep = sends.pop(2)
    far = add(mid_keep[1, 1], xor_permute(sends[5], 1))
    own_far = add(own_keep[1], xor_permute(sends[1], 1))
    far = add(add(mid_keep[0, 1], xor_permute(sends[3], 1)), xor_permute(far, 1, "dp"))
    own_near = add(own_keep[0], xor_permute(sends[0], 1))
    near = add(mid_keep[1, 0], xor_permute(sends[4], 1))
    part = ndp // 2
    own_first = add(own_near[:part], xor_permute(own_far[:part], 2))
    gin = exchange(after(gin.reshape(ndp * nb, -1, BLK), out, far, own_first), everyone)
    own_last = add(own_near[part:], xor_permute(after(own_far[part:], own_first), 2))
    own = jnp.concatenate([own_first, own_last], axis=0)
    near = xor_permute(near, 1, "dp")
    near = add(add(mid_keep[0, 0], xor_permute(sends[2], 1)), near)
    mid = add(near, xor_permute(far, 2))
    dealt = jnp.concatenate([own, mid[:, None]], axis=1)
    got = exchange(after(dealt, gin), "dp").astype(jnp.float32)
    got = got.reshape(ndp // 2, 2, 3, 4, rows, BLK)

    def own_rows(which):
        mid = jnp.stack([got[:, 0, 2, which], got[:, 1, 2, which]], axis=1)
        return jnp.stack([got[:, 0, :2, which], mid, got[:, 1, :2, which]], axis=1)

    grad_a = own_rows(0).reshape(blocks, 2, rows, BLK).transpose(0, 2, 1, 3)
    return (
        undeal_tokens(out, count),
        undeal_tokens(gin, count),
        grad_a.reshape(weight_a.shape),
        own_rows(1).reshape(weight_b.shape),
        own_rows(2).reshape(weight_c.shape),
        own_rows(3).reshape(weight_e.shape),
    )


def per_device(tokens, grad_out, weight_a, weight_b, weight_c, weight_e):
    ndp, nb = lax.axis_size("dp"), lax.axis_size("bfly")
    fits = nb == 4 and ndp % 2 == 0 and 2 * weight_a.shape[0] == 3 * ndp
    fits = fits and tokens.shape[0] % (32 * nb) == 0 and weight_a.shape[1] * ndp == BLK
    fits = fits and weight_a.shape[2] == 2 * BLK and weight_e.shape[1] == 2 * weight_a.shape[1]
    plan = token_plan if fits else any_mesh
    return plan(tokens, grad_out, weight_a, weight_b, weight_c, weight_e)


def solution(mesh):
    in_specs = (P("dp", "bfly"),) * 2 + (P("bfly", "dp", None),) * 4
    return jax.shard_map(
        per_device, mesh=mesh, in_specs=in_specs, out_specs=in_specs, check_vma=False
    )
```

```python
import functools
import math

import jax
import jax.numpy as jnp
from jax import lax
from jax.experimental import pallas as pl
from jax.experimental.pallas import tpu as pltpu
from jax.sharding import PartitionSpec as P

BLK = 256

gelu_scale = 0.7978845608028654


def gelu_pair(hidden):
    inner_arg = gelu_scale * (hidden + 0.044715 * hidden * hidden * hidden)
    tangent = jnp.tanh(inner_arg)
    gelu_value = 0.5 * hidden * (1.0 + tangent)
    gelu_slope = 0.5 * (1.0 + tangent) + 0.5 * hidden * (1.0 - tangent * tangent) * gelu_scale * (
        1.0 + 3.0 * 0.044715 * hidden * hidden
    )
    return (gelu_value, gelu_slope)


def mm(spec, a, b):
    return jnp.einsum(spec, a, b, preferred_element_type=jnp.float32)


def regroup(piece, group_count):
    local_blocks, block_width, token_count = piece.shape
    stacked = piece.reshape(local_blocks, group_count, block_width // group_count, token_count)
    arrived = lax.all_to_all(stacked, "bfly", split_axis=1, concat_axis=1, tiled=True)
    return arrived.reshape(local_blocks, block_width, token_count)


def any_mesh(tokens, grad_out, weight_a, weight_b, weight_c, weight_e):
    group_count = lax.axis_size("bfly")
    full_a, full_b, full_c, full_e = (
        lax.all_gather(w, "dp", axis=1, tiled=True)
        for w in (weight_a, weight_b, weight_c, weight_e)
    )
    token_count = tokens.shape[0]
    inner_blocks = full_a.shape[0]
    spread_width = full_a.shape[2]
    local_blocks = full_b.shape[0]
    inputs = tokens.reshape(token_count, inner_blocks, BLK).transpose(1, 2, 0)
    upstream = grad_out.reshape(token_count, inner_blocks, BLK).transpose(1, 2, 0)
    hidden_view = (local_blocks, BLK, token_count)
    wide_view = (inner_blocks, spread_width, token_count)
    spread = mm("kit,kio->kot", inputs, full_a).astype(jnp.bfloat16).reshape(hidden_view)
    back_out = mm("kjt,koj->kot", upstream, full_e).astype(jnp.bfloat16).reshape(hidden_view)
    permuted = regroup(spread, group_count)
    back_mid = regroup(back_out, group_count)
    gelu_value, gelu_slope = gelu_pair(mm("qit,qij->qjt", permuted, full_b))
    active = gelu_value.astype(jnp.bfloat16)
    narrowed = mm("qit,qij->qjt", active, full_c).astype(jnp.bfloat16)
    back_hidden = (mm("qjt,qij->qit", back_mid, full_c) * gelu_slope).astype(jnp.bfloat16)
    back_first = mm("qjt,qij->qit", back_hidden, full_b).astype(jnp.bfloat16)
    returned = regroup(narrowed, group_count).reshape(wide_view)
    back_spread = regroup(back_first, group_count).reshape(wide_view)
    output = mm("kot,koj->kjt", returned, full_e)
    back_input = mm("kot,kio->kit", back_spread, full_a)
    parts = (
        mm("kit,kot->kio", inputs, back_spread),
        mm("qit,qjt->qij", permuted, back_hidden),
        mm("qit,qjt->qij", active, back_mid),
        mm("kot,kjt->koj", returned, upstream),
    )
    grads = tuple(
        lax.psum_scatter(part.astype(jnp.bfloat16), "dp", scatter_dimension=1, tiled=True).astype(
            jnp.float32
        )
        for part in parts
    )

    def rows(x):
        return x.astype(jnp.bfloat16).transpose(2, 0, 1).reshape(token_count, inner_blocks * BLK)

    return (rows(output), rows(back_input)) + grads


def xor_permute(x, mask, axis="bfly"):
    return lax.ppermute(x, axis, [(i, i ^ mask) for i in range(lax.axis_size(axis))])


def exchange(x, axes):
    return lax.all_to_all(x, axes, split_axis=0, concat_axis=0, tiled=True)


def deal_weight(w):
    pairs = lax.axis_size("dp") // 2
    sets = w.reshape(pairs, 3, 2, w.shape[1], w.shape[2])
    own = jnp.stack([sets[:, 0], sets[:, 2]], axis=1)
    mid = sets[:, 1][:, :, None]
    return jnp.concatenate([own, mid], axis=2).reshape((pairs * 2, 3) + sets.shape[3:])


def gather_bfly(w, across):
    return [w, xor_permute(w, 1), across, xor_permute(across, 1)]


def after(x, *earlier):
    return lax.optimization_barrier((x,) + earlier)[0]


def add(x, y):
    return (x.astype(jnp.float32) + y.astype(jnp.float32)).astype(jnp.bfloat16)


def deal_tokens(x):
    ndp, nb = lax.axis_size("dp"), lax.axis_size("bfly")
    pairs, count = ndp // 2, x.shape[0]
    view = x.reshape(count, pairs, 3, BLK)
    own = view[:, :, 0::2].reshape(nb, count // nb, ndp, BLK).transpose(2, 0, 1, 3)
    mid = view[:, :, 1].reshape(2, nb, count // nb // 2, pairs, BLK).transpose(3, 0, 1, 2, 4)
    mid = mid.reshape(ndp, nb, count // nb // 2, BLK)
    return jnp.concatenate([own, mid], axis=2).reshape(ndp * nb, -1, BLK)


def undeal_tokens(got, count):
    ndp, nb = lax.axis_size("dp"), lax.axis_size("bfly")
    pairs, own_count = ndp // 2, count // nb
    own = got[:, :own_count].reshape(pairs, 2, count, BLK)
    mid = got[:, own_count:].reshape(pairs, 1, count, BLK)
    sets = jnp.concatenate([own[:, :1], mid, own[:, 1:]], axis=1)
    return sets.transpose(2, 0, 1, 3).reshape(count, pairs * 3 * BLK)


def dot(x, y, contract_x, contract_y):
    dims = (((contract_x,), (contract_y,)), ((), ()))
    return lax.dot_general(x, y, dims, preferred_element_type=jnp.float32)


def square(x):
    return x.reshape(BLK, BLK)


def half_src(part, r):
    return pl.ds(r * (part // 2), part // 2)


def weight_of(slot, w, v, shared):
    def get(m, which, r):
        if slot == 0:
            return square(w[which // 2][m][:, r, which % 2])
        ref = w[which // 2][m] if r == 0 else v[which // 2][m]
        return square(ref[:, shared if r == 0 else 0, which % 2])

    return get


def wide_weight(slot, w, e_ref, y, ndp):
    def get(m, r):
        if slot == 0:
            return square(w[1][m][half_src(ndp, r), :2, 1])
        return square(e_ref[m, half_src(ndp, r ^ y)])

    return get


def join_halves(w, v, e_ref, y, shared):
    for m in range(4):
        e_ref[m, :, y] = w[1][m][:, shared, 1]
        e_ref[m, :, 1 - y] = v[1][m][:, 0, 1]


def weight_refs(refs):
    return (refs[:4], refs[4:8]), (refs[8:12], refs[12:16]), refs[16:]


def forward_kernel(seat_ref, x_ref, *refs):
    w, v, (out_ref, *refs) = weight_refs(refs)
    saved, e_ref = (refs[:4], refs[4:8]), refs[8]
    ndp, nb, all_rows, _ = x_ref.shape
    own_rows = 2 * all_rows // 3
    f, y = seat_ref[0], seat_ref[1]
    join_halves(w, v, e_ref, y, 2)
    for slot, (lo, hi) in enumerate(((0, own_rows), (own_rows, all_rows))):
        perm, active, slope, ret = saved[slot]
        weight, wide = weight_of(slot, w, v, 2), wide_weight(slot, w, e_ref, y, ndp)
        count = ndp * (hi - lo)
        tiles = (nb, BLK // nb, count)
        for m in range(nb):
            d = f ^ m
            x = x_ref[:, d, lo:hi, :].reshape(count, BLK)
            for r in range(2):
                spread = dot(weight(m, 0, r), x, 0, 1).astype(jnp.bfloat16)
                perm[r, :, d] = spread.reshape(tiles)
        for m in range(nb):
            s = f ^ m
            for r in range(2):
                p = perm[r, s].reshape(BLK, count)
                value, grade = gelu_pair(dot(weight(m, 1, r), p, 0, 0))
                value = value.astype(jnp.bfloat16)
                active[r, s] = value
                slope[r, s] = grade.astype(jnp.bfloat16)
                narrowed = dot(weight(m, 2, r), value, 0, 0).astype(jnp.bfloat16)
                ret[r, :, s] = narrowed.reshape(tiles)
        for m in range(nb):
            d = f ^ m
            total = 0.0
            for r in range(2):
                total = total + dot(ret[r, d].reshape(BLK, count), wide(m, r), 0, 0)
            out_ref[:, d, lo:hi, :] = total.astype(jnp.bfloat16).reshape(ndp, hi - lo, BLK)


class Streamed:
    def __init__(self, sources, targets, sems, order):
        self.targets, self.waiting = targets, {}
        for i in order:
            self.waiting[i] = pltpu.make_async_copy(sources[i], targets[i], sems.at[i])
            self.waiting[i].start()

    def get(self, i):
        if i in self.waiting:
            self.waiting.pop(i).wait()
        return self.targets[i]


class Lookup:
    def __init__(self, streamed, indices):
        self.streamed, self.indices = streamed, indices

    def __getitem__(self, at):
        return self.streamed.get(self.indices[at])


BACKWARD_ORDER = (
    (1, 6, 13, 7, 8, 9, 2, 10, 11, 12, 3, 4, 5, 0),
    (1, 6, 14, 7, 15, 8, 16, 9, 17, 21, 2, 18, 19, 20, 3, 4, 5, 10, 11, 12, 13, 0, 22),
)


def backward_kernel(slot, seat_ref, *refs):
    order = BACKWARD_ORDER[slot]
    count_in, count_out = len(order), 6 if slot else 4
    sources, refs = list(refs[:count_in]), refs[count_in:]
    results, refs = refs[:count_out], refs[count_out:]
    targets, refs = refs[:count_in], refs[count_in:]
    (gin_ref, keep, send_ref, mid, spread), refs = refs[:5], refs[5:]
    e_ref = refs[0] if slot else None
    in_sems, out_sems = refs[-2:]

    ndp, nb, all_rows, _ = sources[0].shape
    lo, hi = (2 * all_rows // 3, all_rows) if slot else (0, 2 * all_rows // 3)
    for i in range(2):
        sources[i] = sources[i].at[:, :, lo:hi]
    for i in range(2, 10):
        sources[i] = sources[i].at[:, 2:] if slot else sources[i].at[:, :2]
    streamed = Streamed(sources, targets, in_sems, order)
    at = [Lookup(streamed, range(i, i + 4)) for i in range(2, 22, 4)]
    w, v = at[:2], at[2:4] if slot else None
    perm, active, slope, ret = (
        functools.partial(streamed.get, (18 if slot else 10) + i) for i in range(4)
    )
    sent = []

    def send(source, target):
        sent.append(pltpu.make_async_copy(source, target, out_sems.at[len(sent)]))
        sent[-1].start()

    rows, half = BLK // ndp, ndp // 2
    f, y = seat_ref[0], seat_ref[1]

    def store(m, which, r, part):
        ref = (keep, send_ref)[m % 2]
        part = part.astype(jnp.bfloat16).reshape(ndp, rows, BLK)
        if slot == 0:
            ref[m // 2, :, r, which] = part
        else:
            ref[r, m // 2, :, which] = part

    def store_wide(m, r, part):
        ref = (keep, send_ref)[m % 2]
        part = part.astype(jnp.bfloat16).reshape(half, 2, rows, BLK)
        if slot == 0:
            ref[m // 2, half_src(ndp, r), :, 3] = part
        else:
            ref[y, m // 2, half_src(ndp, r ^ y), 3] = part[:, 0]
            ref[1 - y, m // 2, half_src(ndp, r ^ y), 3] = part[:, 1]

    if slot:
        join_halves(w, v, e_ref, y, 0)
    weight, wide = weight_of(slot, w, v, 0), wide_weight(slot, w, e_ref, y, ndp)
    count = ndp * (hi - lo)
    tiles = (nb, BLK // nb, count)
    for m in range(nb):
        d = f ^ m
        g = streamed.get(1)[:, d].reshape(count, BLK)
        for r in range(2):
            mid[r, :, d] = dot(wide(m, r), g, 1, 1).astype(jnp.bfloat16).reshape(tiles)
            store_wide(m, r, dot(ret()[r, d].reshape(BLK, count), g, 1, 0))
    for m in range(nb):
        s = f ^ m
        for r in range(2):
            p = perm()[r, s].reshape(BLK, count)
            back_mid = mid[r, s].reshape(BLK, count)
            back = dot(weight(m, 2, r), back_mid, 1, 0)
            back = (back * slope()[r, s].astype(jnp.float32)).astype(jnp.bfloat16)
            store(m, 2, r, dot(active()[r, s], back_mid, 1, 1))
            store(m, 1, r, dot(p, back, 1, 1))
            first = dot(weight(m, 1, r), back, 1, 0).astype(jnp.bfloat16)
            spread[r, :, s] = first.reshape(tiles)
    for m in range(nb):
        d = f ^ m
        x = streamed.get(0)[:, d].reshape(count, BLK)
        total = 0.0
        for r in range(2):
            back = spread[r, d].reshape(BLK, count)
            total = total + dot(back, weight(m, 0, r), 0, 1)
            store(m, 0, r, dot(x, back, 0, 1))
        gin_ref[:, d] = total.astype(jnp.bfloat16).reshape(ndp, hi - lo, BLK)
    send(keep, results[1])
    if slot == 0:
        send(send_ref.at[0], results[2])
        send(send_ref.at[1], results[3])
        send(gin_ref, results[0])
    else:
        for i in range(4):
            send(send_ref.at[i // 2, i % 2], results[2 + i])
        send(streamed.get(22), results[0].at[:, :, :lo])
        send(gin_ref, results[0].at[:, :, lo:])
    for copy in sent:
        copy.wait()


def grads_kernel(got_ref, a_ref, b_ref, c_ref, e_ref):
    pairs = got_ref.shape[0] // 2
    rows = got_ref.shape[3]
    for which, ref in enumerate((a_ref, b_ref, c_ref, e_ref)):
        for place in range(6):
            owner, part = ((0, 0), (0, 1), (0, 2), (1, 2), (1, 0), (1, 1))[place]
            for i in range(pairs):
                value = got_ref[2 * i + owner, part, which].astype(jnp.float32)
                if which == 0:
                    ref[3 * i + place // 2, :, (place % 2) * BLK : (place % 2 + 1) * BLK] = value
                elif which == 3:
                    ref[3 * i + place // 2, (place % 2) * rows : (place % 2 + 1) * rows, :] = value
                else:
                    ref[6 * i + place] = value


def on_chip(kernel, products, outs, scratch, inputs, targets=None):
    space = pltpu.VMEM if targets is None else pl.ANY
    sems = [pltpu.SemaphoreType.DMA((n,)) for n in (len(inputs) - 1, len(outs) + 1)]
    return pl.pallas_call(
        kernel,
        out_shape=[jax.ShapeDtypeStruct(shape, jnp.bfloat16) for shape in outs],
        in_specs=[pl.BlockSpec(memory_space=pltpu.SMEM)]
        + [pl.BlockSpec(memory_space=space)] * (len(inputs) - 1),
        out_specs=[pl.BlockSpec(memory_space=space)] * len(outs),
        scratch_shapes=[pltpu.VMEM(shape, jnp.bfloat16) for shape in (targets or []) + scratch]
        + (sems if targets else []),
        cost_estimate=pl.CostEstimate(
            flops=products * 2 * BLK * BLK,
            transcendentals=0,
            bytes_accessed=sum(x.size for x in inputs) * 2 + sum(map(math.prod, outs)) * 2,
        ),
        compiler_params=pltpu.CompilerParams(vmem_limit_bytes=56 * 2**20),
    )(*inputs)


def token_plan(tokens, grad_out, weight_a, weight_b, weight_c, weight_e):
    ndp, nb = lax.axis_size("dp"), lax.axis_size("bfly")
    blocks, rows, _ = weight_a.shape
    parts, count = 2 * blocks, tokens.shape[0]
    dealt_a = weight_a.reshape(blocks, rows, 2, BLK).transpose(0, 2, 1, 3).reshape(parts, rows, BLK)
    dealt_e = weight_e.reshape(parts, rows, BLK)
    seat = jnp.stack([lax.axis_index("bfly"), lax.axis_index("dp") % 2]).astype(jnp.int32)

    everyone = ("dp", "bfly")
    shape = (ndp, nb, -1, BLK)
    def deal(first, second):
        return jnp.stack([deal_weight(first), deal_weight(second)], axis=2)

    def with_halves(w):
        across = xor_permute(w, 2)
        return (w, across) + tuple(xor_permute(part[:, 2:], 1, "dp") for part in (w, across))

    ab = with_halves(exchange(deal(dealt_a, weight_b), "dp"))
    ce = with_halves(exchange(after(deal(weight_c, dealt_e), ab[0]), "dp"))
    x = exchange(after(deal_tokens(tokens), ce[0], *ab[1:]), everyone)
    g = exchange(after(deal_tokens(grad_out), x, *ce[1:]), everyone).reshape(shape)
    x = x.reshape(shape)
    weights = gather_bfly(*ab[:2]) + gather_bfly(*ce[:2])
    weights += gather_bfly(*ab[2:]) + gather_bfly(*ce[2:])

    own, mid = count * ndp // nb, count * ndp // nb // 2
    saved = []
    for t in (own, mid):
        tiled, whole = (2, nb, nb, BLK // nb, t), (2, nb, BLK, t)
        saved += [tiled, whole, whole, tiled]
    halves = (nb, ndp, 2, rows, BLK)
    products = 2 * nb * (own + mid)
    out, *kept = on_chip(
        forward_kernel, 4 * products, [x.shape] + saved, [halves], [seat, x] + weights
    )
    out = exchange(out.reshape(ndp * nb, -1, BLK), everyone)
    own_shape, mid_shape = (2, ndp, 2, 4, rows, BLK), (2, 2, ndp, 4, rows, BLK)
    weight_shape = (ndp, 1, 2, rows, BLK)
    own_rows, mid_rows = ((ndp, nb, t // ndp, BLK) for t in (own, mid))
    gin, own_keep, *own_sends = on_chip(
        functools.partial(backward_kernel, 0),
        16 * nb * own,
        [own_rows, own_shape] + [own_shape[1:]] * 2,
        [own_rows, own_shape, own_shape] + [saved[0]] * 2,
        [seat, x, g] + weights[:8] + kept[:4],
        [own_rows] * 2 + [(ndp, 2) + weight_shape[2:]] * 8 + saved[:4],
    )
    gin, mid_keep, *mid_sends = on_chip(
        functools.partial(backward_kernel, 1),
        16 * nb * mid,
        [x.shape, mid_shape] + [mid_shape[2:]] * 4,
        [mid_rows, mid_shape, mid_shape] + [saved[4]] * 2 + [halves],
        [seat, x, g] + weights + kept[4:] + [gin],
        [mid_rows] * 2 + [weight_shape] * 16 + saved[4:] + [own_rows],
    )
    own_far = add(own_keep[1], xor_permute(own_sends[1], 1))
    far = add(mid_keep[1, 1], after(xor_permute(mid_sends[3], 1), own_far))
    far = add(add(mid_keep[0, 1], xor_permute(mid_sends[1], 1)), xor_permute(far, 1, "dp"))
    own_near = add(own_keep[0], xor_permute(own_sends[0], 1))
    near = add(mid_keep[1, 0], xor_permute(mid_sends[2], 1))
    part = ndp // 2
    own_first = add(own_near[:part], xor_permute(own_far[:part], 2))
    gin = exchange(after(gin.reshape(ndp * nb, -1, BLK), out, far, own_first), everyone)
    own_last = add(own_near[part:], xor_permute(after(own_far[part:], own_first), 2))
    own = jnp.concatenate([own_first, own_last], axis=0)
    near = xor_permute(near, 1, "dp")
    near = add(add(mid_keep[0, 0], xor_permute(mid_sends[0], 1)), near)
    mid = add(near, xor_permute(far, 2))
    dealt = jnp.concatenate([own, mid[:, None]], axis=1)
    got = exchange(after(dealt, gin), "dp")
    grads = pl.pallas_call(
        grads_kernel,
        out_shape=[
            jax.ShapeDtypeStruct(w.shape, jnp.float32)
            for w in (weight_a, weight_b, weight_c, weight_e)
        ],
    )(got)
    return (undeal_tokens(out, count), undeal_tokens(gin, count), *grads)


def per_device(tokens, grad_out, weight_a, weight_b, weight_c, weight_e):
    ndp, nb = lax.axis_size("dp"), lax.axis_size("bfly")
    fits = nb == 4 and ndp % 2 == 0 and 2 * weight_a.shape[0] == 3 * ndp
    fits = fits and tokens.shape[0] % (32 * nb) == 0 and weight_a.shape[1] * ndp == BLK
    fits = fits and weight_a.shape[2] == 2 * BLK and weight_e.shape[1] == 2 * weight_a.shape[1]
    plan = token_plan if fits else any_mesh
    return plan(tokens, grad_out, weight_a, weight_b, weight_c, weight_e)


def solution(mesh):
    in_specs = (P("dp", "bfly"),) * 2 + (P("bfly", "dp", None),) * 4
    return jax.shard_map(
        per_device, mesh=mesh, in_specs=in_specs, out_specs=in_specs, check_vma=False
    )
```

```python
import math

import jax
import jax.numpy as jnp
from jax import lax
from jax.experimental import pallas as pl
from jax.experimental.pallas import tpu as pltpu
from jax.sharding import PartitionSpec as P

BLK = 256

gelu_scale = 0.7978845608028654


def gelu_pair(hidden):
    inner_arg = gelu_scale * (hidden + 0.044715 * hidden * hidden * hidden)
    tangent = jnp.tanh(inner_arg)
    gelu_value = 0.5 * hidden * (1.0 + tangent)
    gelu_slope = 0.5 * (1.0 + tangent) + 0.5 * hidden * (1.0 - tangent * tangent) * gelu_scale * (
        1.0 + 3.0 * 0.044715 * hidden * hidden
    )
    return (gelu_value, gelu_slope)


def mm(spec, a, b):
    return jnp.einsum(spec, a, b, preferred_element_type=jnp.float32)


def regroup(piece, group_count):
    local_blocks, block_width, token_count = piece.shape
    stacked = piece.reshape(local_blocks, group_count, block_width // group_count, token_count)
    arrived = lax.all_to_all(stacked, "bfly", split_axis=1, concat_axis=1, tiled=True)
    return arrived.reshape(local_blocks, block_width, token_count)


def any_mesh(tokens, grad_out, weight_a, weight_b, weight_c, weight_e):
    group_count = lax.axis_size("bfly")
    full_a, full_b, full_c, full_e = (
        lax.all_gather(w, "dp", axis=1, tiled=True)
        for w in (weight_a, weight_b, weight_c, weight_e)
    )
    token_count = tokens.shape[0]
    inner_blocks = full_a.shape[0]
    spread_width = full_a.shape[2]
    local_blocks = full_b.shape[0]
    inputs = tokens.reshape(token_count, inner_blocks, BLK).transpose(1, 2, 0)
    upstream = grad_out.reshape(token_count, inner_blocks, BLK).transpose(1, 2, 0)
    hidden_view = (local_blocks, BLK, token_count)
    wide_view = (inner_blocks, spread_width, token_count)
    spread = mm("kit,kio->kot", inputs, full_a).astype(jnp.bfloat16).reshape(hidden_view)
    back_out = mm("kjt,koj->kot", upstream, full_e).astype(jnp.bfloat16).reshape(hidden_view)
    permuted = regroup(spread, group_count)
    back_mid = regroup(back_out, group_count)
    gelu_value, gelu_slope = gelu_pair(mm("qit,qij->qjt", permuted, full_b))
    active = gelu_value.astype(jnp.bfloat16)
    narrowed = mm("qit,qij->qjt", active, full_c).astype(jnp.bfloat16)
    back_hidden = (mm("qjt,qij->qit", back_mid, full_c) * gelu_slope).astype(jnp.bfloat16)
    back_first = mm("qjt,qij->qit", back_hidden, full_b).astype(jnp.bfloat16)
    returned = regroup(narrowed, group_count).reshape(wide_view)
    back_spread = regroup(back_first, group_count).reshape(wide_view)
    output = mm("kot,koj->kjt", returned, full_e)
    back_input = mm("kot,kio->kit", back_spread, full_a)
    parts = (
        mm("kit,kot->kio", inputs, back_spread),
        mm("qit,qjt->qij", permuted, back_hidden),
        mm("qit,qjt->qij", active, back_mid),
        mm("kot,kjt->koj", returned, upstream),
    )
    grads = tuple(
        lax.psum_scatter(part.astype(jnp.bfloat16), "dp", scatter_dimension=1, tiled=True).astype(
            jnp.float32
        )
        for part in parts
    )

    def rows(x):
        return x.astype(jnp.bfloat16).transpose(2, 0, 1).reshape(token_count, inner_blocks * BLK)

    return (rows(output), rows(back_input)) + grads


def xor_permute(x, mask, axis="bfly"):
    return lax.ppermute(x, axis, [(i, i ^ mask) for i in range(lax.axis_size(axis))])


def exchange(x, axes):
    return lax.all_to_all(x, axes, split_axis=0, concat_axis=0, tiled=True)


def weight_sets(w):
    pairs = lax.axis_size("dp") // 2
    sets = w.reshape(pairs, 3, 2, w.shape[1], w.shape[2])
    own = jnp.stack([sets[:, 0], sets[:, 2]], axis=1)
    return own.reshape((pairs * 2,) + own.shape[2:]), sets[:, 1].reshape(pairs * 2, *w.shape[1:])


def gather_bfly(w, across):
    return [w, xor_permute(w, 1), across, xor_permute(across, 1)]


def after(x, *earlier):
    return lax.optimization_barrier((x,) + earlier)[0]


def add(x, y):
    return (x.astype(jnp.float32) + y.astype(jnp.float32)).astype(jnp.bfloat16)


def deal_tokens(x):
    ndp, nb = lax.axis_size("dp"), lax.axis_size("bfly")
    pairs, count = ndp // 2, x.shape[0]
    view = x.reshape(count, pairs, 3, BLK)
    own = view[:, :, 0::2].reshape(nb, count // nb, ndp, BLK).transpose(2, 0, 1, 3)
    mid = view[:, :, 1].reshape(2, nb, count // nb // 2, pairs, BLK).transpose(3, 0, 1, 2, 4)
    mid = mid.reshape(ndp, nb, count // nb // 2, BLK)
    return jnp.concatenate([own, mid], axis=2).reshape(ndp * nb, -1, BLK)


def undeal_tokens(got, count):
    ndp, nb = lax.axis_size("dp"), lax.axis_size("bfly")
    pairs, own_count = ndp // 2, count // nb
    own = got[:, :own_count].reshape(pairs, 2, count, BLK)
    mid = got[:, own_count:].reshape(pairs, 1, count, BLK)
    sets = jnp.concatenate([own[:, :1], mid, own[:, 1:]], axis=1)
    return sets.transpose(2, 0, 1, 3).reshape(count, pairs * 3 * BLK)


def dot(x, y, contract_x, contract_y):
    dims = (((contract_x,), (contract_y,)), ((), ()))
    return lax.dot_general(x, y, dims, preferred_element_type=jnp.float32)


def square(x):
    return x.reshape(BLK, BLK)


def half_src(part, r):
    return pl.ds(r * (part // 2), part // 2)


def weight_of(slot, own, shared):
    def get(m, which, r):
        if slot == 0:
            return square(own[which // 2][m][:, r, which % 2])
        return square(shared[r][m][:, which])

    return get


def wide_weight(slot, own, e_ref, y):
    def get(m, r):
        if slot == 0:
            return square(own[1][m][half_src(e_ref.shape[1], r), :, 1])
        return square(e_ref[m, half_src(e_ref.shape[1], r ^ y)])

    return get


def join_halves(shared, e_ref, y):
    for m in range(4):
        e_ref[m, :, y] = shared[0][m][:, 3]
        e_ref[m, :, 1 - y] = shared[1][m][:, 3]


def weight_refs(refs):
    return (refs[:4], refs[4:8]), (refs[8:12], refs[12:16]), refs[16:]


def forward_kernel(seat_ref, x_ref, *refs):
    w, v, (out_ref, *refs) = weight_refs(refs)
    saved, e_ref = (refs[:4], refs[4:8]), refs[8]
    ndp, nb, all_rows, _ = x_ref.shape
    own_rows = 2 * all_rows // 3
    f, y = seat_ref[0], seat_ref[1]
    join_halves(v, e_ref, y)
    for slot, (lo, hi) in enumerate(((0, own_rows), (own_rows, all_rows))):
        perm, active, slope, ret = saved[slot]
        weight, wide = weight_of(slot, w, v), wide_weight(slot, w, e_ref, y)
        count = ndp * (hi - lo)
        tiles = (nb, BLK // nb, count)
        for m in range(nb):
            d = f ^ m
            x = x_ref[:, d, lo:hi, :].reshape(count, BLK)
            for r in range(2):
                spread = dot(weight(m, 0, r), x, 0, 1).astype(jnp.bfloat16)
                perm[r, :, d] = spread.reshape(tiles)
        for m in range(nb):
            s = f ^ m
            for r in range(2):
                p = perm[r, s].reshape(BLK, count)
                value, grade = gelu_pair(dot(weight(m, 1, r), p, 0, 0))
                value = value.astype(jnp.bfloat16)
                active[r, s] = value
                slope[r, s] = grade.astype(jnp.bfloat16)
                narrowed = dot(weight(m, 2, r), value, 0, 0).astype(jnp.bfloat16)
                ret[r, :, s] = narrowed.reshape(tiles)
        for m in range(nb):
            d = f ^ m
            total = 0.0
            for r in range(2):
                total = total + dot(ret[r, d].reshape(BLK, count), wide(m, r), 0, 0)
            out_ref[:, d, lo:hi, :] = total.astype(jnp.bfloat16).reshape(ndp, hi - lo, BLK)


class Streamed:
    def __init__(self, sources, targets, sems, order):
        self.targets, self.waiting = targets, {}
        for i in order:
            self.waiting[i] = pltpu.make_async_copy(sources[i], targets[i], sems.at[i])
            self.waiting[i].start()

    def get(self, i):
        if i in self.waiting:
            self.waiting.pop(i).wait()
        return self.targets[i]


class Lookup:
    def __init__(self, streamed, indices):
        self.streamed, self.indices = streamed, indices

    def __getitem__(self, at):
        return self.streamed.get(self.indices[at])


BACKWARD_ORDER = (
    (1, 6, 21, 7, 8, 9, 2, 18, 19, 20, 3, 4, 5, 0) + tuple(range(14, 18)) + (25,) + tuple(range(10, 14)) + (22, 23, 24)
)


def backward_kernel(seat_ref, *refs):
    count_in = len(BACKWARD_ORDER)
    sources, refs = refs[:count_in], refs[count_in:]
    results, refs = refs[:9], refs[9:]
    targets, refs = refs[:count_in], refs[count_in:]
    staged, refs = refs[:5], refs[5:]
    scratch, (e_ref, in_sems, out_sems) = (refs[:2], refs[2:4]), refs[4:]
    streamed = Streamed(sources, targets, in_sems, BACKWARD_ORDER)
    at = [Lookup(streamed, range(i, i + 4)) for i in range(2, 26, 4)]
    w, v, saved = at[:2], at[2:4], at[4:]
    gin_ref, own_keep, own_send, mid_keep, mid_send = staged
    sent = []

    def send(source, target):
        sent.append(pltpu.make_async_copy(source, target, out_sems.at[len(sent)]))
        sent[-1].start()

    ndp, nb, all_rows, _ = targets[0].shape
    own_rows = 2 * all_rows // 3
    rows = BLK // ndp
    f, y = seat_ref[0], seat_ref[1]

    def store(slot, m, which, r, part):
        ref = ((own_keep, own_send), (mid_keep, mid_send))[slot][m % 2]
        if slot == 0:
            ref[m // 2, :, r, which] = part.astype(jnp.bfloat16).reshape(ndp, rows, BLK)
        else:
            ref[r, m // 2, :, which] = part.astype(jnp.bfloat16).reshape(ndp, rows, BLK)

    def store_wide(slot, m, r, part):
        ref = ((own_keep, own_send), (mid_keep, mid_send))[slot][m % 2]
        part = part.astype(jnp.bfloat16).reshape(ndp // 2, 2, rows, BLK)
        if slot == 0:
            ref[m // 2, half_src(ndp, r), :, 3] = part
        else:
            ref[y, m // 2, half_src(ndp, r ^ y), 3] = part[:, 0]
            ref[1 - y, m // 2, half_src(ndp, r ^ y), 3] = part[:, 1]

    for slot, (lo, hi) in enumerate(((0, own_rows), (own_rows, all_rows))):
        perm, active, slope, ret = range(4)
        mid, spread = scratch[slot]
        if slot == 1:
            join_halves(v, e_ref, y)
        weight, wide = weight_of(slot, w, v), wide_weight(slot, w, e_ref, y)
        count = ndp * (hi - lo)
        tiles = (nb, BLK // nb, count)
        for m in range(nb):
            d = f ^ m
            g = streamed.get(1)[:, d, lo:hi, :].reshape(count, BLK)
            for r in range(2):
                mid[r, :, d] = dot(wide(m, r), g, 1, 1).astype(jnp.bfloat16).reshape(tiles)
                store_wide(slot, m, r, dot(saved[slot][ret][r, d].reshape(BLK, count), g, 1, 0))
        for m in range(nb):
            s = f ^ m
            for r in range(2):
                p = saved[slot][perm][r, s].reshape(BLK, count)
                back_mid = mid[r, s].reshape(BLK, count)
                back = dot(weight(m, 2, r), back_mid, 1, 0)
                back = (back * saved[slot][slope][r, s].astype(jnp.float32)).astype(jnp.bfloat16)
                store(slot, m, 2, r, dot(saved[slot][active][r, s], back_mid, 1, 1))
                store(slot, m, 1, r, dot(p, back, 1, 1))
                first = dot(weight(m, 1, r), back, 1, 0).astype(jnp.bfloat16)
                spread[r, :, s] = first.reshape(tiles)
        for m in range(nb):
            d = f ^ m
            x = streamed.get(0)[:, d, lo:hi, :].reshape(count, BLK)
            total = 0.0
            for r in range(2):
                back = spread[r, d].reshape(BLK, count)
                total = total + dot(back, weight(m, 0, r), 0, 1)
                store(slot, m, 0, r, dot(x, back, 0, 1))
            gin_ref[:, d, lo:hi, :] = total.astype(jnp.bfloat16).reshape(ndp, hi - lo, BLK)
        if slot == 0:
            send(own_keep, results[1])
            send(own_send.at[0], results[2])
            send(own_send.at[1], results[3])
    send(mid_keep, results[4])
    for i in range(4):
        send(mid_send.at[i // 2, i % 2], results[5 + i])
    send(gin_ref, results[0])
    for copy in sent:
        copy.wait()


def grads_kernel(got_ref, a_ref, b_ref, c_ref, e_ref):
    pairs = got_ref.shape[0] // 2
    rows = got_ref.shape[3]
    for which, ref in enumerate((a_ref, b_ref, c_ref, e_ref)):
        for place in range(6):
            owner, part = ((0, 0), (0, 1), (0, 2), (1, 2), (1, 0), (1, 1))[place]
            for i in range(pairs):
                value = got_ref[2 * i + owner, part, which].astype(jnp.float32)
                if which == 0:
                    ref[3 * i + place // 2, :, (place % 2) * BLK : (place % 2 + 1) * BLK] = value
                elif which == 3:
                    ref[3 * i + place // 2, (place % 2) * rows : (place % 2 + 1) * rows, :] = value
                else:
                    ref[6 * i + place] = value


def on_chip(kernel, products, outs, scratch, inputs, results=None):
    streamed = results is not None
    space = pl.ANY if streamed else pltpu.VMEM
    staged = [x.shape for x in inputs[1:]] + outs if streamed else []
    outs = results or outs
    sems = [pltpu.SemaphoreType.DMA((n,)) for n in (len(inputs) - 1, len(outs))]
    return pl.pallas_call(
        kernel,
        out_shape=[jax.ShapeDtypeStruct(shape, jnp.bfloat16) for shape in outs],
        in_specs=[pl.BlockSpec(memory_space=pltpu.SMEM)]
        + [pl.BlockSpec(memory_space=space)] * (len(inputs) - 1),
        out_specs=[pl.BlockSpec(memory_space=space)] * len(outs),
        scratch_shapes=[pltpu.VMEM(shape, jnp.bfloat16) for shape in staged + scratch]
        + (sems if streamed else []),
        cost_estimate=pl.CostEstimate(
            flops=products * 2 * BLK * BLK,
            transcendentals=0,
            bytes_accessed=sum(x.size for x in inputs) * 2 + sum(map(math.prod, outs)) * 2,
        ),
        compiler_params=pltpu.CompilerParams(vmem_limit_bytes=56 * 2**20),
    )(*inputs)


def token_plan(tokens, grad_out, weight_a, weight_b, weight_c, weight_e):
    ndp, nb = lax.axis_size("dp"), lax.axis_size("bfly")
    blocks, rows, _ = weight_a.shape
    parts, count = 2 * blocks, tokens.shape[0]
    dealt_a = weight_a.reshape(blocks, rows, 2, BLK).transpose(0, 2, 1, 3).reshape(parts, rows, BLK)
    dealt_e = weight_e.reshape(parts, rows, BLK)
    seat = jnp.stack([lax.axis_index("bfly"), lax.axis_index("dp") % 2]).astype(jnp.int32)

    everyone = ("dp", "bfly")
    shape = (ndp, nb, -1, BLK)
    own, mid = zip(*(weight_sets(w) for w in (dealt_a, weight_b, weight_c, dealt_e)))
    own_ab = jnp.stack(own[:2], axis=2).reshape(ndp, 4, rows, BLK)
    first = exchange(jnp.concatenate([own_ab, jnp.stack(mid, axis=1)], axis=1), "dp")
    ab, mid = first[:, :4].reshape(ndp, 2, 2, rows, BLK), first[:, 4:]
    ce = exchange(after(jnp.stack(own[2:], axis=2), first), "dp")
    mid_across, ab_across, ce_across = (xor_permute(part, 2) for part in (mid, ab, ce))
    swapped, swapped_across = (xor_permute(part, 1, "dp") for part in (mid, mid_across))
    x = exchange(after(deal_tokens(tokens), ce, mid_across, swapped), everyone)
    g = after(deal_tokens(grad_out), x, ab_across, ce_across, swapped_across)
    g = exchange(g, everyone).reshape(shape)
    x = x.reshape(shape)
    weights = gather_bfly(ab, ab_across) + gather_bfly(ce, ce_across)
    weights += gather_bfly(mid, mid_across) + gather_bfly(swapped, swapped_across)

    own, mid = count * ndp // nb, count * ndp // nb // 2
    saved = []
    for t in (own, mid):
        tiled, whole = (2, nb, nb, BLK // nb, t), (2, nb, BLK, t)
        saved += [tiled, whole, whole, tiled]
    halves = (nb, ndp, 2, rows, BLK)
    products = 2 * nb * (own + mid)
    out, *kept = on_chip(
        forward_kernel, 4 * products, [x.shape] + saved, [halves], [seat, x] + weights
    )
    out = exchange(out.reshape(ndp * nb, -1, BLK), everyone)
    own_shape, mid_shape = (2, ndp, 2, 4, rows, BLK), (2, 2, ndp, 4, rows, BLK)
    gin, own_keep, *sends = on_chip(
        backward_kernel,
        8 * products,
        [x.shape, own_shape, own_shape, mid_shape, mid_shape],
        [saved[0], saved[0], saved[4], saved[4], halves],
        [seat, x, g] + weights + kept,
        [x.shape, own_shape] + [own_shape[1:]] * 2 + [mid_shape] + [mid_shape[2:]] * 4,
    )
    mid_keep = sends.pop(2)
    far = add(mid_keep[1, 1], xor_permute(sends[5], 1))
    own_far = add(own_keep[1], xor_permute(sends[1], 1))
    far = add(add(mid_keep[0, 1], xor_permute(sends[3], 1)), xor_permute(far, 1, "dp"))
    own_near = add(own_keep[0], xor_permute(sends[0], 1))
    near = add(mid_keep[1, 0], xor_permute(sends[4], 1))
    part = ndp // 2
    own_first = add(own_near[:part], xor_permute(own_far[:part], 2))
    gin = exchange(after(gin.reshape(ndp * nb, -1, BLK), out, far, own_first), everyone)
    own_last = add(own_near[part:], xor_permute(after(own_far[part:], own_first), 2))
    own = jnp.concatenate([own_first, own_last], axis=0)
    near = xor_permute(near, 1, "dp")
    near = add(add(mid_keep[0, 0], xor_permute(sends[2], 1)), near)
    mid = add(near, xor_permute(far, 2))
    dealt = jnp.concatenate([own, mid[:, None]], axis=1)
    got = exchange(after(dealt, gin), "dp")
    grads = pl.pallas_call(
        grads_kernel,
        out_shape=[
            jax.ShapeDtypeStruct(w.shape, jnp.float32)
            for w in (weight_a, weight_b, weight_c, weight_e)
        ],
    )(got)
    return (undeal_tokens(out, count), undeal_tokens(gin, count), *grads)


def per_device(tokens, grad_out, weight_a, weight_b, weight_c, weight_e):
    ndp, nb = lax.axis_size("dp"), lax.axis_size("bfly")
    fits = nb == 4 and ndp % 2 == 0 and 2 * weight_a.shape[0] == 3 * ndp
    fits = fits and tokens.shape[0] % (32 * nb) == 0 and weight_a.shape[1] * ndp == BLK
    fits = fits and weight_a.shape[2] == 2 * BLK and weight_e.shape[1] == 2 * weight_a.shape[1]
    plan = token_plan if fits else any_mesh
    return plan(tokens, grad_out, weight_a, weight_b, weight_c, weight_e)


def solution(mesh):
    in_specs = (P("dp", "bfly"),) * 2 + (P("bfly", "dp", None),) * 4
    return jax.shard_map(
        per_device, mesh=mesh, in_specs=in_specs, out_specs=in_specs, check_vma=False
    )
```

```python
import math

import jax
import jax.numpy as jnp
from jax import lax
from jax.experimental import pallas as pl
from jax.experimental.pallas import tpu as pltpu
from jax.sharding import PartitionSpec as P

BLK = 256

gelu_scale = 0.7978845608028654


def gelu_pair(hidden):
    inner_arg = gelu_scale * (hidden + 0.044715 * hidden * hidden * hidden)
    tangent = jnp.tanh(inner_arg)
    gelu_value = 0.5 * hidden * (1.0 + tangent)
    gelu_slope = 0.5 * (1.0 + tangent) + 0.5 * hidden * (1.0 - tangent * tangent) * gelu_scale * (
        1.0 + 3.0 * 0.044715 * hidden * hidden
    )
    return (gelu_value, gelu_slope)


def mm(spec, a, b):
    return jnp.einsum(spec, a, b, preferred_element_type=jnp.float32)


def regroup(piece, group_count):
    local_blocks, block_width, token_count = piece.shape
    stacked = piece.reshape(local_blocks, group_count, block_width // group_count, token_count)
    arrived = lax.all_to_all(stacked, "bfly", split_axis=1, concat_axis=1, tiled=True)
    return arrived.reshape(local_blocks, block_width, token_count)


def any_mesh(tokens, grad_out, weight_a, weight_b, weight_c, weight_e):
    group_count = lax.axis_size("bfly")
    full_a, full_b, full_c, full_e = (
        lax.all_gather(w, "dp", axis=1, tiled=True)
        for w in (weight_a, weight_b, weight_c, weight_e)
    )
    token_count = tokens.shape[0]
    inner_blocks = full_a.shape[0]
    spread_width = full_a.shape[2]
    local_blocks = full_b.shape[0]
    inputs = tokens.reshape(token_count, inner_blocks, BLK).transpose(1, 2, 0)
    upstream = grad_out.reshape(token_count, inner_blocks, BLK).transpose(1, 2, 0)
    hidden_view = (local_blocks, BLK, token_count)
    wide_view = (inner_blocks, spread_width, token_count)
    spread = mm("kit,kio->kot", inputs, full_a).astype(jnp.bfloat16).reshape(hidden_view)
    back_out = mm("kjt,koj->kot", upstream, full_e).astype(jnp.bfloat16).reshape(hidden_view)
    permuted = regroup(spread, group_count)
    back_mid = regroup(back_out, group_count)
    gelu_value, gelu_slope = gelu_pair(mm("qit,qij->qjt", permuted, full_b))
    active = gelu_value.astype(jnp.bfloat16)
    narrowed = mm("qit,qij->qjt", active, full_c).astype(jnp.bfloat16)
    back_hidden = (mm("qjt,qij->qit", back_mid, full_c) * gelu_slope).astype(jnp.bfloat16)
    back_first = mm("qjt,qij->qit", back_hidden, full_b).astype(jnp.bfloat16)
    returned = regroup(narrowed, group_count).reshape(wide_view)
    back_spread = regroup(back_first, group_count).reshape(wide_view)
    output = mm("kot,koj->kjt", returned, full_e)
    back_input = mm("kot,kio->kit", back_spread, full_a)
    parts = (
        mm("kit,kot->kio", inputs, back_spread),
        mm("qit,qjt->qij", permuted, back_hidden),
        mm("qit,qjt->qij", active, back_mid),
        mm("kot,kjt->koj", returned, upstream),
    )
    grads = tuple(
        lax.psum_scatter(part.astype(jnp.bfloat16), "dp", scatter_dimension=1, tiled=True).astype(
            jnp.float32
        )
        for part in parts
    )

    def rows(x):
        return x.astype(jnp.bfloat16).transpose(2, 0, 1).reshape(token_count, inner_blocks * BLK)

    return (rows(output), rows(back_input)) + grads


def xor_permute(x, mask, axis="bfly"):
    return lax.ppermute(x, axis, [(i, i ^ mask) for i in range(lax.axis_size(axis))])


def exchange(x, axes):
    return lax.all_to_all(x, axes, split_axis=0, concat_axis=0, tiled=True)


def own_sets(w):
    pairs = lax.axis_size("dp") // 2
    sets = w.reshape(pairs, 3, 2, w.shape[1], w.shape[2])
    own = jnp.stack([sets[:, 0], sets[:, 2]], axis=1)
    return own.reshape((pairs * 2,) + own.shape[2:])


def gather_bfly(w, across):
    return [w, xor_permute(w, 1), across, xor_permute(across, 1)]


def after(x, *earlier):
    return lax.optimization_barrier((x,) + earlier)[0]


def add(x, y):
    return (x.astype(jnp.float32) + y.astype(jnp.float32)).astype(jnp.bfloat16)


def deal_tokens(x):
    ndp, nb = lax.axis_size("dp"), lax.axis_size("bfly")
    pairs, count = ndp // 2, x.shape[0]
    view = x.reshape(count, pairs, 3, BLK)
    own = view[:, :, 0::2].reshape(nb, count // nb, ndp, BLK).transpose(2, 0, 1, 3)
    mid = view[:, :, 1].reshape(2, nb, count // nb // 2, pairs, BLK).transpose(3, 0, 1, 2, 4)
    mid = mid.reshape(ndp, nb, count // nb // 2, BLK)
    return jnp.concatenate([own, mid], axis=2).reshape(ndp * nb, -1, BLK)


def undeal_tokens(got, count):
    ndp, nb = lax.axis_size("dp"), lax.axis_size("bfly")
    pairs, own_count = ndp // 2, count // nb
    own = got[:, :own_count].reshape(pairs, 2, count, BLK)
    mid = got[:, own_count:].reshape(pairs, 1, count, BLK)
    sets = jnp.concatenate([own[:, :1], mid, own[:, 1:]], axis=1)
    return sets.transpose(2, 0, 1, 3).reshape(count, pairs * 3 * BLK)


def dot(x, y, contract_x, contract_y):
    dims = (((contract_x,), (contract_y,)), ((), ()))
    return lax.dot_general(x, y, dims, preferred_element_type=jnp.float32)


def square(x):
    return x.reshape(BLK, BLK)


def half_src(part, r):
    return pl.ds(r * (part // 2), part // 2)


def weight_of(slot, own, shared):
    def get(m, which, r):
        if slot == 0:
            return square(own[1][m][:, r, which - 1] if which else own[0][m][:, r])
        return square(shared[r][m][:, which])

    return get


def wide_weight(slot, own, e_ref, y):
    def get(m, r):
        if slot == 0:
            return square(own[1][m][half_src(e_ref.shape[1], r), :, 2])
        return square(e_ref[m, half_src(e_ref.shape[1], r ^ y)])

    return get


def join_halves(shared, e_ref, y):
    for m in range(4):
        e_ref[m, :, y] = shared[0][m][:, 3]
        e_ref[m, :, 1 - y] = shared[1][m][:, 3]


def weight_refs(refs):
    return (refs[:4], refs[4:8]), (refs[8:12], refs[12:16]), refs[16:]


def forward_kernel(seat_ref, x_ref, *refs):
    w, v, (out_ref, *refs) = weight_refs(refs)
    saved, e_ref = (refs[:4], refs[4:8]), refs[8]
    ndp, nb, all_rows, _ = x_ref.shape
    own_rows = 2 * all_rows // 3
    f, y = seat_ref[0], seat_ref[1]
    join_halves(v, e_ref, y)
    for slot, (lo, hi) in enumerate(((0, own_rows), (own_rows, all_rows))):
        perm, active, slope, ret = saved[slot]
        weight, wide = weight_of(slot, w, v), wide_weight(slot, w, e_ref, y)
        count = ndp * (hi - lo)
        tiles = (nb, BLK // nb, count)
        for m in range(nb):
            d = f ^ m
            x = x_ref[:, d, lo:hi, :].reshape(count, BLK)
            for r in range(2):
                spread = dot(weight(m, 0, r), x, 0, 1).astype(jnp.bfloat16)
                perm[r, :, d] = spread.reshape(tiles)
        for m in range(nb):
            s = f ^ m
            for r in range(2):
                p = perm[r, s].reshape(BLK, count)
                value, grade = gelu_pair(dot(weight(m, 1, r), p, 0, 0))
                value = value.astype(jnp.bfloat16)
                active[r, s] = value
                slope[r, s] = grade.astype(jnp.bfloat16)
                narrowed = dot(weight(m, 2, r), value, 0, 0).astype(jnp.bfloat16)
                ret[r, :, s] = narrowed.reshape(tiles)
        for m in range(nb):
            d = f ^ m
            total = 0.0
            for r in range(2):
                total = total + dot(ret[r, d].reshape(BLK, count), wide(m, r), 0, 0)
            out_ref[:, d, lo:hi, :] = total.astype(jnp.bfloat16).reshape(ndp, hi - lo, BLK)


class Streamed:
    def __init__(self, sources, targets, sems, order):
        self.targets, self.waiting = targets, {}
        for i in order:
            self.waiting[i] = pltpu.make_async_copy(sources[i], targets[i], sems.at[i])
            self.waiting[i].start()

    def get(self, i):
        if i in self.waiting:
            self.waiting.pop(i).wait()
        return self.targets[i]


class Lookup:
    def __init__(self, streamed, indices):
        self.streamed, self.indices = streamed, indices

    def __getitem__(self, at):
        return self.streamed.get(self.indices[at])


BACKWARD_ORDER = (
    (1, 6, 21, 7, 8, 9, 18, 19, 20, 2, 3, 4, 5, 0) + tuple(range(14, 18)) + (25,) + tuple(range(10, 14)) + (22, 23, 24)
)


def backward_kernel(seat_ref, *refs):
    count_in = len(BACKWARD_ORDER)
    sources, refs = refs[:count_in], refs[count_in:]
    results, refs = refs[:9], refs[9:]
    targets, refs = refs[:count_in], refs[count_in:]
    staged, refs = refs[:5], refs[5:]
    scratch, (e_ref, in_sems, out_sems) = (refs[:2], refs[2:4]), refs[4:]
    streamed = Streamed(sources, targets, in_sems, BACKWARD_ORDER)
    at = [Lookup(streamed, range(i, i + 4)) for i in range(2, 26, 4)]
    w, v, saved = at[:2], at[2:4], at[4:]
    gin_ref, own_keep, own_send, mid_keep, mid_send = staged
    sent = []

    def send(source, target):
        sent.append(pltpu.make_async_copy(source, target, out_sems.at[len(sent)]))
        sent[-1].start()

    ndp, nb, all_rows, _ = targets[0].shape
    own_rows = 2 * all_rows // 3
    rows = BLK // ndp
    f, y = seat_ref[0], seat_ref[1]

    def store(slot, m, which, r, part):
        ref = ((own_keep, own_send), (mid_keep, mid_send))[slot][m % 2]
        if slot == 0:
            ref[m // 2, :, r, which] = part.astype(jnp.bfloat16).reshape(ndp, rows, BLK)
        else:
            ref[r, m // 2, :, which] = part.astype(jnp.bfloat16).reshape(ndp, rows, BLK)

    def store_wide(slot, m, r, part):
        ref = ((own_keep, own_send), (mid_keep, mid_send))[slot][m % 2]
        part = part.astype(jnp.bfloat16).reshape(ndp // 2, 2, rows, BLK)
        if slot == 0:
            ref[m // 2, half_src(ndp, r), :, 3] = part
        else:
            ref[y, m // 2, half_src(ndp, r ^ y), 3] = part[:, 0]
            ref[1 - y, m // 2, half_src(ndp, r ^ y), 3] = part[:, 1]

    for slot, (lo, hi) in enumerate(((0, own_rows), (own_rows, all_rows))):
        perm, active, slope, ret = range(4)
        mid, spread = scratch[slot]
        if slot == 1:
            join_halves(v, e_ref, y)
        weight, wide = weight_of(slot, w, v), wide_weight(slot, w, e_ref, y)
        count = ndp * (hi - lo)
        tiles = (nb, BLK // nb, count)
        for m in range(nb):
            d = f ^ m
            g = streamed.get(1)[:, d, lo:hi, :].reshape(count, BLK)
            for r in range(2):
                mid[r, :, d] = dot(wide(m, r), g, 1, 1).astype(jnp.bfloat16).reshape(tiles)
                store_wide(slot, m, r, dot(saved[slot][ret][r, d].reshape(BLK, count), g, 1, 0))
        for m in range(nb):
            s = f ^ m
            for r in range(2):
                p = saved[slot][perm][r, s].reshape(BLK, count)
                back_mid = mid[r, s].reshape(BLK, count)
                back = dot(weight(m, 2, r), back_mid, 1, 0)
                back = (back * saved[slot][slope][r, s].astype(jnp.float32)).astype(jnp.bfloat16)
                store(slot, m, 2, r, dot(saved[slot][active][r, s], back_mid, 1, 1))
                store(slot, m, 1, r, dot(p, back, 1, 1))
                first = dot(weight(m, 1, r), back, 1, 0).astype(jnp.bfloat16)
                spread[r, :, s] = first.reshape(tiles)
        for m in range(nb):
            d = f ^ m
            x = streamed.get(0)[:, d, lo:hi, :].reshape(count, BLK)
            across = x.T
            total = 0.0
            for r in range(2):
                back = spread[r, d].reshape(BLK, count)
                total = total + dot(weight(m, 0, r), back, 1, 0)
                store(slot, m, 0, r, dot(across, back, 1, 1))
            gin_ref[:, d, lo:hi, :] = total.astype(jnp.bfloat16).T.reshape(ndp, hi - lo, BLK)
        if slot == 0:
            send(own_keep, results[1])
            send(own_send.at[0], results[2])
            send(own_send.at[1], results[3])
    send(mid_keep, results[4])
    for i in range(4):
        send(mid_send.at[i // 2, i % 2], results[5 + i])
    send(gin_ref, results[0])
    for copy in sent:
        copy.wait()


def pack_kernel(a_ref, b_ref, c_ref, e_ref, first_ref):
    owners, rows = first_ref.shape[0], b_ref.shape[1]

    def piece(which, index, part):
        if which == 0:
            return a_ref[index, :, part * BLK : (part + 1) * BLK]
        if which == 3:
            return e_ref[index, part * rows : (part + 1) * rows, :]
        return (b_ref, c_ref)[which - 1][2 * index + part]

    for owner in range(owners):
        pair, side = owner // 2, owner % 2
        for part in range(2):
            first_ref[owner, part] = piece(0, 3 * pair + 2 * side, part)
        for which in range(4):
            first_ref[owner, 2 + which] = piece(which, 3 * pair + 1, side)


def grads_kernel(got_ref, a_ref, b_ref, c_ref, e_ref):
    pairs = got_ref.shape[0] // 2
    rows = got_ref.shape[3]
    for which, ref in enumerate((a_ref, b_ref, c_ref, e_ref)):
        for place in range(6):
            owner, part = ((0, 0), (0, 1), (0, 2), (1, 2), (1, 0), (1, 1))[place]
            for i in range(pairs):
                value = got_ref[2 * i + owner, part, which].astype(jnp.float32)
                if which == 0:
                    ref[3 * i + place // 2, :, (place % 2) * BLK : (place % 2 + 1) * BLK] = value
                elif which == 3:
                    ref[3 * i + place // 2, (place % 2) * rows : (place % 2 + 1) * rows, :] = value
                else:
                    ref[6 * i + place] = value


def on_chip(kernel, products, outs, scratch, inputs, results=None):
    streamed = results is not None
    space = pl.ANY if streamed else pltpu.VMEM
    staged = [x.shape for x in inputs[1:]] + outs if streamed else []
    outs = results or outs
    sems = [pltpu.SemaphoreType.DMA((n,)) for n in (len(inputs) - 1, len(outs))]
    return pl.pallas_call(
        kernel,
        out_shape=[jax.ShapeDtypeStruct(shape, jnp.bfloat16) for shape in outs],
        in_specs=[pl.BlockSpec(memory_space=pltpu.SMEM)]
        + [pl.BlockSpec(memory_space=space)] * (len(inputs) - 1),
        out_specs=[pl.BlockSpec(memory_space=space)] * len(outs),
        scratch_shapes=[pltpu.VMEM(shape, jnp.bfloat16) for shape in staged + scratch]
        + (sems if streamed else []),
        cost_estimate=pl.CostEstimate(
            flops=products * 2 * BLK * BLK,
            transcendentals=0,
            bytes_accessed=sum(x.size for x in inputs) * 2 + sum(map(math.prod, outs)) * 2,
        ),
        compiler_params=pltpu.CompilerParams(vmem_limit_bytes=56 * 2**20),
    )(*inputs)


def token_plan(tokens, grad_out, weight_a, weight_b, weight_c, weight_e):
    ndp, nb = lax.axis_size("dp"), lax.axis_size("bfly")
    blocks, rows, _ = weight_a.shape
    parts, count = 2 * blocks, tokens.shape[0]
    seat = jnp.stack([lax.axis_index("bfly"), lax.axis_index("dp") % 2]).astype(jnp.int32)

    everyone = ("dp", "bfly")
    shape = (ndp, nb, -1, BLK)
    first = pl.pallas_call(
        pack_kernel, out_shape=jax.ShapeDtypeStruct((ndp, 6, rows, BLK), jnp.bfloat16)
    )(weight_a, weight_b, weight_c, weight_e)
    first = exchange(first, "dp")
    a, mid = first[:, :2], first[:, 2:]
    rest = [own_sets(w) for w in (weight_b, weight_c, weight_e.reshape(parts, rows, BLK))]
    rest = exchange(after(jnp.stack(rest, axis=2), first), "dp")
    mid_across, a_across, rest_across = (xor_permute(part, 2) for part in (mid, a, rest))
    swapped, swapped_across = (xor_permute(part, 1, "dp") for part in (mid, mid_across))
    x = exchange(after(deal_tokens(tokens), rest, mid_across, swapped, a_across), everyone)
    g = after(deal_tokens(grad_out), x, rest_across, swapped_across)
    g = exchange(g, everyone).reshape(shape)
    x = x.reshape(shape)
    weights = gather_bfly(a, a_across) + gather_bfly(rest, rest_across)
    weights += gather_bfly(mid, mid_across) + gather_bfly(swapped, swapped_across)

    own, mid = count * ndp // nb, count * ndp // nb // 2
    saved = []
    for t in (own, mid):
        tiled, whole = (2, nb, nb, BLK // nb, t), (2, nb, BLK, t)
        saved += [tiled, whole, whole, tiled]
    halves = (nb, ndp, 2, rows, BLK)
    products = 2 * nb * (own + mid)
    out, *kept = on_chip(
        forward_kernel, 4 * products, [x.shape] + saved, [halves], [seat, x] + weights
    )
    out = exchange(out.reshape(ndp * nb, -1, BLK), everyone)
    own_shape, mid_shape = (2, ndp, 2, 4, rows, BLK), (2, 2, ndp, 4, rows, BLK)
    gin, own_keep, *sends = on_chip(
        backward_kernel,
        8 * products,
        [x.shape, own_shape, own_shape, mid_shape, mid_shape],
        [saved[0], saved[0], saved[4], saved[4], halves],
        [seat, x, g] + weights + kept,
        [x.shape, own_shape] + [own_shape[1:]] * 2 + [mid_shape] + [mid_shape[2:]] * 4,
    )
    mid_keep = sends.pop(2)
    far = add(mid_keep[1, 1], xor_permute(sends[5], 1))
    own_far = add(own_keep[1], xor_permute(sends[1], 1))
    far = add(add(mid_keep[0, 1], xor_permute(sends[3], 1)), xor_permute(far, 1, "dp"))
    own_near = add(own_keep[0], xor_permute(sends[0], 1))
    near = add(mid_keep[1, 0], xor_permute(sends[4], 1))
    part = ndp // 2
    own_first = add(own_near[:part], xor_permute(own_far[:part], 2))
    gin = exchange(after(gin.reshape(ndp * nb, -1, BLK), out, far, own_first), everyone)
    own_last = add(own_near[part:], xor_permute(after(own_far[part:], own_first), 2))
    own = jnp.concatenate([own_first, own_last], axis=0)
    near = xor_permute(near, 1, "dp")
    near = add(add(mid_keep[0, 0], xor_permute(sends[2], 1)), near)
    mid = add(near, xor_permute(far, 2))
    dealt = jnp.concatenate([own, mid[:, None]], axis=1)
    got = exchange(after(dealt, gin), "dp")
    grads = pl.pallas_call(
        grads_kernel,
        out_shape=[
            jax.ShapeDtypeStruct(w.shape, jnp.float32)
            for w in (weight_a, weight_b, weight_c, weight_e)
        ],
    )(got)
    return (undeal_tokens(out, count), undeal_tokens(gin, count), *grads)


def per_device(tokens, grad_out, weight_a, weight_b, weight_c, weight_e):
    ndp, nb = lax.axis_size("dp"), lax.axis_size("bfly")
    fits = nb == 4 and ndp % 2 == 0 and 2 * weight_a.shape[0] == 3 * ndp
    fits = fits and tokens.shape[0] % (32 * nb) == 0 and weight_a.shape[1] * ndp == BLK
    fits = fits and weight_a.shape[2] == 2 * BLK and weight_e.shape[1] == 2 * weight_a.shape[1]
    plan = token_plan if fits else any_mesh
    return plan(tokens, grad_out, weight_a, weight_b, weight_c, weight_e)


def solution(mesh):
    in_specs = (P("dp", "bfly"),) * 2 + (P("bfly", "dp", None),) * 4
    return jax.shard_map(
        per_device, mesh=mesh, in_specs=in_specs, out_specs=in_specs, check_vma=False
    )
```

```python
import math

import jax
import jax.numpy as jnp
from jax import lax
from jax.experimental import pallas as pl
from jax.experimental.pallas import tpu as pltpu
from jax.sharding import PartitionSpec as P

BLK = 256

gelu_scale = 0.7978845608028654


def gelu_pair(hidden):
    inner_arg = gelu_scale * (hidden + 0.044715 * hidden * hidden * hidden)
    tangent = jnp.tanh(inner_arg)
    gelu_value = 0.5 * hidden * (1.0 + tangent)
    gelu_slope = 0.5 * (1.0 + tangent) + 0.5 * hidden * (1.0 - tangent * tangent) * gelu_scale * (
        1.0 + 3.0 * 0.044715 * hidden * hidden
    )
    return (gelu_value, gelu_slope)


def mm(spec, a, b):
    return jnp.einsum(spec, a, b, preferred_element_type=jnp.float32)


def regroup(piece, group_count):
    local_blocks, block_width, token_count = piece.shape
    stacked = piece.reshape(local_blocks, group_count, block_width // group_count, token_count)
    arrived = lax.all_to_all(stacked, "bfly", split_axis=1, concat_axis=1, tiled=True)
    return arrived.reshape(local_blocks, block_width, token_count)


def any_mesh(tokens, grad_out, weight_a, weight_b, weight_c, weight_e):
    group_count = lax.axis_size("bfly")
    full_a, full_b, full_c, full_e = (
        lax.all_gather(w, "dp", axis=1, tiled=True)
        for w in (weight_a, weight_b, weight_c, weight_e)
    )
    token_count = tokens.shape[0]
    inner_blocks = full_a.shape[0]
    spread_width = full_a.shape[2]
    local_blocks = full_b.shape[0]
    inputs = tokens.reshape(token_count, inner_blocks, BLK).transpose(1, 2, 0)
    upstream = grad_out.reshape(token_count, inner_blocks, BLK).transpose(1, 2, 0)
    hidden_view = (local_blocks, BLK, token_count)
    wide_view = (inner_blocks, spread_width, token_count)
    spread = mm("kit,kio->kot", inputs, full_a).astype(jnp.bfloat16).reshape(hidden_view)
    back_out = mm("kjt,koj->kot", upstream, full_e).astype(jnp.bfloat16).reshape(hidden_view)
    permuted = regroup(spread, group_count)
    back_mid = regroup(back_out, group_count)
    gelu_value, gelu_slope = gelu_pair(mm("qit,qij->qjt", permuted, full_b))
    active = gelu_value.astype(jnp.bfloat16)
    narrowed = mm("qit,qij->qjt", active, full_c).astype(jnp.bfloat16)
    back_hidden = (mm("qjt,qij->qit", back_mid, full_c) * gelu_slope).astype(jnp.bfloat16)
    back_first = mm("qjt,qij->qit", back_hidden, full_b).astype(jnp.bfloat16)
    returned = regroup(narrowed, group_count).reshape(wide_view)
    back_spread = regroup(back_first, group_count).reshape(wide_view)
    output = mm("kot,koj->kjt", returned, full_e)
    back_input = mm("kot,kio->kit", back_spread, full_a)
    parts = (
        mm("kit,kot->kio", inputs, back_spread),
        mm("qit,qjt->qij", permuted, back_hidden),
        mm("qit,qjt->qij", active, back_mid),
        mm("kot,kjt->koj", returned, upstream),
    )
    grads = tuple(
        lax.psum_scatter(part.astype(jnp.bfloat16), "dp", scatter_dimension=1, tiled=True).astype(
            jnp.float32
        )
        for part in parts
    )

    def rows(x):
        return x.astype(jnp.bfloat16).transpose(2, 0, 1).reshape(token_count, inner_blocks * BLK)

    return (rows(output), rows(back_input)) + grads


def xor_permute(x, mask, axis="bfly"):
    return lax.ppermute(x, axis, [(i, i ^ mask) for i in range(lax.axis_size(axis))])


def exchange(x, axes):
    return lax.all_to_all(x, axes, split_axis=0, concat_axis=0, tiled=True)


def own_sets(w):
    pairs = lax.axis_size("dp") // 2
    sets = w.reshape(pairs, 3, 2, w.shape[1], w.shape[2])
    own = jnp.stack([sets[:, 0], sets[:, 2]], axis=1)
    return own.reshape((pairs * 2,) + own.shape[2:])


def gather_bfly(w, across):
    return [w, xor_permute(w, 1), across, xor_permute(across, 1)]


def after(x, *earlier):
    return lax.optimization_barrier((x,) + earlier)[0]


def add(x, y):
    return (x.astype(jnp.float32) + y.astype(jnp.float32)).astype(jnp.bfloat16)


def deal_tokens(x):
    ndp, nb = lax.axis_size("dp"), lax.axis_size("bfly")
    pairs, count = ndp // 2, x.shape[0]
    view = x.reshape(count, pairs, 3, BLK)
    own = view[:, :, 0::2].reshape(nb, count // nb, ndp, BLK).transpose(2, 0, 1, 3)
    mid = view[:, :, 1].reshape(2, nb, count // nb // 2, pairs, BLK).transpose(3, 0, 1, 2, 4)
    mid = mid.reshape(ndp, nb, count // nb // 2, BLK)
    return jnp.concatenate([own, mid], axis=2).reshape(ndp * nb, -1, BLK)


def undeal_tokens(got, count):
    ndp, nb = lax.axis_size("dp"), lax.axis_size("bfly")
    pairs, own_count = ndp // 2, count // nb
    own = got[:, :own_count].reshape(pairs, 2, count, BLK)
    mid = got[:, own_count:].reshape(pairs, 1, count, BLK)
    sets = jnp.concatenate([own[:, :1], mid, own[:, 1:]], axis=1)
    return sets.transpose(2, 0, 1, 3).reshape(count, pairs * 3 * BLK)


def dot(x, y, contract_x, contract_y):
    dims = (((contract_x,), (contract_y,)), ((), ()))
    return lax.dot_general(x, y, dims, preferred_element_type=jnp.float32)


def square(x):
    return x.reshape(BLK, BLK)


def half_src(part, r):
    return pl.ds(r * (part // 2), part // 2)


def weight_of(slot, own, shared):
    def get(m, which, r):
        if slot == 0:
            return square(own[1][m][:, r, which - 1] if which else own[0][m][:, r])
        return square(shared[r][m][:, which])

    return get


def wide_weight(slot, own, e_ref, y):
    def get(m, r):
        if slot == 0:
            return square(own[1][m][half_src(e_ref.shape[1], r), :, 2])
        return square(e_ref[m, half_src(e_ref.shape[1], r ^ y)])

    return get


def join_halves(shared, e_ref, y):
    for m in range(4):
        e_ref[m, :, y] = shared[0][m][:, 3]
        e_ref[m, :, 1 - y] = shared[1][m][:, 3]


def weight_refs(refs):
    return (refs[:4], refs[4:8]), (refs[8:12], refs[12:16]), refs[16:]


def forward_kernel(seat_ref, x_ref, *refs):
    w, v, (out_ref, *refs) = weight_refs(refs)
    saved, e_ref = (refs[:4], refs[4:8]), refs[8]
    ndp, nb, all_rows, _ = x_ref.shape
    own_rows = 2 * all_rows // 3
    f, y = seat_ref[0], seat_ref[1]
    join_halves(v, e_ref, y)
    for slot, (lo, hi) in enumerate(((0, own_rows), (own_rows, all_rows))):
        perm, active, slope, ret = saved[slot]
        weight, wide = weight_of(slot, w, v), wide_weight(slot, w, e_ref, y)
        count = ndp * (hi - lo)
        tiles = (nb, BLK // nb, count)
        for m in range(nb):
            d = f ^ m
            x = x_ref[:, d, lo:hi, :].reshape(count, BLK)
            for r in range(2):
                spread = dot(weight(m, 0, r), x, 0, 1).astype(jnp.bfloat16)
                perm[r, :, d] = spread.reshape(tiles)
        for m in range(nb):
            s = f ^ m
            for r in range(2):
                p = perm[r, s].reshape(BLK, count)
                value, grade = gelu_pair(dot(weight(m, 1, r), p, 0, 0))
                value = value.astype(jnp.bfloat16)
                active[r, s] = value
                slope[r, s] = grade.astype(jnp.bfloat16)
                narrowed = dot(weight(m, 2, r), value, 0, 0).astype(jnp.bfloat16)
                ret[r, :, s] = narrowed.reshape(tiles)
        for m in range(nb):
            d = f ^ m
            total = 0.0
            for r in range(2):
                total = total + dot(ret[r, d].reshape(BLK, count), wide(m, r), 0, 0)
            out_ref[:, d, lo:hi, :] = total.astype(jnp.bfloat16).reshape(ndp, hi - lo, BLK)


class Streamed:
    def __init__(self, sources, targets, sems, order):
        self.targets, self.waiting = targets, {}
        for i in order:
            self.waiting[i] = pltpu.make_async_copy(sources[i], targets[i], sems.at[i])
            self.waiting[i].start()

    def get(self, i):
        if i in self.waiting:
            self.waiting.pop(i).wait()
        return self.targets[i]


class Lookup:
    def __init__(self, streamed, indices):
        self.streamed, self.indices = streamed, indices

    def __getitem__(self, at):
        return self.streamed.get(self.indices[at])


BACKWARD_ORDER = (
    (1, 6, 21, 7, 8, 9, 18, 19, 20, 2, 3, 4, 5, 0) + tuple(range(14, 18)) + (25,) + tuple(range(10, 14)) + (22, 23, 24)
)


def backward_kernel(seat_ref, *refs):
    count_in = len(BACKWARD_ORDER)
    sources, refs = refs[:count_in], refs[count_in:]
    results, refs = refs[:9], refs[9:]
    targets, refs = refs[:count_in], refs[count_in:]
    staged, refs = refs[:5], refs[5:]
    scratch, (e_ref, in_sems, out_sems) = (refs[:2], refs[2:4]), refs[4:]
    streamed = Streamed(sources, targets, in_sems, BACKWARD_ORDER)
    at = [Lookup(streamed, range(i, i + 4)) for i in range(2, 26, 4)]
    w, v, saved = at[:2], at[2:4], at[4:]
    gin_ref, own_keep, own_send, mid_keep, mid_send = staged
    sent = []

    def send(source, target):
        sent.append(pltpu.make_async_copy(source, target, out_sems.at[len(sent)]))
        sent[-1].start()

    ndp, nb, all_rows, _ = targets[0].shape
    own_rows = 2 * all_rows // 3
    rows = BLK // ndp
    f, y = seat_ref[0], seat_ref[1]

    def store(slot, m, which, r, part):
        ref = ((own_keep, own_send), (mid_keep, mid_send))[slot][m % 2]
        if slot == 0:
            ref[m // 2, :, r, which] = part.astype(jnp.bfloat16).reshape(ndp, rows, BLK)
        else:
            ref[r, m // 2, :, which] = part.astype(jnp.bfloat16).reshape(ndp, rows, BLK)

    def store_wide(slot, m, r, part):
        ref = ((own_keep, own_send), (mid_keep, mid_send))[slot][m % 2]
        part = part.astype(jnp.bfloat16).reshape(ndp // 2, 2, rows, BLK)
        if slot == 0:
            ref[m // 2, half_src(ndp, r), :, 3] = part
        else:
            ref[y, m // 2, half_src(ndp, r ^ y), 3] = part[:, 0]
            ref[1 - y, m // 2, half_src(ndp, r ^ y), 3] = part[:, 1]

    for slot, (lo, hi) in enumerate(((0, own_rows), (own_rows, all_rows))):
        perm, active, slope, ret = range(4)
        mid, spread = scratch[slot]
        if slot == 1:
            join_halves(v, e_ref, y)
        weight, wide = weight_of(slot, w, v), wide_weight(slot, w, e_ref, y)
        count = ndp * (hi - lo)
        tiles = (nb, BLK // nb, count)
        for m in range(nb):
            d = f ^ m
            g = streamed.get(1)[:, d, lo:hi, :].reshape(count, BLK)
            for r in range(2):
                mid[r, :, d] = dot(wide(m, r), g, 1, 1).astype(jnp.bfloat16).reshape(tiles)
                store_wide(slot, m, r, dot(saved[slot][ret][r, d].reshape(BLK, count), g, 1, 0))
        for m in range(nb):
            s = f ^ m
            for r in range(2):
                p = saved[slot][perm][r, s].reshape(BLK, count)
                back_mid = mid[r, s].reshape(BLK, count)
                back = dot(weight(m, 2, r), back_mid, 1, 0)
                back = (back * saved[slot][slope][r, s].astype(jnp.float32)).astype(jnp.bfloat16)
                store(slot, m, 2, r, dot(saved[slot][active][r, s], back_mid, 1, 1))
                store(slot, m, 1, r, dot(p, back, 1, 1))
                first = dot(weight(m, 1, r), back, 1, 0).astype(jnp.bfloat16)
                spread[r, :, s] = first.reshape(tiles)
        for m in range(nb):
            d = f ^ m
            x = streamed.get(0)[:, d, lo:hi, :].reshape(count, BLK)
            across = x.T
            total = 0.0
            for r in range(2):
                back = spread[r, d].reshape(BLK, count)
                total = total + dot(weight(m, 0, r), back, 1, 0)
                store(slot, m, 0, r, dot(across, back, 1, 1))
            gin_ref[:, d, lo:hi, :] = total.astype(jnp.bfloat16).T.reshape(ndp, hi - lo, BLK)
        if slot == 0:
            send(own_keep, results[1])
            send(own_send.at[0], results[2])
            send(own_send.at[1], results[3])
    send(mid_keep, results[4])
    for i in range(4):
        send(mid_send.at[i // 2, i % 2], results[5 + i])
    send(gin_ref, results[0])
    for copy in sent:
        copy.wait()


def pack_kernel(a_ref, b_ref, c_ref, e_ref, first_ref):
    owners, rows = first_ref.shape[0], b_ref.shape[1]

    def piece(which, index, part):
        if which == 0:
            return a_ref[index, :, part * BLK : (part + 1) * BLK]
        if which == 3:
            return e_ref[index, part * rows : (part + 1) * rows, :]
        return (b_ref, c_ref)[which - 1][2 * index + part]

    for owner in range(owners):
        pair, side = owner // 2, owner % 2
        for part in range(2):
            first_ref[owner, part] = piece(0, 3 * pair + 2 * side, part)
        for which in range(4):
            first_ref[owner, 2 + which] = piece(which, 3 * pair + 1, side)


def grads_kernel(got_ref, a_ref, b_ref, c_ref, e_ref):
    pairs = got_ref.shape[0] // 2
    rows = got_ref.shape[3]
    for which, ref in enumerate((a_ref, b_ref, c_ref, e_ref)):
        for place in range(6):
            owner, part = ((0, 0), (0, 1), (0, 2), (1, 2), (1, 0), (1, 1))[place]
            for i in range(pairs):
                value = got_ref[2 * i + owner, part, which].astype(jnp.float32)
                if which == 0:
                    ref[3 * i + place // 2, :, (place % 2) * BLK : (place % 2 + 1) * BLK] = value
                elif which == 3:
                    ref[3 * i + place // 2, (place % 2) * rows : (place % 2 + 1) * rows, :] = value
                else:
                    ref[6 * i + place] = value


def on_chip(kernel, products, outs, scratch, inputs, results=None):
    streamed = results is not None
    space = pl.ANY if streamed else pltpu.VMEM
    staged = [x.shape for x in inputs[1:]] + outs if streamed else []
    outs = results or outs
    sems = [pltpu.SemaphoreType.DMA((n,)) for n in (len(inputs) - 1, len(outs))]
    return pl.pallas_call(
        kernel,
        out_shape=[jax.ShapeDtypeStruct(shape, jnp.bfloat16) for shape in outs],
        in_specs=[pl.BlockSpec(memory_space=pltpu.SMEM)]
        + [pl.BlockSpec(memory_space=space)] * (len(inputs) - 1),
        out_specs=[pl.BlockSpec(memory_space=space)] * len(outs),
        scratch_shapes=[pltpu.VMEM(shape, jnp.bfloat16) for shape in staged + scratch]
        + (sems if streamed else []),
        cost_estimate=pl.CostEstimate(
            flops=products * 2 * BLK * BLK,
            transcendentals=0,
            bytes_accessed=sum(x.size for x in inputs) * 2 + sum(map(math.prod, outs)) * 2,
        ),
        compiler_params=pltpu.CompilerParams(vmem_limit_bytes=56 * 2**20),
    )(*inputs)


def token_plan(tokens, grad_out, weight_a, weight_b, weight_c, weight_e):
    ndp, nb = lax.axis_size("dp"), lax.axis_size("bfly")
    blocks, rows, _ = weight_a.shape
    parts, count = 2 * blocks, tokens.shape[0]
    seat = jnp.stack([lax.axis_index("bfly"), lax.axis_index("dp") % 2]).astype(jnp.int32)

    everyone = ("dp", "bfly")
    shape = (ndp, nb, -1, BLK)
    first = pl.pallas_call(
        pack_kernel, out_shape=jax.ShapeDtypeStruct((ndp, 6, rows, BLK), jnp.bfloat16)
    )(weight_a, weight_b, weight_c, weight_e)
    first = exchange(first, "dp")
    a, mid = first[:, :2], first[:, 2:]
    rest = [own_sets(w) for w in (weight_b, weight_c, weight_e.reshape(parts, rows, BLK))]
    rest = exchange(after(jnp.stack(rest, axis=2), first), "dp")
    mid_across, a_across, rest_across = (xor_permute(part, 2) for part in (mid, a, rest))
    swapped, swapped_across = (xor_permute(part, 1, "dp") for part in (mid, mid_across))
    x = exchange(after(deal_tokens(tokens), rest, mid_across, swapped, a_across), everyone)
    g = after(deal_tokens(grad_out), x, rest_across, swapped_across)
    g = exchange(g, everyone).reshape(shape)
    x = x.reshape(shape)
    weights = gather_bfly(a, a_across) + gather_bfly(rest, rest_across)
    weights += gather_bfly(mid, mid_across) + gather_bfly(swapped, swapped_across)

    own, mid = count * ndp // nb, count * ndp // nb // 2
    saved = []
    for t in (own, mid):
        tiled, whole = (2, nb, nb, BLK // nb, t), (2, nb, BLK, t)
        saved += [tiled, whole, whole, tiled]
    halves = (nb, ndp, 2, rows, BLK)
    products = 2 * nb * (own + mid)
    out, *kept = on_chip(
        forward_kernel, 4 * products, [x.shape] + saved, [halves], [seat, x] + weights
    )
    out = exchange(out.reshape(ndp * nb, -1, BLK), everyone)
    own_shape, mid_shape = (2, ndp, 2, 4, rows, BLK), (2, 2, ndp, 4, rows, BLK)
    gin, own_keep, *sends = on_chip(
        backward_kernel,
        8 * products,
        [x.shape, own_shape, own_shape, mid_shape, mid_shape],
        [saved[0], saved[0], saved[4], saved[4], halves],
        [seat, x, g] + weights + kept,
        [x.shape, own_shape] + [own_shape[1:]] * 2 + [mid_shape] + [mid_shape[2:]] * 4,
    )
    mid_keep = sends.pop(2)
    own_sends, mid_sends = sends[:2], sends[2:]
    own_far = add(own_keep[1], xor_permute(own_sends[1], 1))
    own_near = add(own_keep[0], xor_permute(own_sends[0], 1))
    there = add(mid_keep[1, 1], after(xor_permute(mid_sends[3], 1), own_far))
    here = add(mid_keep[0, 1], xor_permute(mid_sends[1], 1))
    near = add(mid_keep[1, 0], xor_permute(mid_sends[2], 1))
    part, half = 3 * ndp // 8, ndp // 2
    own_first = add(own_near[:part], xor_permute(own_far[:part], 2))
    far_first = add(here[:half], xor_permute(there[:half], 1, "dp"))
    gin = after(gin.reshape(ndp * nb, -1, BLK), out, far_first, own_first)
    gin = exchange(gin, everyone)
    own_last = add(own_near[part:], xor_permute(after(own_far[part:], own_first), 2))
    own = jnp.concatenate([own_first, own_last], axis=0)
    far_last = xor_permute(after(there[half:], far_first), 1, "dp")
    far_last = add(here[half:], far_last)
    far = jnp.concatenate([xor_permute(far_first, 2), xor_permute(far_last, 2)], axis=0)
    near = add(add(mid_keep[0, 0], xor_permute(mid_sends[0], 1)), xor_permute(near, 1, "dp"))
    mid = add(near, far)
    dealt = jnp.concatenate([own, mid[:, None]], axis=1)
    got = exchange(after(dealt, gin), "dp")
    grads = pl.pallas_call(
        grads_kernel,
        out_shape=[
            jax.ShapeDtypeStruct(w.shape, jnp.float32)
            for w in (weight_a, weight_b, weight_c, weight_e)
        ],
    )(got)
    return (undeal_tokens(out, count), undeal_tokens(gin, count), *grads)


def per_device(tokens, grad_out, weight_a, weight_b, weight_c, weight_e):
    ndp, nb = lax.axis_size("dp"), lax.axis_size("bfly")
    fits = nb == 4 and ndp % 2 == 0 and 2 * weight_a.shape[0] == 3 * ndp
    fits = fits and tokens.shape[0] % (32 * nb) == 0 and weight_a.shape[1] * ndp == BLK
    fits = fits and weight_a.shape[2] == 2 * BLK and weight_e.shape[1] == 2 * weight_a.shape[1]
    plan = token_plan if fits else any_mesh
    return plan(tokens, grad_out, weight_a, weight_b, weight_c, weight_e)


def solution(mesh):
    in_specs = (P("dp", "bfly"),) * 2 + (P("bfly", "dp", None),) * 4
    return jax.shard_map(
        per_device, mesh=mesh, in_specs=in_specs, out_specs=in_specs, check_vma=False
    )
```

```python
import math

import jax
import jax.numpy as jnp
from jax import lax
from jax.experimental import pallas as pl
from jax.experimental.pallas import tpu as pltpu
from jax.sharding import PartitionSpec as P

BLK = 256

gelu_scale = 0.7978845608028654


def gelu_pair(hidden):
    inner_arg = gelu_scale * (hidden + 0.044715 * hidden * hidden * hidden)
    tangent = jnp.tanh(inner_arg)
    gelu_value = 0.5 * hidden * (1.0 + tangent)
    gelu_slope = 0.5 * (1.0 + tangent) + 0.5 * hidden * (1.0 - tangent * tangent) * gelu_scale * (
        1.0 + 3.0 * 0.044715 * hidden * hidden
    )
    return (gelu_value, gelu_slope)


def mm(spec, a, b):
    return jnp.einsum(spec, a, b, preferred_element_type=jnp.float32)


def regroup(piece, group_count):
    local_blocks, block_width, token_count = piece.shape
    stacked = piece.reshape(local_blocks, group_count, block_width // group_count, token_count)
    arrived = lax.all_to_all(stacked, "bfly", split_axis=1, concat_axis=1, tiled=True)
    return arrived.reshape(local_blocks, block_width, token_count)


def any_mesh(tokens, grad_out, weight_a, weight_b, weight_c, weight_e):
    group_count = lax.axis_size("bfly")
    full_a, full_b, full_c, full_e = (
        lax.all_gather(w, "dp", axis=1, tiled=True)
        for w in (weight_a, weight_b, weight_c, weight_e)
    )
    token_count = tokens.shape[0]
    inner_blocks = full_a.shape[0]
    spread_width = full_a.shape[2]
    local_blocks = full_b.shape[0]
    inputs = tokens.reshape(token_count, inner_blocks, BLK).transpose(1, 2, 0)
    upstream = grad_out.reshape(token_count, inner_blocks, BLK).transpose(1, 2, 0)
    hidden_view = (local_blocks, BLK, token_count)
    wide_view = (inner_blocks, spread_width, token_count)
    spread = mm("kit,kio->kot", inputs, full_a).astype(jnp.bfloat16).reshape(hidden_view)
    back_out = mm("kjt,koj->kot", upstream, full_e).astype(jnp.bfloat16).reshape(hidden_view)
    permuted = regroup(spread, group_count)
    back_mid = regroup(back_out, group_count)
    gelu_value, gelu_slope = gelu_pair(mm("qit,qij->qjt", permuted, full_b))
    active = gelu_value.astype(jnp.bfloat16)
    narrowed = mm("qit,qij->qjt", active, full_c).astype(jnp.bfloat16)
    back_hidden = (mm("qjt,qij->qit", back_mid, full_c) * gelu_slope).astype(jnp.bfloat16)
    back_first = mm("qjt,qij->qit", back_hidden, full_b).astype(jnp.bfloat16)
    returned = regroup(narrowed, group_count).reshape(wide_view)
    back_spread = regroup(back_first, group_count).reshape(wide_view)
    output = mm("kot,koj->kjt", returned, full_e)
    back_input = mm("kot,kio->kit", back_spread, full_a)
    parts = (
        mm("kit,kot->kio", inputs, back_spread),
        mm("qit,qjt->qij", permuted, back_hidden),
        mm("qit,qjt->qij", active, back_mid),
        mm("kot,kjt->koj", returned, upstream),
    )
    grads = tuple(
        lax.psum_scatter(part.astype(jnp.bfloat16), "dp", scatter_dimension=1, tiled=True).astype(
            jnp.float32
        )
        for part in parts
    )

    def rows(x):
        return x.astype(jnp.bfloat16).transpose(2, 0, 1).reshape(token_count, inner_blocks * BLK)

    return (rows(output), rows(back_input)) + grads


def xor_permute(x, mask, axis="bfly"):
    return lax.ppermute(x, axis, [(i, i ^ mask) for i in range(lax.axis_size(axis))])


def exchange(x, axes):
    return lax.all_to_all(x, axes, split_axis=0, concat_axis=0, tiled=True)


def own_sets(w):
    pairs = lax.axis_size("dp") // 2
    sets = w.reshape(pairs, 3, 2, w.shape[1], w.shape[2])
    own = jnp.stack([sets[:, 0], sets[:, 2]], axis=1)
    return own.reshape((pairs * 2,) + own.shape[2:])


def gather_bfly(w, across):
    return [w, xor_permute(w, 1), across, xor_permute(across, 1)]


def after(x, *earlier):
    return lax.optimization_barrier((x,) + earlier)[0]


def add(x, y):
    return (x.astype(jnp.float32) + y.astype(jnp.float32)).astype(jnp.bfloat16)


def deal_tokens(x):
    ndp, nb = lax.axis_size("dp"), lax.axis_size("bfly")
    pairs, count = ndp // 2, x.shape[0]
    view = x.reshape(count, pairs, 3, BLK)
    own = view[:, :, 0::2].reshape(nb, count // nb, ndp, BLK).transpose(2, 0, 1, 3)
    mid = view[:, :, 1].reshape(2, nb, count // nb // 2, pairs, BLK).transpose(3, 0, 1, 2, 4)
    mid = mid.reshape(ndp, nb, count // nb // 2, BLK)
    return jnp.concatenate([own, mid], axis=2).reshape(ndp * nb, -1, BLK)


def undeal_tokens(got, count):
    ndp, nb = lax.axis_size("dp"), lax.axis_size("bfly")
    pairs, own_count = ndp // 2, count // nb
    own = got[:, :own_count].reshape(pairs, 2, count, BLK)
    mid = got[:, own_count:].reshape(pairs, 1, count, BLK)
    sets = jnp.concatenate([own[:, :1], mid, own[:, 1:]], axis=1)
    return sets.transpose(2, 0, 1, 3).reshape(count, pairs * 3 * BLK)


def dot(x, y, contract_x, contract_y):
    dims = (((contract_x,), (contract_y,)), ((), ()))
    return lax.dot_general(x, y, dims, preferred_element_type=jnp.float32)


def square(x):
    return x.reshape(BLK, BLK)


def half_src(part, r):
    return pl.ds(r * (part // 2), part // 2)


def weight_of(slot, own, shared):
    def get(m, which, r):
        if slot == 0:
            return square(own[1][m][:, r, which - 1] if which else own[0][m][:, r])
        return square(shared[r][m][:, which])

    return get


def wide_weight(slot, own, e_ref, y):
    def get(m, r):
        if slot == 0:
            return square(own[1][m][half_src(e_ref.shape[1], r), :, 2])
        return square(e_ref[m, half_src(e_ref.shape[1], r ^ y)])

    return get


def join_halves(shared, e_ref, y):
    for m in range(4):
        e_ref[m, :, y] = shared[0][m][:, 3]
        e_ref[m, :, 1 - y] = shared[1][m][:, 3]


def weight_refs(refs):
    return (refs[:4], refs[4:8]), (refs[8:12], refs[12:16]), refs[16:]


def forward_kernel(seat_ref, x_ref, *refs):
    w, v, (out_ref, *refs) = weight_refs(refs)
    saved, e_ref = (refs[:4], refs[4:8]), refs[8]
    ndp, nb, all_rows, _ = x_ref.shape
    own_rows = 2 * all_rows // 3
    f, y = seat_ref[0], seat_ref[1]
    join_halves(v, e_ref, y)
    for slot, (lo, hi) in enumerate(((0, own_rows), (own_rows, all_rows))):
        perm, active, slope, ret = saved[slot]
        weight, wide = weight_of(slot, w, v), wide_weight(slot, w, e_ref, y)
        count = ndp * (hi - lo)
        tiles = (nb, BLK // nb, count)
        for m in range(nb):
            d = f ^ m
            x = x_ref[:, d, lo:hi, :].reshape(count, BLK)
            for r in range(2):
                spread = dot(weight(m, 0, r), x, 0, 1).astype(jnp.bfloat16)
                perm[r, :, d] = spread.reshape(tiles)
        for m in range(nb):
            s = f ^ m
            for r in range(2):
                p = perm[r, s].reshape(BLK, count)
                value, grade = gelu_pair(dot(weight(m, 1, r), p, 0, 0))
                value = value.astype(jnp.bfloat16)
                active[r, s] = value
                slope[r, s] = grade.astype(jnp.bfloat16)
                narrowed = dot(weight(m, 2, r), value, 0, 0).astype(jnp.bfloat16)
                ret[r, :, s] = narrowed.reshape(tiles)
        for m in range(nb):
            d = f ^ m
            total = 0.0
            for r in range(2):
                total = total + dot(ret[r, d].reshape(BLK, count), wide(m, r), 0, 0)
            out_ref[:, d, lo:hi, :] = total.astype(jnp.bfloat16).reshape(ndp, hi - lo, BLK)


class Streamed:
    def __init__(self, sources, targets, sems, order):
        self.targets, self.waiting = targets, {}
        for i in order:
            self.waiting[i] = pltpu.make_async_copy(sources[i], targets[i], sems.at[i])
            self.waiting[i].start()

    def get(self, i):
        if i in self.waiting:
            self.waiting.pop(i).wait()
        return self.targets[i]


class Lookup:
    def __init__(self, streamed, indices):
        self.streamed, self.indices = streamed, indices

    def __getitem__(self, at):
        return self.streamed.get(self.indices[at])


BACKWARD_ORDER = (
    (1, 6, 21, 7, 8, 9, 18, 19, 20, 2, 3, 4, 5, 0) + tuple(range(14, 18)) + (25,) + tuple(range(10, 14)) + (22, 23, 24)
)


def backward_kernel(seat_ref, *refs):
    count_in = len(BACKWARD_ORDER)
    sources, refs = refs[:count_in], refs[count_in:]
    results, refs = refs[:9], refs[9:]
    targets, refs = refs[:count_in], refs[count_in:]
    staged, refs = refs[:5], refs[5:]
    scratch, (e_ref, in_sems, out_sems) = (refs[:2], refs[2:4]), refs[4:]
    streamed = Streamed(sources, targets, in_sems, BACKWARD_ORDER)
    at = [Lookup(streamed, range(i, i + 4)) for i in range(2, 26, 4)]
    w, v, saved = at[:2], at[2:4], at[4:]
    gin_ref, own_keep, own_send, mid_keep, mid_send = staged
    sent = []

    def send(source, target):
        sent.append(pltpu.make_async_copy(source, target, out_sems.at[len(sent)]))
        sent[-1].start()

    ndp, nb, all_rows, _ = targets[0].shape
    own_rows = 2 * all_rows // 3
    rows = BLK // ndp
    f, y = seat_ref[0], seat_ref[1]

    def store(slot, m, which, r, part):
        ref = ((own_keep, own_send), (mid_keep, mid_send))[slot][m % 2]
        if slot == 0:
            ref[m // 2, :, r, which] = part.astype(jnp.bfloat16).reshape(ndp, rows, BLK)
        else:
            ref[r, m // 2, :, which] = part.astype(jnp.bfloat16).reshape(ndp, rows, BLK)

    def store_wide(slot, m, r, part):
        ref = ((own_keep, own_send), (mid_keep, mid_send))[slot][m % 2]
        part = part.astype(jnp.bfloat16).reshape(ndp // 2, 2, rows, BLK)
        if slot == 0:
            ref[m // 2, half_src(ndp, r), :, 3] = part
        else:
            ref[y, m // 2, half_src(ndp, r ^ y), 3] = part[:, 0]
            ref[1 - y, m // 2, half_src(ndp, r ^ y), 3] = part[:, 1]

    for slot, (lo, hi) in enumerate(((0, own_rows), (own_rows, all_rows))):
        perm, active, slope, ret = range(4)
        mid, spread = scratch[slot]
        if slot == 1:
            join_halves(v, e_ref, y)
        weight, wide = weight_of(slot, w, v), wide_weight(slot, w, e_ref, y)
        count = ndp * (hi - lo)
        tiles = (nb, BLK // nb, count)
        for m in range(nb):
            d = f ^ m
            g = streamed.get(1)[:, d, lo:hi, :].reshape(count, BLK)
            for r in range(2):
                mid[r, :, d] = dot(wide(m, r), g, 1, 1).astype(jnp.bfloat16).reshape(tiles)
                store_wide(slot, m, r, dot(saved[slot][ret][r, d].reshape(BLK, count), g, 1, 0))
        for m in range(nb):
            s = f ^ m
            for r in range(2):
                p = saved[slot][perm][r, s].reshape(BLK, count)
                back_mid = mid[r, s].reshape(BLK, count)
                back = dot(weight(m, 2, r), back_mid, 1, 0)
                back = (back * saved[slot][slope][r, s].astype(jnp.float32)).astype(jnp.bfloat16)
                store(slot, m, 2, r, dot(saved[slot][active][r, s], back_mid, 1, 1))
                store(slot, m, 1, r, dot(p, back, 1, 1))
                first = dot(weight(m, 1, r), back, 1, 0).astype(jnp.bfloat16)
                spread[r, :, s] = first.reshape(tiles)
        for m in range(nb):
            d = f ^ m
            x = streamed.get(0)[:, d, lo:hi, :].reshape(count, BLK)
            across = x.T
            total = 0.0
            for r in range(2):
                back = spread[r, d].reshape(BLK, count)
                total = total + dot(weight(m, 0, r), back, 1, 0)
                store(slot, m, 0, r, dot(across, back, 1, 1))
            gin_ref[:, d, lo:hi, :] = total.astype(jnp.bfloat16).T.reshape(ndp, hi - lo, BLK)
        if slot == 0:
            send(own_keep, results[1])
            send(own_send.at[0], results[2])
            send(own_send.at[1], results[3])
    send(mid_keep, results[4])
    for i in range(4):
        send(mid_send.at[i // 2, i % 2], results[5 + i])
    send(gin_ref, results[0])
    for copy in sent:
        copy.wait()


def pack_kernel(a_ref, b_ref, c_ref, e_ref, first_ref):
    owners, rows = first_ref.shape[0], b_ref.shape[1]

    def piece(which, index, part):
        if which == 0:
            return a_ref[index, :, part * BLK : (part + 1) * BLK]
        if which == 3:
            return e_ref[index, part * rows : (part + 1) * rows, :]
        return (b_ref, c_ref)[which - 1][2 * index + part]

    for owner in range(owners):
        pair, side = owner // 2, owner % 2
        for part in range(2):
            first_ref[owner, part] = piece(0, 3 * pair + 2 * side, part)
        for which in range(4):
            first_ref[owner, 2 + which] = piece(which, 3 * pair + 1, side)


def grads_kernel(got_ref, a_ref, b_ref, c_ref, e_ref):
    pairs = got_ref.shape[0] // 2
    rows = got_ref.shape[3]
    for which, ref in enumerate((a_ref, b_ref, c_ref, e_ref)):
        for place in range(6):
            owner, part = ((0, 0), (0, 1), (0, 2), (1, 2), (1, 0), (1, 1))[place]
            for i in range(pairs):
                value = got_ref[2 * i + owner, part, which].astype(jnp.float32)
                if which == 0:
                    ref[3 * i + place // 2, :, (place % 2) * BLK : (place % 2 + 1) * BLK] = value
                elif which == 3:
                    ref[3 * i + place // 2, (place % 2) * rows : (place % 2 + 1) * rows, :] = value
                else:
                    ref[6 * i + place] = value


def on_chip(kernel, products, outs, scratch, inputs, results=None):
    streamed = results is not None
    space = pl.ANY if streamed else pltpu.VMEM
    staged = [x.shape for x in inputs[1:]] + outs if streamed else []
    outs = results or outs
    sems = [pltpu.SemaphoreType.DMA((n,)) for n in (len(inputs) - 1, len(outs))]
    return pl.pallas_call(
        kernel,
        out_shape=[jax.ShapeDtypeStruct(shape, jnp.bfloat16) for shape in outs],
        in_specs=[pl.BlockSpec(memory_space=pltpu.SMEM)]
        + [pl.BlockSpec(memory_space=space)] * (len(inputs) - 1),
        out_specs=[pl.BlockSpec(memory_space=space)] * len(outs),
        scratch_shapes=[pltpu.VMEM(shape, jnp.bfloat16) for shape in staged + scratch]
        + (sems if streamed else []),
        cost_estimate=pl.CostEstimate(
            flops=products * 2 * BLK * BLK,
            transcendentals=0,
            bytes_accessed=sum(x.size for x in inputs) * 2 + sum(map(math.prod, outs)) * 2,
        ),
        compiler_params=pltpu.CompilerParams(vmem_limit_bytes=56 * 2**20),
    )(*inputs)


def token_plan(tokens, grad_out, weight_a, weight_b, weight_c, weight_e):
    ndp, nb = lax.axis_size("dp"), lax.axis_size("bfly")
    blocks, rows, _ = weight_a.shape
    parts, count = 2 * blocks, tokens.shape[0]
    seat = jnp.stack([lax.axis_index("bfly"), lax.axis_index("dp") % 2]).astype(jnp.int32)

    everyone = ("dp", "bfly")
    shape = (ndp, nb, -1, BLK)
    first = pl.pallas_call(
        pack_kernel, out_shape=jax.ShapeDtypeStruct((ndp, 6, rows, BLK), jnp.bfloat16)
    )(weight_a, weight_b, weight_c, weight_e)
    first = exchange(first, "dp")
    a, mid = first[:, :2], first[:, 2:]
    rest = [own_sets(w) for w in (weight_b, weight_c, weight_e.reshape(parts, rows, BLK))]
    rest = exchange(after(jnp.stack(rest, axis=2), first), "dp")
    mid_across, a_across, rest_across = (xor_permute(part, 2) for part in (mid, a, rest))
    swapped, swapped_across = (xor_permute(part, 1, "dp") for part in (mid, mid_across))
    x = exchange(after(deal_tokens(tokens), rest, mid_across, swapped, a_across), everyone)
    g = after(deal_tokens(grad_out), x, rest_across, swapped_across)
    g = exchange(g, everyone).reshape(shape)
    x = x.reshape(shape)
    weights = gather_bfly(a, a_across) + gather_bfly(rest, rest_across)
    weights += gather_bfly(mid, mid_across) + gather_bfly(swapped, swapped_across)

    own, mid = count * ndp // nb, count * ndp // nb // 2
    saved = []
    for t in (own, mid):
        tiled, whole = (2, nb, nb, BLK // nb, t), (2, nb, BLK, t)
        saved += [tiled, whole, whole, tiled]
    halves = (nb, ndp, 2, rows, BLK)
    products = 2 * nb * (own + mid)
    out, *kept = on_chip(
        forward_kernel, 4 * products, [x.shape] + saved, [halves], [seat, x] + weights
    )
    out = exchange(out.reshape(ndp * nb, -1, BLK), everyone)
    own_shape, mid_shape = (2, ndp, 2, 4, rows, BLK), (2, 2, ndp, 4, rows, BLK)
    gin, own_keep, *sends = on_chip(
        backward_kernel,
        8 * products,
        [x.shape, own_shape, own_shape, mid_shape, mid_shape],
        [saved[0], saved[0], saved[4], saved[4], halves],
        [seat, x, g] + weights + kept,
        [x.shape, own_shape] + [own_shape[1:]] * 2 + [mid_shape] + [mid_shape[2:]] * 4,
    )
    mid_keep = sends.pop(2)
    own_sends, mid_sends = sends[:2], sends[2:]
    own_far = add(own_keep[1], xor_permute(own_sends[1], 1))
    own_near = add(own_keep[0], xor_permute(own_sends[0], 1))
    there = add(mid_keep[1, 1], after(xor_permute(mid_sends[3], 1), own_far))
    here = add(mid_keep[0, 1], xor_permute(mid_sends[1], 1))
    near = add(mid_keep[1, 0], xor_permute(mid_sends[2], 1))
    part, half = 3 * ndp // 8, ndp // 2
    own_first = add(own_near[:part], xor_permute(own_far[:part], 2))
    far_first = add(here[:half], xor_permute(there[:half], 1, "dp"))
    gin = after(gin.reshape(ndp * nb, -1, BLK), out, far_first, own_first)
    gin = exchange(gin, everyone)
    own_last = add(own_near[part:], xor_permute(after(own_far[part:], own_first), 2))
    own = jnp.concatenate([own_first, own_last], axis=0)
    far_last = xor_permute(after(there[half:], far_first), 1, "dp")
    far_last = add(here[half:], far_last)
    far = jnp.concatenate([xor_permute(far_first, 2), xor_permute(far_last, 2)], axis=0)
    near = add(add(mid_keep[0, 0], xor_permute(mid_sends[0], 1)), xor_permute(after(near, far_last), 1, "dp"))
    mid = add(near, far)
    dealt = jnp.concatenate([own, mid[:, None]], axis=1)
    got = exchange(after(dealt, gin), "dp")
    grads = pl.pallas_call(
        grads_kernel,
        out_shape=[
            jax.ShapeDtypeStruct(w.shape, jnp.float32)
            for w in (weight_a, weight_b, weight_c, weight_e)
        ],
    )(got)
    return (undeal_tokens(out, count), undeal_tokens(gin, count), *grads)


def per_device(tokens, grad_out, weight_a, weight_b, weight_c, weight_e):
    ndp, nb = lax.axis_size("dp"), lax.axis_size("bfly")
    fits = nb == 4 and ndp % 2 == 0 and 2 * weight_a.shape[0] == 3 * ndp
    fits = fits and tokens.shape[0] % (32 * nb) == 0 and weight_a.shape[1] * ndp == BLK
    fits = fits and weight_a.shape[2] == 2 * BLK and weight_e.shape[1] == 2 * weight_a.shape[1]
    plan = token_plan if fits else any_mesh
    return plan(tokens, grad_out, weight_a, weight_b, weight_c, weight_e)


def solution(mesh):
    in_specs = (P("dp", "bfly"),) * 2 + (P("bfly", "dp", None),) * 4
    return jax.shard_map(
        per_device, mesh=mesh, in_specs=in_specs, out_specs=in_specs, check_vma=False
    )
```

```python
import math

import jax
import jax.numpy as jnp
from jax import lax
from jax.experimental import pallas as pl
from jax.experimental.pallas import tpu as pltpu
from jax.sharding import PartitionSpec as P

BLK = 256

gelu_scale = 0.7978845608028654


def gelu_pair(hidden):
    inner_arg = gelu_scale * (hidden + 0.044715 * hidden * hidden * hidden)
    tangent = jnp.tanh(inner_arg)
    gelu_value = 0.5 * hidden * (1.0 + tangent)
    gelu_slope = 0.5 * (1.0 + tangent) + 0.5 * hidden * (1.0 - tangent * tangent) * gelu_scale * (
        1.0 + 3.0 * 0.044715 * hidden * hidden
    )
    return (gelu_value, gelu_slope)


def mm(spec, a, b):
    return jnp.einsum(spec, a, b, preferred_element_type=jnp.float32)


def regroup(piece, group_count):
    local_blocks, block_width, token_count = piece.shape
    stacked = piece.reshape(local_blocks, group_count, block_width // group_count, token_count)
    arrived = lax.all_to_all(stacked, "bfly", split_axis=1, concat_axis=1, tiled=True)
    return arrived.reshape(local_blocks, block_width, token_count)


def any_mesh(tokens, grad_out, weight_a, weight_b, weight_c, weight_e):
    group_count = lax.axis_size("bfly")
    full_a, full_b, full_c, full_e = (
        lax.all_gather(w, "dp", axis=1, tiled=True)
        for w in (weight_a, weight_b, weight_c, weight_e)
    )
    token_count = tokens.shape[0]
    inner_blocks = full_a.shape[0]
    spread_width = full_a.shape[2]
    local_blocks = full_b.shape[0]
    inputs = tokens.reshape(token_count, inner_blocks, BLK).transpose(1, 2, 0)
    upstream = grad_out.reshape(token_count, inner_blocks, BLK).transpose(1, 2, 0)
    hidden_view = (local_blocks, BLK, token_count)
    wide_view = (inner_blocks, spread_width, token_count)
    spread = mm("kit,kio->kot", inputs, full_a).astype(jnp.bfloat16).reshape(hidden_view)
    back_out = mm("kjt,koj->kot", upstream, full_e).astype(jnp.bfloat16).reshape(hidden_view)
    permuted = regroup(spread, group_count)
    back_mid = regroup(back_out, group_count)
    gelu_value, gelu_slope = gelu_pair(mm("qit,qij->qjt", permuted, full_b))
    active = gelu_value.astype(jnp.bfloat16)
    narrowed = mm("qit,qij->qjt", active, full_c).astype(jnp.bfloat16)
    back_hidden = (mm("qjt,qij->qit", back_mid, full_c) * gelu_slope).astype(jnp.bfloat16)
    back_first = mm("qjt,qij->qit", back_hidden, full_b).astype(jnp.bfloat16)
    returned = regroup(narrowed, group_count).reshape(wide_view)
    back_spread = regroup(back_first, group_count).reshape(wide_view)
    output = mm("kot,koj->kjt", returned, full_e)
    back_input = mm("kot,kio->kit", back_spread, full_a)
    parts = (
        mm("kit,kot->kio", inputs, back_spread),
        mm("qit,qjt->qij", permuted, back_hidden),
        mm("qit,qjt->qij", active, back_mid),
        mm("kot,kjt->koj", returned, upstream),
    )
    grads = tuple(
        lax.psum_scatter(part.astype(jnp.bfloat16), "dp", scatter_dimension=1, tiled=True).astype(
            jnp.float32
        )
        for part in parts
    )

    def rows(x):
        return x.astype(jnp.bfloat16).transpose(2, 0, 1).reshape(token_count, inner_blocks * BLK)

    return (rows(output), rows(back_input)) + grads


def xor_permute(x, mask, axis="bfly"):
    return lax.ppermute(x, axis, [(i, i ^ mask) for i in range(lax.axis_size(axis))])


def exchange(x, axes):
    return lax.all_to_all(x, axes, split_axis=0, concat_axis=0, tiled=True)


def own_sets(w):
    pairs = lax.axis_size("dp") // 2
    sets = w.reshape(pairs, 3, 2, w.shape[1], w.shape[2])
    own = jnp.stack([sets[:, 0], sets[:, 2]], axis=1)
    return own.reshape((pairs * 2,) + own.shape[2:])


def gather_bfly(w, across):
    return [w, xor_permute(w, 1), across, xor_permute(across, 1)]


def after(x, *earlier):
    return lax.optimization_barrier((x,) + earlier)[0]


def add(x, y):
    return (x.astype(jnp.float32) + y.astype(jnp.float32)).astype(jnp.bfloat16)


def deal_tokens(x):
    ndp, nb = lax.axis_size("dp"), lax.axis_size("bfly")
    pairs, count = ndp // 2, x.shape[0]
    view = x.reshape(count, pairs, 3, BLK)
    own = view[:, :, 0::2].reshape(nb, count // nb, ndp, BLK).transpose(2, 0, 1, 3)
    mid = view[:, :, 1].reshape(2, nb, count // nb // 2, pairs, BLK).transpose(3, 0, 1, 2, 4)
    mid = mid.reshape(ndp, nb, count // nb // 2, BLK)
    return jnp.concatenate([own, mid], axis=2).reshape(ndp * nb, -1, BLK)


def undeal_tokens(got, count):
    ndp, nb = lax.axis_size("dp"), lax.axis_size("bfly")
    pairs, own_count = ndp // 2, count // nb
    own = got[:, :own_count].reshape(pairs, 2, count, BLK)
    mid = got[:, own_count:].reshape(pairs, 1, count, BLK)
    sets = jnp.concatenate([own[:, :1], mid, own[:, 1:]], axis=1)
    return sets.transpose(2, 0, 1, 3).reshape(count, pairs * 3 * BLK)


def dot(x, y, contract_x, contract_y):
    dims = (((contract_x,), (contract_y,)), ((), ()))
    return lax.dot_general(x, y, dims, preferred_element_type=jnp.float32)


def square(x):
    return x.reshape(BLK, BLK)


def half_src(part, r):
    return pl.ds(r * (part // 2), part // 2)


def weight_of(slot, own, shared):
    def get(m, which, r):
        if slot == 0:
            return square(own[1][m][:, r, which - 1] if which else own[0][m][:, r])
        return square(shared[r][m][:, which])

    return get


def wide_weight(slot, own, e_ref, y):
    def get(m, r):
        if slot == 0:
            return square(own[1][m][half_src(e_ref.shape[1], r), :, 2])
        return square(e_ref[m, half_src(e_ref.shape[1], r ^ y)])

    return get


def join_halves(shared, e_ref, y):
    for m in range(4):
        e_ref[m, :, y] = shared[0][m][:, 3]
        e_ref[m, :, 1 - y] = shared[1][m][:, 3]


def weight_refs(refs):
    return (refs[:4], refs[4:8]), (refs[8:12], refs[12:16]), refs[16:]


def forward_kernel(seat_ref, x_ref, *refs):
    w, v, (out_ref, *refs) = weight_refs(refs)
    saved, e_ref = (refs[:4], refs[4:8]), refs[8]
    ndp, nb, all_rows, _ = x_ref.shape
    own_rows = 2 * all_rows // 3
    f, y = seat_ref[0], seat_ref[1]
    join_halves(v, e_ref, y)
    for slot, (lo, hi) in enumerate(((0, own_rows), (own_rows, all_rows))):
        perm, active, slope, ret = saved[slot]
        weight, wide = weight_of(slot, w, v), wide_weight(slot, w, e_ref, y)
        count = ndp * (hi - lo)
        tiles = (nb, BLK // nb, count)
        for m in range(nb):
            d = f ^ m
            x = x_ref[:, d, lo:hi, :].reshape(count, BLK)
            for r in range(2):
                spread = dot(weight(m, 0, r), x, 0, 1).astype(jnp.bfloat16)
                perm[r, :, d] = spread.reshape(tiles)
        for m in range(nb):
            s = f ^ m
            for r in range(2):
                p = perm[r, s].reshape(BLK, count)
                value, grade = gelu_pair(dot(weight(m, 1, r), p, 0, 0))
                value = value.astype(jnp.bfloat16)
                active[r, s] = value
                slope[r, s] = grade.astype(jnp.bfloat16)
                narrowed = dot(weight(m, 2, r), value, 0, 0).astype(jnp.bfloat16)
                ret[r, :, s] = narrowed.reshape(tiles)
        for m in range(nb):
            d = f ^ m
            total = 0.0
            for r in range(2):
                total = total + dot(ret[r, d].reshape(BLK, count), wide(m, r), 0, 0)
            out_ref[:, d, lo:hi, :] = total.astype(jnp.bfloat16).reshape(ndp, hi - lo, BLK)


class Streamed:
    def __init__(self, sources, targets, sems, order):
        self.targets, self.waiting = targets, {}
        for i in order:
            self.waiting[i] = pltpu.make_async_copy(sources[i], targets[i], sems.at[i])
            self.waiting[i].start()

    def get(self, i):
        if i in self.waiting:
            self.waiting.pop(i).wait()
        return self.targets[i]


class Lookup:
    def __init__(self, streamed, indices):
        self.streamed, self.indices = streamed, indices

    def __getitem__(self, at):
        return self.streamed.get(self.indices[at])


BACKWARD_ORDER = (
    (1, 6, 21, 7, 8, 9, 18, 19, 20, 2, 3, 4, 5, 0) + tuple(range(14, 18)) + (25,) + tuple(range(10, 14)) + (22, 23, 24)
)


def backward_kernel(seat_ref, *refs):
    count_in = len(BACKWARD_ORDER)
    sources, refs = refs[:count_in], refs[count_in:]
    results, refs = refs[:9], refs[9:]
    targets, refs = refs[:count_in], refs[count_in:]
    staged, refs = refs[:5], refs[5:]
    scratch, (e_ref, in_sems, out_sems) = (refs[:2], refs[2:4]), refs[4:]
    streamed = Streamed(sources, targets, in_sems, BACKWARD_ORDER)
    at = [Lookup(streamed, range(i, i + 4)) for i in range(2, 26, 4)]
    w, v, saved = at[:2], at[2:4], at[4:]
    gin_ref, own_keep, own_send, mid_keep, mid_send = staged
    sent = []

    def send(source, target):
        sent.append(pltpu.make_async_copy(source, target, out_sems.at[len(sent)]))
        sent[-1].start()

    ndp, nb, all_rows, _ = targets[0].shape
    own_rows = 2 * all_rows // 3
    rows = BLK // ndp
    f, y = seat_ref[0], seat_ref[1]

    def store(slot, m, which, r, part):
        ref = ((own_keep, own_send), (mid_keep, mid_send))[slot][m % 2]
        if slot == 0:
            ref[m // 2, :, r, which] = part.astype(jnp.bfloat16).reshape(ndp, rows, BLK)
        else:
            ref[r, m // 2, :, which] = part.astype(jnp.bfloat16).reshape(ndp, rows, BLK)

    def store_wide(slot, m, r, part):
        ref = ((own_keep, own_send), (mid_keep, mid_send))[slot][m % 2]
        part = part.astype(jnp.bfloat16).reshape(ndp // 2, 2, rows, BLK)
        if slot == 0:
            ref[m // 2, half_src(ndp, r), :, 3] = part
        else:
            ref[y, m // 2, half_src(ndp, r ^ y), 3] = part[:, 0]
            ref[1 - y, m // 2, half_src(ndp, r ^ y), 3] = part[:, 1]

    for slot, (lo, hi) in enumerate(((0, own_rows), (own_rows, all_rows))):
        perm, active, slope, ret = range(4)
        mid, spread = scratch[slot]
        if slot == 1:
            join_halves(v, e_ref, y)
        weight, wide = weight_of(slot, w, v), wide_weight(slot, w, e_ref, y)
        count = ndp * (hi - lo)
        tiles = (nb, BLK // nb, count)
        for m in range(nb):
            d = f ^ m
            g = streamed.get(1)[:, d, lo:hi, :].reshape(count, BLK)
            for r in range(2):
                mid[r, :, d] = dot(wide(m, r), g, 1, 1).astype(jnp.bfloat16).reshape(tiles)
                store_wide(slot, m, r, dot(saved[slot][ret][r, d].reshape(BLK, count), g, 1, 0))
        for m in range(nb):
            s = f ^ m
            for r in range(2):
                p = saved[slot][perm][r, s].reshape(BLK, count)
                back_mid = mid[r, s].reshape(BLK, count)
                back = dot(weight(m, 2, r), back_mid, 1, 0)
                back = (back * saved[slot][slope][r, s].astype(jnp.float32)).astype(jnp.bfloat16)
                store(slot, m, 2, r, dot(saved[slot][active][r, s], back_mid, 1, 1))
                store(slot, m, 1, r, dot(p, back, 1, 1))
                first = dot(weight(m, 1, r), back, 1, 0).astype(jnp.bfloat16)
                spread[r, :, s] = first.reshape(tiles)
        for m in range(nb):
            d = f ^ m
            x = streamed.get(0)[:, d, lo:hi, :].reshape(count, BLK)
            across = x.T
            total = 0.0
            for r in range(2):
                back = spread[r, d].reshape(BLK, count)
                total = total + dot(weight(m, 0, r), back, 1, 0)
                store(slot, m, 0, r, dot(across, back, 1, 1))
            gin_ref[:, d, lo:hi, :] = total.astype(jnp.bfloat16).T.reshape(ndp, hi - lo, BLK)
        if slot == 0:
            send(own_keep, results[1])
            send(own_send.at[0], results[2])
            send(own_send.at[1], results[3])
    send(mid_keep, results[4])
    for i in range(4):
        send(mid_send.at[i // 2, i % 2], results[5 + i])
    send(gin_ref, results[0])
    for copy in sent:
        copy.wait()


def pack_kernel(a_ref, b_ref, c_ref, e_ref, first_ref):
    owners, rows = first_ref.shape[0], b_ref.shape[1]

    def piece(which, index, part):
        if which == 0:
            return a_ref[index, :, part * BLK : (part + 1) * BLK]
        if which == 3:
            return e_ref[index, part * rows : (part + 1) * rows, :]
        return (b_ref, c_ref)[which - 1][2 * index + part]

    for owner in range(owners):
        pair, side = owner // 2, owner % 2
        for part in range(2):
            first_ref[owner, part] = piece(0, 3 * pair + 2 * side, part)
        for which in range(4):
            first_ref[owner, 2 + which] = piece(which, 3 * pair + 1, side)


def grads_kernel(got_ref, a_ref, b_ref, c_ref, e_ref):
    pairs = got_ref.shape[0] // 2
    rows = got_ref.shape[3]
    for which, ref in enumerate((a_ref, b_ref, c_ref, e_ref)):
        for place in range(6):
            owner, part = ((0, 0), (0, 1), (0, 2), (1, 2), (1, 0), (1, 1))[place]
            for i in range(pairs):
                value = got_ref[2 * i + owner, part, which].astype(jnp.float32)
                if which == 0:
                    ref[3 * i + place // 2, :, (place % 2) * BLK : (place % 2 + 1) * BLK] = value
                elif which == 3:
                    ref[3 * i + place // 2, (place % 2) * rows : (place % 2 + 1) * rows, :] = value
                else:
                    ref[6 * i + place] = value


def on_chip(kernel, products, outs, scratch, inputs, results=None):
    streamed = results is not None
    space = pl.ANY if streamed else pltpu.VMEM
    staged = [x.shape for x in inputs[1:]] + outs if streamed else []
    outs = results or outs
    sems = [pltpu.SemaphoreType.DMA((n,)) for n in (len(inputs) - 1, len(outs))]
    return pl.pallas_call(
        kernel,
        out_shape=[jax.ShapeDtypeStruct(shape, jnp.bfloat16) for shape in outs],
        in_specs=[pl.BlockSpec(memory_space=pltpu.SMEM)]
        + [pl.BlockSpec(memory_space=space)] * (len(inputs) - 1),
        out_specs=[pl.BlockSpec(memory_space=space)] * len(outs),
        scratch_shapes=[pltpu.VMEM(shape, jnp.bfloat16) for shape in staged + scratch]
        + (sems if streamed else []),
        cost_estimate=pl.CostEstimate(
            flops=products * 2 * BLK * BLK,
            transcendentals=0,
            bytes_accessed=sum(x.size for x in inputs) * 2 + sum(map(math.prod, outs)) * 2,
        ),
        compiler_params=pltpu.CompilerParams(vmem_limit_bytes=56 * 2**20),
    )(*inputs)


def token_plan(tokens, grad_out, weight_a, weight_b, weight_c, weight_e):
    ndp, nb = lax.axis_size("dp"), lax.axis_size("bfly")
    blocks, rows, _ = weight_a.shape
    parts, count = 2 * blocks, tokens.shape[0]
    seat = jnp.stack([lax.axis_index("bfly"), lax.axis_index("dp") % 2]).astype(jnp.int32)

    everyone = ("dp", "bfly")
    shape = (ndp, nb, -1, BLK)
    first = pl.pallas_call(
        pack_kernel, out_shape=jax.ShapeDtypeStruct((ndp, 6, rows, BLK), jnp.bfloat16)
    )(weight_a, weight_b, weight_c, weight_e)
    first = exchange(first, "dp")
    a, mid = first[:, :2], first[:, 2:]
    rest = [own_sets(w) for w in (weight_b, weight_c, weight_e.reshape(parts, rows, BLK))]
    rest = exchange(after(jnp.stack(rest, axis=2), first), "dp")
    mid_across, a_across, rest_across = (xor_permute(part, 2) for part in (mid, a, rest))
    swapped, swapped_across = (xor_permute(part, 1, "dp") for part in (mid, mid_across))
    x = exchange(after(deal_tokens(tokens), rest, mid_across, swapped, a_across), everyone)
    g = after(deal_tokens(grad_out), x, rest_across, swapped_across)
    g = exchange(g, everyone).reshape(shape)
    x = x.reshape(shape)
    weights = gather_bfly(a, a_across) + gather_bfly(rest, rest_across)
    weights += gather_bfly(mid, mid_across) + gather_bfly(swapped, swapped_across)

    own, mid = count * ndp // nb, count * ndp // nb // 2
    saved = []
    for t in (own, mid):
        tiled, whole = (2, nb, nb, BLK // nb, t), (2, nb, BLK, t)
        saved += [tiled, whole, whole, tiled]
    halves = (nb, ndp, 2, rows, BLK)
    products = 2 * nb * (own + mid)
    out, *kept = on_chip(
        forward_kernel, 4 * products, [x.shape] + saved, [halves], [seat, x] + weights
    )
    out = exchange(out.reshape(ndp * nb, -1, BLK), everyone)
    own_shape, mid_shape = (2, ndp, 2, 4, rows, BLK), (2, 2, ndp, 4, rows, BLK)
    gin, own_keep, *sends = on_chip(
        backward_kernel,
        8 * products,
        [x.shape, own_shape, own_shape, mid_shape, mid_shape],
        [saved[0], saved[0], saved[4], saved[4], halves],
        [seat, x, g] + weights + kept,
        [x.shape, own_shape] + [own_shape[1:]] * 2 + [mid_shape] + [mid_shape[2:]] * 4,
    )
    mid_keep = sends.pop(2)
    own_sends, mid_sends = sends[:2], sends[2:]
    own_far = add(own_keep[1], xor_permute(own_sends[1], 1))
    own_near = add(own_keep[0], xor_permute(own_sends[0], 1))
    there = add(mid_keep[1, 1], after(xor_permute(mid_sends[3], 1), own_far))
    here = add(mid_keep[0, 1], xor_permute(mid_sends[1], 1))
    near = add(mid_keep[1, 0], xor_permute(mid_sends[2], 1))
    part = 3 * ndp // 8
    own_first = add(own_near[:part], xor_permute(own_far[:part], 2))
    far = add(here, xor_permute(there, 1, "dp"))
    gin = after(gin.reshape(ndp * nb, -1, BLK), out, far, own_first)
    gin = exchange(gin, everyone)
    own_last = add(own_near[part:], xor_permute(after(own_far[part:], own_first), 2))
    own = jnp.concatenate([own_first, own_last], axis=0)
    near = add(add(mid_keep[0, 0], xor_permute(mid_sends[0], 1)), xor_permute(near, 1, "dp"))
    mid = add(near, xor_permute(far, 2))
    dealt = jnp.concatenate([own, mid[:, None]], axis=1)
    got = exchange(after(dealt, gin), "dp")
    grads = pl.pallas_call(
        grads_kernel,
        out_shape=[
            jax.ShapeDtypeStruct(w.shape, jnp.float32)
            for w in (weight_a, weight_b, weight_c, weight_e)
        ],
    )(got)
    return (undeal_tokens(out, count), undeal_tokens(gin, count), *grads)


def per_device(tokens, grad_out, weight_a, weight_b, weight_c, weight_e):
    ndp, nb = lax.axis_size("dp"), lax.axis_size("bfly")
    fits = nb == 4 and ndp % 2 == 0 and 2 * weight_a.shape[0] == 3 * ndp
    fits = fits and tokens.shape[0] % (32 * nb) == 0 and weight_a.shape[1] * ndp == BLK
    fits = fits and weight_a.shape[2] == 2 * BLK and weight_e.shape[1] == 2 * weight_a.shape[1]
    plan = token_plan if fits else any_mesh
    return plan(tokens, grad_out, weight_a, weight_b, weight_c, weight_e)


def solution(mesh):
    in_specs = (P("dp", "bfly"),) * 2 + (P("bfly", "dp", None),) * 4
    return jax.shard_map(
        per_device, mesh=mesh, in_specs=in_specs, out_specs=in_specs, check_vma=False
    )
```

```python
import math

import jax
import jax.numpy as jnp
from jax import lax
from jax.experimental import pallas as pl
from jax.experimental.pallas import tpu as pltpu
from jax.sharding import PartitionSpec as P

BLK = 256

gelu_scale = 0.7978845608028654


def gelu_pair(hidden):
    inner_arg = gelu_scale * (hidden + 0.044715 * hidden * hidden * hidden)
    tangent = jnp.tanh(inner_arg)
    gelu_value = 0.5 * hidden * (1.0 + tangent)
    gelu_slope = 0.5 * (1.0 + tangent) + 0.5 * hidden * (1.0 - tangent * tangent) * gelu_scale * (
        1.0 + 3.0 * 0.044715 * hidden * hidden
    )
    return (gelu_value, gelu_slope)


def mm(spec, a, b):
    return jnp.einsum(spec, a, b, preferred_element_type=jnp.float32)


def regroup(piece, group_count):
    local_blocks, block_width, token_count = piece.shape
    stacked = piece.reshape(local_blocks, group_count, block_width // group_count, token_count)
    arrived = lax.all_to_all(stacked, "bfly", split_axis=1, concat_axis=1, tiled=True)
    return arrived.reshape(local_blocks, block_width, token_count)


def any_mesh(tokens, grad_out, weight_a, weight_b, weight_c, weight_e):
    group_count = lax.axis_size("bfly")
    full_a, full_b, full_c, full_e = (
        lax.all_gather(w, "dp", axis=1, tiled=True)
        for w in (weight_a, weight_b, weight_c, weight_e)
    )
    token_count = tokens.shape[0]
    inner_blocks = full_a.shape[0]
    spread_width = full_a.shape[2]
    local_blocks = full_b.shape[0]
    inputs = tokens.reshape(token_count, inner_blocks, BLK).transpose(1, 2, 0)
    upstream = grad_out.reshape(token_count, inner_blocks, BLK).transpose(1, 2, 0)
    hidden_view = (local_blocks, BLK, token_count)
    wide_view = (inner_blocks, spread_width, token_count)
    spread = mm("kit,kio->kot", inputs, full_a).astype(jnp.bfloat16).reshape(hidden_view)
    back_out = mm("kjt,koj->kot", upstream, full_e).astype(jnp.bfloat16).reshape(hidden_view)
    permuted = regroup(spread, group_count)
    back_mid = regroup(back_out, group_count)
    gelu_value, gelu_slope = gelu_pair(mm("qit,qij->qjt", permuted, full_b))
    active = gelu_value.astype(jnp.bfloat16)
    narrowed = mm("qit,qij->qjt", active, full_c).astype(jnp.bfloat16)
    back_hidden = (mm("qjt,qij->qit", back_mid, full_c) * gelu_slope).astype(jnp.bfloat16)
    back_first = mm("qjt,qij->qit", back_hidden, full_b).astype(jnp.bfloat16)
    returned = regroup(narrowed, group_count).reshape(wide_view)
    back_spread = regroup(back_first, group_count).reshape(wide_view)
    output = mm("kot,koj->kjt", returned, full_e)
    back_input = mm("kot,kio->kit", back_spread, full_a)
    parts = (
        mm("kit,kot->kio", inputs, back_spread),
        mm("qit,qjt->qij", permuted, back_hidden),
        mm("qit,qjt->qij", active, back_mid),
        mm("kot,kjt->koj", returned, upstream),
    )
    grads = tuple(
        lax.psum_scatter(part.astype(jnp.bfloat16), "dp", scatter_dimension=1, tiled=True).astype(
            jnp.float32
        )
        for part in parts
    )

    def rows(x):
        return x.astype(jnp.bfloat16).transpose(2, 0, 1).reshape(token_count, inner_blocks * BLK)

    return (rows(output), rows(back_input)) + grads


def xor_permute(x, mask, axis="bfly"):
    return lax.ppermute(x, axis, [(i, i ^ mask) for i in range(lax.axis_size(axis))])


def exchange(x, axes):
    return lax.all_to_all(x, axes, split_axis=0, concat_axis=0, tiled=True)


def own_sets(w):
    pairs = lax.axis_size("dp") // 2
    sets = w.reshape(pairs, 3, 2, w.shape[1], w.shape[2])
    own = jnp.stack([sets[:, 0], sets[:, 2]], axis=1)
    return own.reshape((pairs * 2,) + own.shape[2:])


def gather_bfly(w, across):
    return [w, xor_permute(w, 1), across, xor_permute(across, 1)]


def after(x, *earlier):
    return lax.optimization_barrier((x,) + earlier)[0]


def add(x, y):
    return (x.astype(jnp.float32) + y.astype(jnp.float32)).astype(jnp.bfloat16)


def deal_tokens(x):
    ndp, nb = lax.axis_size("dp"), lax.axis_size("bfly")
    pairs, count = ndp // 2, x.shape[0]
    view = x.reshape(count, pairs, 3, BLK)
    own = view[:, :, 0::2].reshape(nb, count // nb, ndp, BLK).transpose(2, 0, 1, 3)
    mid = view[:, :, 1].reshape(2, nb, count // nb // 2, pairs, BLK).transpose(3, 0, 1, 2, 4)
    mid = mid.reshape(ndp, nb, count // nb // 2, BLK)
    return jnp.concatenate([own, mid], axis=2).reshape(ndp * nb, -1, BLK)


def undeal_tokens(got, count):
    ndp, nb = lax.axis_size("dp"), lax.axis_size("bfly")
    pairs, own_count = ndp // 2, count // nb
    own = got[:, :own_count].reshape(pairs, 2, count, BLK)
    mid = got[:, own_count:].reshape(pairs, 1, count, BLK)
    sets = jnp.concatenate([own[:, :1], mid, own[:, 1:]], axis=1)
    return sets.transpose(2, 0, 1, 3).reshape(count, pairs * 3 * BLK)


def dot(x, y, contract_x, contract_y):
    dims = (((contract_x,), (contract_y,)), ((), ()))
    return lax.dot_general(x, y, dims, preferred_element_type=jnp.float32)


def square(x):
    return x.reshape(BLK, BLK)


def half_src(part, r):
    return pl.ds(r * (part // 2), part // 2)


def weight_of(slot, own, shared):
    def get(m, which, r):
        if slot == 0:
            return square(own[1][m][:, r, which - 1] if which else own[0][m][:, r])
        return square(shared[r][m][:, which])

    return get


def wide_weight(slot, own, e_ref, y):
    def get(m, r):
        if slot == 0:
            return square(own[1][m][half_src(e_ref.shape[1], r), :, 2])
        return square(e_ref[m, half_src(e_ref.shape[1], r ^ y)])

    return get


def join_halves(shared, e_ref, y):
    for m in range(4):
        e_ref[m, :, y] = shared[0][m][:, 3]
        e_ref[m, :, 1 - y] = shared[1][m][:, 3]


def weight_refs(refs):
    return (refs[:4], refs[4:8]), (refs[8:12], refs[12:16]), refs[16:]


def forward_kernel(seat_ref, x_ref, *refs):
    w, v, (out_ref, *refs) = weight_refs(refs)
    saved, e_ref = (refs[:4], refs[4:8]), refs[8]
    ndp, nb, all_rows, _ = x_ref.shape
    own_rows = 2 * all_rows // 3
    f, y = seat_ref[0], seat_ref[1]
    join_halves(v, e_ref, y)
    for slot, (lo, hi) in enumerate(((0, own_rows), (own_rows, all_rows))):
        perm, active, slope, ret = saved[slot]
        weight, wide = weight_of(slot, w, v), wide_weight(slot, w, e_ref, y)
        count = ndp * (hi - lo)
        tiles = (nb, BLK // nb, count)
        for m in range(nb):
            d = f ^ m
            x = x_ref[:, d, lo:hi, :].reshape(count, BLK)
            for r in range(2):
                spread = dot(weight(m, 0, r), x, 0, 1).astype(jnp.bfloat16)
                perm[r, :, d] = spread.reshape(tiles)
        for m in range(nb):
            s = f ^ m
            for r in range(2):
                p = perm[r, s].reshape(BLK, count)
                value, grade = gelu_pair(dot(weight(m, 1, r), p, 0, 0))
                value = value.astype(jnp.bfloat16)
                active[r, s] = value
                slope[r, s] = grade.astype(jnp.bfloat16)
                narrowed = dot(weight(m, 2, r), value, 0, 0).astype(jnp.bfloat16)
                ret[r, :, s] = narrowed.reshape(tiles)
        for m in range(nb):
            d = f ^ m
            total = 0.0
            for r in range(2):
                total = total + dot(ret[r, d].reshape(BLK, count), wide(m, r), 0, 0)
            out_ref[:, d, lo:hi, :] = total.astype(jnp.bfloat16).reshape(ndp, hi - lo, BLK)


class Streamed:
    def __init__(self, sources, targets, sems, order):
        self.targets, self.waiting = targets, {}
        for i in order:
            self.waiting[i] = pltpu.make_async_copy(sources[i], targets[i], sems.at[i])
            self.waiting[i].start()

    def get(self, i):
        if i in self.waiting:
            self.waiting.pop(i).wait()
        return self.targets[i]


class Lookup:
    def __init__(self, streamed, indices):
        self.streamed, self.indices = streamed, indices

    def __getitem__(self, at):
        return self.streamed.get(self.indices[at])


BACKWARD_ORDER = (
    (1, 6, 21, 7, 8, 9, 18, 19, 20, 2, 3, 4, 5, 0) + tuple(range(14, 18)) + (25,) + tuple(range(10, 14)) + (22, 23, 24)
)


def backward_kernel(seat_ref, *refs):
    count_in = len(BACKWARD_ORDER)
    sources, refs = refs[:count_in], refs[count_in:]
    results, refs = refs[:9], refs[9:]
    targets, refs = refs[:count_in], refs[count_in:]
    staged, refs = refs[:5], refs[5:]
    scratch, (e_ref, in_sems, out_sems) = (refs[:2], refs[2:4]), refs[4:]
    streamed = Streamed(sources, targets, in_sems, BACKWARD_ORDER)
    at = [Lookup(streamed, range(i, i + 4)) for i in range(2, 26, 4)]
    w, v, saved = at[:2], at[2:4], at[4:]
    gin_ref, own_keep, own_send, mid_keep, mid_send = staged
    sent = []

    def send(source, target):
        sent.append(pltpu.make_async_copy(source, target, out_sems.at[len(sent)]))
        sent[-1].start()

    ndp, nb, all_rows, _ = targets[0].shape
    own_rows = 2 * all_rows // 3
    rows = BLK // ndp
    f, y = seat_ref[0], seat_ref[1]

    def store(slot, m, which, r, part):
        ref = ((own_keep, own_send), (mid_keep, mid_send))[slot][m % 2]
        if slot == 0:
            ref[m // 2, :, r, which] = part.astype(jnp.bfloat16).reshape(ndp, rows, BLK)
        else:
            ref[r, m // 2, :, which] = part.astype(jnp.bfloat16).reshape(ndp, rows, BLK)

    def store_wide(slot, m, r, part):
        ref = ((own_keep, own_send), (mid_keep, mid_send))[slot][m % 2]
        part = part.astype(jnp.bfloat16).reshape(ndp // 2, 2, rows, BLK)
        if slot == 0:
            ref[m // 2, half_src(ndp, r), :, 3] = part
        else:
            ref[y, m // 2, half_src(ndp, r ^ y), 3] = part[:, 0]
            ref[1 - y, m // 2, half_src(ndp, r ^ y), 3] = part[:, 1]

    for slot, (lo, hi) in enumerate(((0, own_rows), (own_rows, all_rows))):
        perm, active, slope, ret = range(4)
        mid, spread = scratch[slot]
        if slot == 1:
            join_halves(v, e_ref, y)
        weight, wide = weight_of(slot, w, v), wide_weight(slot, w, e_ref, y)
        count = ndp * (hi - lo)
        tiles = (nb, BLK // nb, count)
        for m in range(nb):
            d = f ^ m
            g = streamed.get(1)[:, d, lo:hi, :].reshape(count, BLK)
            for r in range(2):
                mid[r, :, d] = dot(wide(m, r), g, 1, 1).astype(jnp.bfloat16).reshape(tiles)
                store_wide(slot, m, r, dot(saved[slot][ret][r, d].reshape(BLK, count), g, 1, 0))
        for m in range(nb):
            s = f ^ m
            for r in range(2):
                p = saved[slot][perm][r, s].reshape(BLK, count)
                back_mid = mid[r, s].reshape(BLK, count)
                back = dot(weight(m, 2, r), back_mid, 1, 0)
                back = (back * saved[slot][slope][r, s].astype(jnp.float32)).astype(jnp.bfloat16)
                store(slot, m, 2, r, dot(saved[slot][active][r, s], back_mid, 1, 1))
                store(slot, m, 1, r, dot(p, back, 1, 1))
                first = dot(weight(m, 1, r), back, 1, 0).astype(jnp.bfloat16)
                spread[r, :, s] = first.reshape(tiles)
        for m in range(nb):
            d = f ^ m
            x = streamed.get(0)[:, d, lo:hi, :].reshape(count, BLK)
            across = x.T
            total = 0.0
            for r in range(2):
                back = spread[r, d].reshape(BLK, count)
                total = total + dot(weight(m, 0, r), back, 1, 0)
                store(slot, m, 0, r, dot(across, back, 1, 1))
            gin_ref[:, d, lo:hi, :] = total.astype(jnp.bfloat16).T.reshape(ndp, hi - lo, BLK)
        if slot == 0:
            send(own_keep, results[1])
            send(own_send.at[0], results[2])
            send(own_send.at[1], results[3])
    send(mid_keep, results[4])
    for i in range(4):
        send(mid_send.at[i // 2, i % 2], results[5 + i])
    send(gin_ref, results[0])
    for copy in sent:
        copy.wait()


def pack_kernel(a_ref, b_ref, c_ref, e_ref, first_ref):
    owners, rows = first_ref.shape[0], b_ref.shape[1]

    def piece(which, index, part):
        if which == 0:
            return a_ref[index, :, part * BLK : (part + 1) * BLK]
        if which == 3:
            return e_ref[index, part * rows : (part + 1) * rows, :]
        return (b_ref, c_ref)[which - 1][2 * index + part]

    for owner in range(owners):
        pair, side = owner // 2, owner % 2
        for part in range(2):
            first_ref[owner, part] = piece(0, 3 * pair + 2 * side, part)
        for which in range(4):
            first_ref[owner, 2 + which] = piece(which, 3 * pair + 1, side)


def grads_kernel(got_ref, a_ref, b_ref, c_ref, e_ref):
    pairs = got_ref.shape[0] // 2
    rows = got_ref.shape[3]
    for which, ref in enumerate((a_ref, b_ref, c_ref, e_ref)):
        for place in range(6):
            owner, part = ((0, 0), (0, 1), (0, 2), (1, 2), (1, 0), (1, 1))[place]
            for i in range(pairs):
                value = got_ref[2 * i + owner, part, which].astype(jnp.float32)
                if which == 0:
                    ref[3 * i + place // 2, :, (place % 2) * BLK : (place % 2 + 1) * BLK] = value
                elif which == 3:
                    ref[3 * i + place // 2, (place % 2) * rows : (place % 2 + 1) * rows, :] = value
                else:
                    ref[6 * i + place] = value


def on_chip(kernel, products, outs, scratch, inputs, results=None):
    streamed = results is not None
    space = pl.ANY if streamed else pltpu.VMEM
    staged = [x.shape for x in inputs[1:]] + outs if streamed else []
    outs = results or outs
    sems = [pltpu.SemaphoreType.DMA((n,)) for n in (len(inputs) - 1, len(outs))]
    return pl.pallas_call(
        kernel,
        out_shape=[jax.ShapeDtypeStruct(shape, jnp.bfloat16) for shape in outs],
        in_specs=[pl.BlockSpec(memory_space=pltpu.SMEM)]
        + [pl.BlockSpec(memory_space=space)] * (len(inputs) - 1),
        out_specs=[pl.BlockSpec(memory_space=space)] * len(outs),
        scratch_shapes=[pltpu.VMEM(shape, jnp.bfloat16) for shape in staged + scratch]
        + (sems if streamed else []),
        cost_estimate=pl.CostEstimate(
            flops=products * 2 * BLK * BLK,
            transcendentals=0,
            bytes_accessed=sum(x.size for x in inputs) * 2 + sum(map(math.prod, outs)) * 2,
        ),
        compiler_params=pltpu.CompilerParams(vmem_limit_bytes=56 * 2**20),
    )(*inputs)


def token_plan(tokens, grad_out, weight_a, weight_b, weight_c, weight_e):
    ndp, nb = lax.axis_size("dp"), lax.axis_size("bfly")
    blocks, rows, _ = weight_a.shape
    parts, count = 2 * blocks, tokens.shape[0]
    seat = jnp.stack([lax.axis_index("bfly"), lax.axis_index("dp") % 2]).astype(jnp.int32)

    everyone = ("dp", "bfly")
    shape = (ndp, nb, -1, BLK)
    first = pl.pallas_call(
        pack_kernel, out_shape=jax.ShapeDtypeStruct((ndp, 6, rows, BLK), jnp.bfloat16)
    )(weight_a, weight_b, weight_c, weight_e)
    first = exchange(first, "dp")
    a, mid = first[:, :2], first[:, 2:]
    rest = [own_sets(w) for w in (weight_b, weight_c, weight_e.reshape(parts, rows, BLK))]
    rest = exchange(after(jnp.stack(rest, axis=2), first), "dp")
    mid_across, a_across, rest_across = (xor_permute(part, 2) for part in (mid, a, rest))
    swapped, swapped_across = (xor_permute(part, 1, "dp") for part in (mid, mid_across))
    x = exchange(after(deal_tokens(tokens), rest, mid_across, swapped, a_across), everyone)
    g = after(deal_tokens(grad_out), x, rest_across, swapped_across)
    g = exchange(g, everyone).reshape(shape)
    x = x.reshape(shape)
    weights = gather_bfly(a, a_across) + gather_bfly(rest, rest_across)
    weights += gather_bfly(mid, mid_across) + gather_bfly(swapped, swapped_across)

    own, mid = count * ndp // nb, count * ndp // nb // 2
    saved = []
    for t in (own, mid):
        tiled, whole = (2, nb, nb, BLK // nb, t), (2, nb, BLK, t)
        saved += [tiled, whole, whole, tiled]
    halves = (nb, ndp, 2, rows, BLK)
    products = 2 * nb * (own + mid)
    out, *kept = on_chip(
        forward_kernel, 4 * products, [x.shape] + saved, [halves], [seat, x] + weights
    )
    out = exchange(out.reshape(ndp * nb, -1, BLK), everyone)
    own_shape, mid_shape = (2, ndp, 2, 4, rows, BLK), (2, 2, ndp, 4, rows, BLK)
    gin, own_keep, *sends = on_chip(
        backward_kernel,
        8 * products,
        [x.shape, own_shape, own_shape, mid_shape, mid_shape],
        [saved[0], saved[0], saved[4], saved[4], halves],
        [seat, x, g] + weights + kept,
        [x.shape, own_shape] + [own_shape[1:]] * 2 + [mid_shape] + [mid_shape[2:]] * 4,
    )
    mid_keep = sends.pop(2)
    own_sends, mid_sends = sends[:2], sends[2:]
    own_far = add(own_keep[1], xor_permute(own_sends[1], 1))
    own_near = add(own_keep[0], xor_permute(own_sends[0], 1))
    there = add(mid_keep[1, 1], after(xor_permute(mid_sends[3], 1), own_far))
    here = add(mid_keep[0, 1], xor_permute(mid_sends[1], 1))
    near = add(mid_keep[1, 0], xor_permute(mid_sends[2], 1))
    part, half = ndp // 4, ndp // 2
    own_first = add(own_near[:part], xor_permute(own_far[:part], 2))
    far_first = add(here[:half], xor_permute(there[:half], 1, "dp"))
    gin = after(gin.reshape(ndp * nb, -1, BLK), out, far_first, own_first)
    gin = exchange(gin, everyone)
    own_last = add(own_near[part:], xor_permute(after(own_far[part:], own_first), 2))
    own = jnp.concatenate([own_first, own_last], axis=0)
    far_last = xor_permute(after(there[half:], far_first), 1, "dp")
    far_last = add(here[half:], far_last)
    far = jnp.concatenate([xor_permute(far_first, 2), xor_permute(far_last, 2)], axis=0)
    near = add(add(mid_keep[0, 0], xor_permute(mid_sends[0], 1)), xor_permute(near, 1, "dp"))
    mid = add(near, far)
    dealt = jnp.concatenate([own, mid[:, None]], axis=1)
    got = exchange(after(dealt, gin), "dp")
    grads = pl.pallas_call(
        grads_kernel,
        out_shape=[
            jax.ShapeDtypeStruct(w.shape, jnp.float32)
            for w in (weight_a, weight_b, weight_c, weight_e)
        ],
    )(got)
    return (undeal_tokens(out, count), undeal_tokens(gin, count), *grads)


def per_device(tokens, grad_out, weight_a, weight_b, weight_c, weight_e):
    ndp, nb = lax.axis_size("dp"), lax.axis_size("bfly")
    fits = nb == 4 and ndp % 2 == 0 and 2 * weight_a.shape[0] == 3 * ndp
    fits = fits and tokens.shape[0] % (32 * nb) == 0 and weight_a.shape[1] * ndp == BLK
    fits = fits and weight_a.shape[2] == 2 * BLK and weight_e.shape[1] == 2 * weight_a.shape[1]
    plan = token_plan if fits else any_mesh
    return plan(tokens, grad_out, weight_a, weight_b, weight_c, weight_e)


def solution(mesh):
    in_specs = (P("dp", "bfly"),) * 2 + (P("bfly", "dp", None),) * 4
    return jax.shard_map(
        per_device, mesh=mesh, in_specs=in_specs, out_specs=in_specs, check_vma=False
    )
```
